512 devices in a mesh: tm: 32 (over x, z), space: 16 (over y, core).
Axes of the slice: x: 4, y: 8, z: 8, core: 2. Of those that a mesh axis runs over, the one named last changes fastest.
Arguments:
- inverse_factor: bfloat16 [32, 2048, 2048], P('tm', None, 'space'), as said below
- arrow_factor: bfloat16 [32, 64, 2048], P('tm', None, 'space'), may hold values from -6 to 6
- decay: float32 [32, 2048], P('tm'), may hold values from 0 to 1
- tip_inverse: float32 [64, 64], replicated, may hold values from -0.75 to 0.75
- sigma_end: float32 [2048, 2048], P(None, 'space'), may hold values from -2.7 to 2.7, as said below
- arrow_end: float32 [2048, 64], P('space'), may hold values from -6 to 6
Outputs:
- sigmas: float32 [32, 2048, 2048], P('tm', None, 'space')
- arrows: float32 [32, 2048, 64], P('tm', 'space')
The draws below stay inside these ranges and needn't reach their ends.
Inputs may be any that keep to these rules, and one draw needn't show every extreme that they name: `inverse_factor`: each K_t is lower triangular with a positive diagonal. `sigma_end`: symmetric.
All inputs are finite; a program needn't handle non-finite values.
Results may differ from the reference program's by a relative error of at most 0.0003.
Values may be sent and summed in bfloat16 or wider, within the bound.
No kernel may reach another device: no remote copies, remote signals or barrier semaphores. Data moves between devices by JAX's collectives and lax.ppermute only.
A program may use at most 128 MiB of HBM per device.

```python
import math
import jax
import jax.numpy as jnp
from jax import lax

N = 2048
ARROW = 64
PERIOD_TOTAL = 32


def draw_inverse_factor(key, part):
    key_off = jax.random.fold_in(key, 11)
    key_diag = jax.random.fold_in(key, 12)
    rows = lax.broadcasted_iota(jnp.int32, (PERIOD_TOTAL, N, N), 1)
    cols = lax.broadcasted_iota(jnp.int32, (PERIOD_TOTAL, N, N), 2)
    off = jnp.clip(jax.random.normal(key_off, (PERIOD_TOTAL, N, N), jnp.float32), -6.0, 6.0)
    diag = jax.random.uniform(key_diag, (PERIOD_TOTAL, 1, N), jnp.float32, 1.0, 2.0)
    full = jnp.where(rows > cols, off / math.sqrt(N), 0.0) + jnp.where(rows == cols, diag, 0.0)
    return (0.25 * full).astype(jnp.bfloat16)


def draw_decay(key, part):
    key_rate = jax.random.fold_in(key, 21)
    key_step = jax.random.fold_in(key, 22)
    surplus_draw_salt = jax.random.fold_in(key, 23)
    key_loss = jax.random.fold_in(key, 24)
    low = math.log(0.06 / PERIOD_TOTAL)
    high = math.log(0.5)
    node_rate = jnp.exp(jax.random.uniform(key_rate, (1, N), jnp.float32, low, high))
    step_factor = jnp.exp(jax.random.uniform(key_step, (PERIOD_TOTAL, 1), jnp.float32, math.log(0.5), math.log(2.0)))
    widened_period_total = jax.random.randint(surplus_draw_salt, (3,), 0, PERIOD_TOTAL)
    period_moments = lax.broadcasted_iota(jnp.int32, (PERIOD_TOTAL, 1), 0)
    dropped_periods = jnp.any(period_moments == widened_period_total[None, :], axis=1, keepdims=True)
    loss = jax.random.uniform(key_loss, (PERIOD_TOTAL, N), jnp.float32, 0.5, 0.8)
    values = jnp.exp(-node_rate * step_factor) * jnp.where(dropped_periods, loss, 1.0)
    return values.astype(jnp.float32)


def draw_sigma_end(key, part):
    key_base = jax.random.fold_in(key, 31)
    base = jnp.clip(jax.random.normal(key_base, (N, N), jnp.float32), -4.0, 4.0)
    rows = lax.broadcasted_iota(jnp.int32, (N, N), 0)
    cols = lax.broadcasted_iota(jnp.int32, (N, N), 1)
    symmetric = 0.2 * (base + base.T) + jnp.where(rows == cols, 1.0, 0.0)
    return symmetric.astype(jnp.float32)


def level_of(stream_key, extent, pieces, least, largest):
    def one(dim, parts):
        steps = jax.random.uniform(jax.random.fold_in(jax.random.fold_in(stream_key, 6), dim), (parts,), jnp.float32, least / len(pieces), largest / len(pieces))
        return jnp.repeat(jnp.exp(steps), extent[dim] // parts).reshape((-1,) + (1,) * (len(extent) - dim - 1))

    loudness = one(*pieces[0])
    for cut in pieces[1:]:
        loudness = loudness * one(*cut)
    return loudness


def noise(stream_key, shape, deviation, reach, split=(), held_as=jnp.bfloat16):
    values = jax.random.normal(stream_key, shape, jnp.float32) * deviation
    if len(split) > 0:
        values = level_of(stream_key, shape, split, -0.22, 0.18) * values
    return jnp.clip(values, min=-reach, max=reach).astype(held_as)


def setup_inputs(seed: int = 0) -> dict:
    arg_keys = jax.random.split(jax.random.key(seed), 7)
    inverse_factor = draw_inverse_factor(jax.random.fold_in(arg_keys[6], 71), 0)
    arrow_factor = noise(arg_keys[1], (PERIOD_TOTAL, ARROW, N), 1.0, 6.0, ((0, 32), (2, 16)))
    decay = draw_decay(jax.random.fold_in(arg_keys[6], 71), 0)
    tip_inverse = noise(arg_keys[3], (ARROW, ARROW), ARROW ** -0.5, 0.75, (), jnp.float32)
    sigma_end = draw_sigma_end(jax.random.fold_in(arg_keys[6], 71), 0)
    arrow_end = noise(arg_keys[5], (N, ARROW), 1.0, 6.0, ((0, 16),), jnp.float32)
    return dict(inverse_factor=inverse_factor, arrow_factor=arrow_factor, decay=decay, tip_inverse=tip_inverse, sigma_end=sigma_end, arrow_end=arrow_end)


def reference(inverse_factor, arrow_factor, decay, tip_inverse, sigma_end, arrow_end):
    highest = lax.Precision.HIGHEST

    def one_block(carry, inputs):
        covariance_following, spike_ahead = carry
        factor_block, arrow_block, damping_block = inputs
        factor_wide = factor_block.astype(jnp.float32)
        block_precision = jnp.dot(factor_wide.T, factor_wide, precision=highest)
        cross = jnp.dot(block_precision, arrow_block.astype(jnp.float32).T, precision=highest)
        sigma_now = block_precision + damping_block[:, None] * damping_block[None, :] * covariance_following
        arrow_now = -jnp.dot(cross, tip_inverse, precision=highest) + damping_block[:, None] * spike_ahead
        return (sigma_now, arrow_now), (sigma_now, arrow_now)

    _, (sigmas, arrows) = lax.scan(one_block, (sigma_end, arrow_end), (inverse_factor, arrow_factor, decay), reverse=True)
    return sigmas, arrows
```

```python
import jax
import jax.numpy as jnp
from jax import lax
from jax.experimental import pallas as pl
from jax.experimental.pallas import tpu as pltpu
from jax.sharding import PartitionSpec as P

PAD = 8


def split3(x):
    hi = x.astype(jnp.bfloat16)
    rest = x - hi.astype(jnp.float32)
    mid = rest.astype(jnp.bfloat16)
    low = (rest - mid.astype(jnp.float32)).astype(jnp.bfloat16)
    return hi, mid, low


def panel_kernel(order, arrow, pieces, gathered, mine, tip_t, decay_rows, decay_cols, out, total):
    step = pl.program_id(0)
    width = mine.shape[1]
    rows = order // pieces
    per = width // rows

    @pl.when(step == 0)
    def _():
        total[...] = jnp.zeros_like(total)

    tile = lax.dot_general(
        gathered[0, :order, :], mine[...], (((0,), (0,)), ((), ())), preferred_element_type=jnp.float32
    )
    out[pl.ds(step * per, per), :rows, :] = tile.reshape(per, rows, width)
    border = gathered[0, order:, :]
    acc = total[...]
    for part in split3(tile):
        acc = acc + jnp.dot(border, part, preferred_element_type=jnp.float32)
    total[...] = acc

    @pl.when(step == pl.num_programs(0) - 1)
    def _():
        own = -jnp.dot(
            tip_t[...], total[...], precision=lax.Precision.HIGHEST, preferred_element_type=jnp.float32
        )
        share = arrow // pieces
        for r in range(pieces):
            out[r, rows : rows + share, :] = own[r * share : (r + 1) * share, :]
            out[r, rows + share : rows + share + 1, :] = decay_rows[r : r + 1, :]
            out[r, rows + share + 1 : rows + share + 2, :] = decay_cols[...]
            out[r, rows + share + 2 :, :] = jnp.zeros((PAD - share - 2, width), jnp.float32)


def scan_kernel(rows, share, got, end, out, turned):
    pieces = got.shape[0]
    width = got.shape[2]
    for s in range(pieces):
        turned[s : s + 1, :] = got[s, rows + share : rows + share + 1, :]
    columns = turned[...].T
    carry = end[...]
    tail = jnp.where(lax.broadcasted_iota(jnp.int32, (PAD, width), 0) < share, 1.0, 0.0)
    for s in range(pieces - 1, -1, -1):
        by_row = jnp.concatenate([jnp.broadcast_to(columns[:rows, s : s + 1], (rows, width)), tail], axis=0)
        by_col = got[s, rows + share + 1 : rows + share + 2, :]
        carry = got[s] + by_row * by_col * carry
        out[s] = carry


def body(inverse_factor, arrow_factor, decay, tip_inverse, sigma_end, arrow_end):
    factor_cols = inverse_factor[0]
    order, width = factor_cols.shape
    arrow = tip_inverse.shape[0]
    pieces = lax.axis_size("tm")
    rows, share = order // pieces, arrow // pieces
    column_at = lax.axis_index("space")
    piece_at = lax.axis_index("tm")

    gathered = lax.all_gather(jnp.concatenate([factor_cols, arrow_factor[0]], axis=0), "space", axis=0)
    panels = gathered.shape[0]
    decay_rows = jnp.pad(decay[0].reshape(pieces, rows), ((0, 0), (0, width - rows)))
    decay_cols = lax.dynamic_slice_in_dim(decay, column_at * width, width, axis=1)
    whole = lambda shape: pl.BlockSpec(shape, lambda i: (0,) * len(shape))
    send = pl.pallas_call(
        lambda *refs: panel_kernel(order, arrow, pieces, *refs),
        grid=(panels,),
        out_shape=jax.ShapeDtypeStruct((pieces, rows + PAD, width), jnp.float32),
        in_specs=[
            pl.BlockSpec((1, order + arrow, width), lambda i: (i, 0, 0)),
            whole((order, width)),
            whole((arrow, arrow)),
            whole((pieces, width)),
            whole((1, width)),
        ],
        out_specs=whole((pieces, rows + PAD, width)),
        scratch_shapes=[pltpu.VMEM((arrow, width), jnp.float32)],
        name="panel",
    )(gathered, factor_cols, tip_inverse.T, decay_rows, decay_cols)

    got = lax.all_to_all(send, "tm", 0, 0, tiled=True)
    end = jnp.concatenate(
        [
            lax.dynamic_slice_in_dim(sigma_end, piece_at * rows, rows, axis=0),
            lax.dynamic_slice_in_dim(arrow_end.T, piece_at * share, share, axis=0),
            jnp.zeros((PAD - share, width), jnp.float32),
        ],
        axis=0,
    )
    done = pl.pallas_call(
        lambda *refs: scan_kernel(rows, share, *refs),
        out_shape=jax.ShapeDtypeStruct(got.shape, jnp.float32),
        scratch_shapes=[pltpu.VMEM((pieces, width), jnp.float32)],
        name="suffix",
    )(got, end)
    back = lax.all_to_all(done, "tm", 0, 0, tiled=True)
    sigma = back[:, :rows].reshape(order, width)
    arrows = back[:, rows : rows + share].reshape(arrow, width).T
    return sigma[None], arrows[None]


def solution(mesh):
    placed = (
        P("tm", None, "space"),
        P("tm", None, "space"),
        P("tm", None),
        P(),
        P(None, "space"),
        P("space", None),
    )
    return jax.shard_map(
        body,
        mesh=mesh,
        in_specs=placed,
        out_specs=(P("tm", None, "space"), P("tm", "space", None)),
        check_vma=False,
    )
```

```python
import jax
import jax.numpy as jnp
from jax import lax
from jax.experimental import pallas as pl
from jax.experimental.pallas import tpu as pltpu
from jax.sharding import PartitionSpec as P

CORNER = 4
PAD = 8
TOP = 14.0


def whole(shape):
    return pl.BlockSpec(shape, lambda i: (0,) * len(shape))


def split3(x):
    hi = x.astype(jnp.bfloat16)
    rest = x - hi.astype(jnp.float32)
    mid = rest.astype(jnp.bfloat16)
    low = (rest - mid.astype(jnp.float32)).astype(jnp.bfloat16)
    return hi, mid, low


def dot(a, b):
    return jnp.dot(a, b, preferred_element_type=jnp.float32)


def border_times(border, tile):
    hi, mid, low = split3(tile)
    return dot(border, hi) + dot(border, mid) + dot(border, low)


def exponent(x):
    largest = jnp.max(jnp.abs(x), axis=0, keepdims=True)
    return jnp.ceil(jnp.log2(jnp.maximum(largest, 2.0**-100)))


def encode(panel, pair):
    at = lax.broadcasted_iota(jnp.int32, pair.shape, 0)
    level, pair_level = exponent(panel), exponent(pair)
    scaled = pair * jnp.exp2(TOP - pair_level)
    high = scaled.astype(jnp.bfloat16).astype(jnp.float32)
    tail = jnp.where(at < 2, high, jnp.where(at < 4, scaled - high, 0.0))
    tail = jnp.where(at == 4, level, jnp.where(at == 5, pair_level, tail))
    return panel * jnp.exp2(TOP - level), tail


def decode(message, rows):
    tail = message[rows:, :]
    at = lax.broadcasted_iota(jnp.int32, tail.shape, 0)
    panel = message[:rows, :] * jnp.exp2(tail[4:5, :] - TOP)
    both = tail + jnp.where(at < 2, jnp.roll(tail, -2, axis=0), jnp.roll(tail, 2, axis=0))
    return panel, jnp.where(at < 4, both * jnp.exp2(tail[5:6, :] - TOP), 0.0)


def doubled(pair):
    return jnp.concatenate([pair, pair, jnp.zeros((PAD - 4, pair.shape[1]), jnp.float32)], axis=0)


def panel_kernel(cut, rows, at, gathered, mine_t, own_top, *refs):
    tops = (own_top, *refs[: CORNER - 1])
    tip_t, out, total = refs[CORNER - 1 :]
    step = pl.program_id(0)
    group, depth, width = gathered.shape[0], mine_t.shape[1] - cut, mine_t.shape[0]
    per = width // rows

    @pl.when(step == 0)
    def _():
        total[...] = jnp.zeros_like(total)

    for q in range(0, group, 2):
        pair = jnp.concatenate([gathered[q, :depth], gathered[q + 1, :depth]], axis=1)
        border = jnp.concatenate([gathered[q, depth:], gathered[q + 1, depth:]], axis=1)
        tile = dot(mine_t[:, cut:], pair).T
        out[pl.ds((step * group + q) * per, 2 * per), :rows, :] = tile.reshape(2 * per, rows, width)
        total[...] += border_times(border, tile)

    @pl.when(step == 0)
    def _():
        for other, top in enumerate(tops):
            panel = other ^ (at[0] & (CORNER - 1))
            tile = dot(mine_t[:, :cut], top[...]).T
            out[pl.ds(panel * per, per), :rows, :] += tile.reshape(per, rows, width)
            total[...] += border_times(gathered[panel, depth:], tile)

    @pl.when(step == pl.num_programs(0) - 1)
    def _():
        own = -jnp.dot(
            tip_t[...], total[...], precision=lax.Precision.HIGHEST, preferred_element_type=jnp.float32
        )
        for r in range(out.shape[0]):
            panel, tail = encode(out[r, :rows, :], doubled(own[2 * r : 2 * r + 2, :]))
            out[r, :rows, :] = panel
            out[r, rows:, :] = tail


def scan_kernel(rows, got, decays, end, out, turned):
    pieces, _, width = got.shape
    for s in range(pieces):
        turned[s : s + 1, :] = decays[s, 0:1, :]
    columns = turned[...].T[:rows, :]
    carry, pair = end[:rows, :], end[rows:, :]
    for s in range(pieces - 1, -1, -1):
        out[s, :rows, :], out[s, rows:, :] = encode(carry, pair)
        if s == 0:
            break
        panel, arrow = decode(got[s], rows)
        by_col = decays[s, 1:2, :]
        by_row = jnp.broadcast_to(columns[:, s : s + 1], (rows, width))
        carry = panel + by_row * by_col * carry
        pair = arrow + by_col * pair


def last_kernel(rows, sent, got, decay_rows, by_col, sigma, arrows):
    columns = decay_rows[...].T[:rows, :]
    for r in range(sent.shape[0]):
        panel, arrow = decode(sent[r], rows)
        later, later_arrow = decode(got[r], rows)
        by_row = jnp.broadcast_to(columns[:, r : r + 1], panel.shape)
        sigma[r * rows : (r + 1) * rows, :] = panel + by_row * by_col[...] * later
        arrows[2 * r : 2 * r + 2, :] = (arrow + by_col[...] * later_arrow)[:2, :]


def body(inverse_factor, arrow_factor, decay, tip_inverse, sigma_end, arrow_end):
    factor_cols = inverse_factor[0]
    order, width = factor_cols.shape
    arrow = tip_inverse.shape[0]
    pieces = lax.axis_size("tm")
    cut = CORNER * width
    rows, share = order // pieces, arrow // pieces
    column_at = lax.axis_index("space")
    piece_at = lax.axis_index("tm")

    gathered = lax.all_gather(jnp.concatenate([factor_cols[cut:], arrow_factor[0]], axis=0), "space", axis=0)
    panels, tall = gathered.shape[:2]
    top = factor_cols[:cut]
    tops = [top] + [
        lax.ppermute(top, "space", [(q, q ^ other) for q in range(CORNER)]) for other in range(1, CORNER)
    ]
    decay_rows = jnp.pad(decay[0].reshape(pieces, rows), ((0, 0), (0, width - rows)))
    by_col = lax.dynamic_slice_in_dim(decay, column_at * width, width, axis=1)
    decays = jnp.concatenate(
        [
            decay_rows[:, None],
            jnp.broadcast_to(by_col[None], (pieces, 1, width)),
            jnp.zeros((pieces, PAD - 2, width), jnp.float32),
        ],
        axis=1,
    )
    gathered, decays = lax.optimization_barrier(
        (gathered, lax.all_to_all(decays, "tm", 0, 0, tiled=True))
    )
    pair_end = lax.dynamic_slice_in_dim(arrow_end.T, piece_at * share, share, axis=0)
    end = jnp.concatenate(
        [
            lax.dynamic_slice_in_dim(sigma_end, piece_at * rows, rows, axis=0),
            pair_end,
            pair_end,
            jnp.zeros((PAD - 2 * share, width), jnp.float32),
        ],
        axis=0,
    )

    group = 4
    message = jax.ShapeDtypeStruct((pieces, rows + PAD, width), jnp.float32)
    sent = pl.pallas_call(
        lambda *refs: panel_kernel(cut, rows, *refs),
        grid=(panels // group,),
        out_shape=message,
        in_specs=[
            pl.BlockSpec(memory_space=pltpu.SMEM),
            pl.BlockSpec((group, tall, width), lambda i: (i, 0, 0)),
            whole((width, order)),
            *[whole((cut, width)) for _ in range(CORNER)],
            whole((arrow, arrow)),
        ],
        out_specs=whole(message.shape),
        scratch_shapes=[pltpu.VMEM((arrow, width), jnp.float32)],
        name="panel",
    )(column_at.reshape(1), gathered, factor_cols.T, *tops, tip_inverse.T)

    def exchange(values):
        moved = lax.all_to_all(values.astype(jnp.float16), "tm", 0, 0, tiled=True)
        return moved.astype(jnp.float32)

    ahead = pl.pallas_call(
        lambda *refs: scan_kernel(rows, *refs),
        out_shape=message,
        scratch_shapes=[pltpu.VMEM((pieces, width), jnp.float32)],
        name="suffix",
    )(exchange(sent), decays, end)
    sigma, arrows = pl.pallas_call(
        lambda *refs: last_kernel(rows, *refs),
        out_shape=(
            jax.ShapeDtypeStruct((order, width), jnp.float32),
            jax.ShapeDtypeStruct((arrow, width), jnp.float32),
        ),
        name="last",
    )(sent, exchange(ahead), decay_rows, by_col)
    return sigma[None], arrows.T[None]


def solution(mesh):
    placed = (
        P("tm", None, "space"),
        P("tm", None, "space"),
        P("tm", None),
        P(),
        P(None, "space"),
        P("space", None),
    )
    return jax.shard_map(
        body,
        mesh=mesh,
        in_specs=placed,
        out_specs=(P("tm", None, "space"), P("tm", "space", None)),
        check_vma=False,
    )
```

```python
import jax
import jax.numpy as jnp
from jax import lax
from jax.experimental import pallas as pl
from jax.experimental.pallas import tpu as pltpu
from jax.sharding import PartitionSpec as P

CORES = 2
PAD = 8
TOP = 14.0
DECAY = 1024.0


def split3(x):
    hi = x.astype(jnp.bfloat16)
    rest = x - hi.astype(jnp.float32)
    mid = rest.astype(jnp.bfloat16)
    low = (rest - mid.astype(jnp.float32)).astype(jnp.bfloat16)
    return hi, mid, low


def dot(a, b):
    return jnp.dot(a, b, preferred_element_type=jnp.float32)


def border_times(border, tile):
    hi, mid, low = split3(tile)
    return dot(border, hi) + dot(border, mid) + dot(border, low)


def exponent(x):
    largest = jnp.max(jnp.abs(x), axis=0, keepdims=True)
    return jnp.ceil(jnp.log2(jnp.maximum(largest, 2.0**-100)))


def squared(x, level):
    unit = x * jnp.exp2(TOP / 2 - level)
    return unit * jnp.abs(unit)


def rooted(x, level):
    root = jnp.sqrt(jnp.abs(x))
    return jnp.where(x < 0, -root, root) * jnp.exp2(level - TOP / 2)


def encode(panel, pair, extra):
    at = lax.broadcasted_iota(jnp.int32, pair.shape, 0)
    level, pair_level = exponent(panel), exponent(pair)
    tail = jnp.where(at < 2, squared(pair, pair_level), extra)
    tail = jnp.where(at == 2, level, jnp.where(at == 3, pair_level, tail))
    return squared(panel, level), tail


def decode(message, rows):
    tail = message[rows:, :]
    at = lax.broadcasted_iota(jnp.int32, tail.shape, 0)
    panel = rooted(message[:rows, :], tail[2:3, :])
    return panel, jnp.where(at < 2, rooted(tail, tail[3:4, :]), 0.0)


def own_kernel(mine, other, mine_top, other_top, tile, both_t, total):
    tall = mine.shape[0]
    depth = both_t.shape[1]
    turned = jnp.concatenate([mine[:depth, :].T, other[:depth, :].T], axis=0)
    top = jnp.concatenate([mine_top[...].T, other_top[...].T], axis=0)
    both_t[...] = turned
    got = dot(turned, mine[:depth, :]) + dot(top, mine_top[...])
    tile[...] = got
    border = jnp.concatenate([mine[depth:tall, :], other[depth:tall, :]], axis=1)
    total[...] = jnp.concatenate([border_times(border, got), jnp.zeros(total.shape[:1] + got.shape[1:])], axis=1)


def far_tiles(panels, both_t, before):
    depth = both_t.shape[1]
    tall = panels[0].shape[0]
    joined = jnp.concatenate([p[:depth, :] for p in panels], axis=1)
    border = jnp.concatenate([p[depth:tall, :] for p in panels], axis=1)
    tile = dot(both_t[...], joined).T
    return tile, before[...] + border_times(border, tile)


def far_kernel(first, second, both_t, before, keep, give, total):
    tile, total[...] = far_tiles((first, second), both_t, before)
    width = keep.shape[1]
    keep[...] = tile[:, :width]
    give[...] = tile[:, width:]


def farthest_kernel(first, both_t, before, keep, give):
    tile, total = far_tiles((first,), both_t, before)
    width = keep.shape[1]
    count = tile.shape[0]
    keep[:count, :] = tile[:, :width]
    keep[count:, :] = total[:, :width]
    give[:count, :] = tile[:, width:]
    give[count:, :] = total[:, width:]


def message_kernel(rows, chips, at, own, *refs):
    hops = (len(refs) - 4) // 2
    kept, given = refs[:hops], refs[hops : 2 * hops]
    tip_t, decay_rows, decay_cols, out = refs[2 * hops :]
    width = own.shape[1]
    per = width // rows
    chip, core = at[0] // CORES, at[0] % CORES
    way = 1 - 2 * core

    def put(block, hop, parity):
        spot = lax.rem(chip + hop + chips, chips) * CORES + parity
        out[pl.ds(spot * per, per), :rows, :] = block.reshape(per, rows, width)

    put(own[:width, :], 0, core)
    put(own[width:, :], 0, 1 - core)
    for s in range(hops):
        hop = (s + 1) * way
        put(kept[s][:width, :], -hop, core)
        put(given[s][:width, :], hop, 1 - core)
        if s < hops - 1:
            put(kept[s][width:, :], -hop, 1 - core)
            put(given[s][width:, :], hop, core)
    total = kept[-1][width:, :] + given[-1][width:, :]
    arrow = -jnp.dot(tip_t[...], total, precision=lax.Precision.HIGHEST, preferred_element_type=jnp.float32)
    fill = jnp.zeros((PAD - 2, width), jnp.float32)
    cols = decay_cols[...]
    place = lax.broadcasted_iota(jnp.int32, cols.shape, 0)
    for r in range(out.shape[0]):
        extra = jnp.where(place == 4, decay_rows[r : r + 1, :], cols)
        pair = jnp.concatenate([arrow[2 * r : 2 * r + 2, :], fill], axis=0)
        out[r, :rows, :], out[r, rows:, :] = encode(out[r, :rows, :], pair, extra)


def scan_kernel(rows, got, end, out, turned):
    pieces, _, width = got.shape
    for s in range(pieces):
        turned[s : s + 1, :] = got[s, rows + 4 : rows + 5, :]
    columns = turned[...].T
    columns = (columns[:rows, :] + columns[rows : 2 * rows, :] * (1 / 256)) * (1 / DECAY)
    carry, pair = end[:rows, :], end[rows:, :]
    for s in range(pieces - 1, -1, -1):
        out[s, :rows, :], out[s, rows:, :] = encode(carry, pair, jnp.zeros_like(pair))
        if s == 0:
            break
        panel, arrow = decode(got[s], rows)
        by_col = (got[s, rows + 5 : rows + 6, :] + got[s, rows + 6 : rows + 7, :] * (1 / 256)) * (1 / DECAY)
        by_row = jnp.broadcast_to(columns[:, s : s + 1], (rows, width))
        carry = panel + by_row * by_col * carry
        pair = arrow + by_col * pair


def last_kernel(rows, sent, got, decay_rows, by_col, sigma, arrows):
    columns = decay_rows[...].T[:rows, :]
    for r in range(sent.shape[0]):
        panel, arrow = decode(sent[r], rows)
        later, later_arrow = decode(got[r], rows)
        by_row = jnp.broadcast_to(columns[:, r : r + 1], panel.shape)
        sigma[r * rows : (r + 1) * rows, :] = panel + by_row * by_col[...] * later
        arrows[2 * r : 2 * r + 2, :] = (arrow + by_col[...] * later_arrow)[:2, :]


def two_parts(decay):
    scaled = decay * DECAY
    high = lax.reduce_precision(scaled, 8, 7)
    return high, (scaled - high) * 256


def body(inverse_factor, arrow_factor, decay, tip_inverse, sigma_end, arrow_end):
    factor_cols = inverse_factor[0]
    order, width = factor_cols.shape
    arrow = tip_inverse.shape[0]
    pieces, devices = lax.axis_size("tm"), lax.axis_size("space")
    chips, cut = devices // CORES, CORES * width
    rows, share = order // pieces, arrow // pieces
    column_at = lax.axis_index("space")
    piece_at = lax.axis_index("tm")
    swapped = [(p, p ^ 1) for p in range(devices)]
    around = [
        (p, (p // CORES + 1 - 2 * (p % CORES)) % chips * CORES + p % CORES) for p in range(devices)
    ]
    depth = order - cut
    tall = depth + arrow
    f32 = lambda *shape: jax.ShapeDtypeStruct(shape, jnp.float32)

    def pack_kernel(cols, border, out):
        out[:depth, :] = cols[cut:, :]
        out[depth:, :] = border[...]

    mine = pl.pallas_call(
        pack_kernel, out_shape=jax.ShapeDtypeStruct((tall, width), jnp.bfloat16), name="pack"
    )(factor_cols, arrow_factor[0])
    top = factor_cols[:cut]
    first = [lax.ppermute(mine, "space", around)]
    other = lax.ppermute(mine, "space", swapped)
    other_top = lax.ppermute(top, "space", swapped)
    second = [lax.ppermute(other, "space", around)]
    hops = chips // 2
    for s in range(1, hops):
        first.append(lax.ppermute(first[-1], "space", around))
        if s < hops - 1:
            second.append(lax.ppermute(second[-1], "space", around))

    own, both_t, total = pl.pallas_call(
        own_kernel,
        out_shape=(
            f32(CORES * width, width),
            jax.ShapeDtypeStruct((CORES * width, depth), jnp.bfloat16),
            f32(arrow, CORES * width),
        ),
        name="own",
    )(mine, other, top, other_top)
    kept, given = [], []
    for s in range(hops - 1):
        keep, give, total = pl.pallas_call(
            far_kernel,
            out_shape=(f32(2 * width, width), f32(2 * width, width), f32(arrow, CORES * width)),
            name="far",
        )(first[s], second[s], both_t, total)
        kept.append(keep)
        given.append(lax.ppermute(give, "space", swapped))
    keep, give = pl.pallas_call(
        farthest_kernel, out_shape=(f32(width + arrow, width), f32(width + arrow, width)), name="farthest"
    )(first[-1], both_t, total)
    kept.append(keep)
    given.append(lax.ppermute(give, "space", swapped))

    by_col = lax.dynamic_slice_in_dim(decay, column_at * width, width, axis=1)
    decay_rows = decay[0].reshape(pieces, rows)
    row_parts = jnp.concatenate(two_parts(decay_rows), axis=1)
    row_parts = jnp.pad(row_parts, ((0, 0), (0, width - 2 * rows)))
    col_parts = jnp.pad(jnp.concatenate(two_parts(by_col), axis=0), ((5, PAD - 7), (0, 0)))
    message = f32(pieces, rows + PAD, width)
    vmem, smem = pl.BlockSpec(memory_space=pltpu.VMEM), pl.BlockSpec(memory_space=pltpu.SMEM)
    sent = pl.pallas_call(
        lambda *refs: message_kernel(rows, chips, *refs),
        out_shape=message,
        in_specs=[smem] + [vmem] * (2 * hops + 4),
        name="message",
    )(column_at.reshape(1), own, *kept, *given, tip_inverse.T, row_parts, col_parts)

    def exchange(values):
        moved = lax.all_to_all(values.astype(jnp.float16), "tm", 0, 0, tiled=True)
        return moved.astype(jnp.float32)

    end = jnp.concatenate(
        [
            lax.dynamic_slice_in_dim(sigma_end, piece_at * rows, rows, axis=0),
            lax.dynamic_slice_in_dim(arrow_end.T, piece_at * share, share, axis=0),
            jnp.zeros((PAD - share, width), jnp.float32),
        ],
        axis=0,
    )
    ahead = pl.pallas_call(
        lambda *refs: scan_kernel(rows, *refs),
        out_shape=message,
        scratch_shapes=[pltpu.VMEM((pieces, width), jnp.float32)],
        name="suffix",
    )(exchange(sent), end)
    sigma, arrows = pl.pallas_call(
        lambda *refs: last_kernel(rows, *refs),
        out_shape=(f32(order, width), f32(arrow, width)),
        name="last",
    )(sent, exchange(ahead), jnp.pad(decay_rows, ((0, 0), (0, width - rows))), by_col)
    return sigma[None], arrows.T[None]


def solution(mesh):
    placed = (
        P("tm", None, "space"),
        P("tm", None, "space"),
        P("tm", None),
        P(),
        P(None, "space"),
        P("space", None),
    )
    return jax.shard_map(
        body,
        mesh=mesh,
        in_specs=placed,
        out_specs=(P("tm", None, "space"), P("tm", "space", None)),
        check_vma=False,
    )
```

```python
import jax
import jax.numpy as jnp
from jax import lax
from jax.experimental import pallas as pl
from jax.experimental.pallas import tpu as pltpu
from jax.sharding import PartitionSpec as P

CORES = 2
PAD = 8
TOP = 14.0
DECAY = 1024.0


def split3(x):
    hi = x.astype(jnp.bfloat16)
    rest = x - hi.astype(jnp.float32)
    mid = rest.astype(jnp.bfloat16)
    low = (rest - mid.astype(jnp.float32)).astype(jnp.bfloat16)
    return hi, mid, low


def dot(a, b):
    return jnp.dot(a, b, preferred_element_type=jnp.float32)


def border_times(border, tile):
    hi, mid, low = split3(tile)
    return dot(border, hi) + dot(border, mid) + dot(border, low)


def exponent(x):
    largest = jnp.max(jnp.abs(x), axis=0, keepdims=True)
    return jnp.ceil(jnp.log2(jnp.maximum(largest, 2.0**-100)))


def squared(x, level):
    unit = x * jnp.exp2(TOP / 2 - level)
    return unit * jnp.abs(unit)


def rooted(x, level):
    root = jnp.sqrt(jnp.abs(x))
    return jnp.where(x < 0, -root, root) * jnp.exp2(level - TOP / 2)


def encode(panel, pair, extra):
    at = lax.broadcasted_iota(jnp.int32, pair.shape, 0)
    level, pair_level = exponent(panel), exponent(pair)
    tail = jnp.where(at < 2, squared(pair, pair_level), extra)
    tail = jnp.where(at == 2, level, jnp.where(at == 3, pair_level, tail))
    return squared(panel, level), tail


def decode(message, rows):
    tail = message[rows:, :]
    at = lax.broadcasted_iota(jnp.int32, tail.shape, 0)
    panel = rooted(message[:rows, :], tail[2:3, :])
    return panel, jnp.where(at < 2, rooted(tail, tail[3:4, :]), 0.0)


def own_kernel(mine, other, mine_top, other_top, tile, both_t, total):
    tall = mine.shape[0]
    depth = both_t.shape[1]
    turned = jnp.concatenate([mine[:depth, :].T, other[:depth, :].T], axis=0)
    top = jnp.concatenate([mine_top[...].T, other_top[...].T], axis=0)
    both_t[...] = turned
    got = dot(turned, mine[:depth, :]) + dot(top, mine_top[...])
    tile[...] = got
    border = jnp.concatenate([mine[depth:tall, :], other[depth:tall, :]], axis=1)
    total[...] = jnp.concatenate([border_times(border, got), jnp.zeros(total.shape[:1] + got.shape[1:])], axis=1)


def far_tiles(panels, both_t, before):
    depth = both_t.shape[1]
    tall = panels[0].shape[0]
    joined = jnp.concatenate([p[:depth, :] for p in panels], axis=1)
    border = jnp.concatenate([p[depth:tall, :] for p in panels], axis=1)
    tile = dot(both_t[...], joined).T
    return tile, before[...] + border_times(border, tile)


def far_kernel(first, second, both_t, before, keep, give, total):
    tile, total[...] = far_tiles((first, second), both_t, before)
    width = keep.shape[1]
    keep[...] = tile[:, :width]
    give[...] = tile[:, width:]


def farthest_kernel(first, both_t, before, keep, give):
    tile, total = far_tiles((first,), both_t, before)
    width = keep.shape[1]
    count = tile.shape[0]
    keep[:count, :] = tile[:, :width]
    keep[count:, :] = total[:, :width]
    give[:count, :] = tile[:, width:]
    give[count:, :] = total[:, width:]


def message_kernel(rows, chips, hops, at, own, *refs):
    kept, given = refs[:hops], refs[hops : 2 * hops]
    tip_t, decay_rows, decay_cols, out, copied, own_arrow, plain, done = refs[2 * hops :]
    width = own.shape[1]
    per = width // rows
    chip, core = at[0] // CORES, at[0] % CORES
    way = 1 - 2 * core

    def put(block, hop, parity):
        spot = lax.rem(chip + hop + chips, chips) * CORES + parity
        plain[pl.ds(spot * per, per), :, :] = block.reshape(per, rows, width)

    put(own[:width, :], 0, core)
    put(own[width:, :], 0, 1 - core)
    for s in range(hops):
        hop = (s + 1) * way
        put(kept[s][:width, :], -hop, core)
        put(given[s][:width, :], hop, 1 - core)
        if s < hops - 1:
            put(kept[s][width:, :], -hop, 1 - core)
            put(given[s][width:, :], hop, core)
    copy = pltpu.make_async_copy(plain, copied, done)
    copy.start()
    total = kept[-1][width:, :] + given[-1][width:, :]
    arrow = -jnp.dot(tip_t[...], total, precision=lax.Precision.HIGHEST, preferred_element_type=jnp.float32)
    own_arrow[...] = arrow
    fill = jnp.zeros((PAD - 2, width), jnp.float32)
    cols = decay_cols[...]
    place = lax.broadcasted_iota(jnp.int32, cols.shape, 0)
    for r in range(out.shape[0]):
        extra = jnp.where(place == 4, decay_rows[r : r + 1, :], cols)
        pair = jnp.concatenate([arrow[2 * r : 2 * r + 2, :], fill], axis=0)
        out[r, :rows, :], out[r, rows:, :] = encode(plain[r], pair, extra)
    copy.wait()


def scan_kernel(rows, got, end, out, turned):
    pieces, _, width = got.shape
    for s in range(pieces):
        turned[s : s + 1, :] = got[s, rows + 4 : rows + 5, :]
    columns = turned[...].T
    columns = (columns[:rows, :] + columns[rows : 2 * rows, :] * (1 / 256)) * (1 / DECAY)
    carry, pair = end[:rows, :], end[rows:, :]
    for s in range(pieces - 1, -1, -1):
        out[s, :rows, :], out[s, rows:, :] = encode(carry, pair, jnp.zeros_like(pair))
        if s == 0:
            break
        panel, arrow = decode(got[s], rows)
        by_col = (got[s, rows + 5 : rows + 6, :] + got[s, rows + 6 : rows + 7, :] * (1 / 256)) * (1 / DECAY)
        by_row = jnp.broadcast_to(columns[:, s : s + 1], (rows, width))
        carry = panel + by_row * by_col * carry
        pair = arrow + by_col * pair


def last_kernel(rows, plain, own_arrow, got, decay_rows, by_col, sigma, arrows):
    columns = decay_rows[...].T[:rows, :]
    for r in range(plain.shape[0]):
        later, later_arrow = decode(got[r], rows)
        by_row = jnp.broadcast_to(columns[:, r : r + 1], later.shape)
        sigma[r * rows : (r + 1) * rows, :] = plain[r] + by_row * by_col[...] * later
        pair = slice(2 * r, 2 * r + 2)
        arrows[pair, :] = own_arrow[pair, :] + by_col[...] * later_arrow[:2, :]


def two_parts(decay):
    scaled = decay * DECAY
    high = lax.reduce_precision(scaled, 8, 7)
    return high, (scaled - high) * 256


VMEM = pl.BlockSpec(memory_space=pltpu.VMEM)
SMEM = pl.BlockSpec(memory_space=pltpu.SMEM)


def near(x):
    return pltpu.with_memory_space_constraint(x, pltpu.VMEM)


def held(kernel, name, results, *operands, scratch=()):
    return pl.pallas_call(
        kernel,
        out_shape=tuple(pltpu.VMEM(shape, dtype) for shape, dtype in results),
        in_specs=[VMEM] * len(operands),
        out_specs=(VMEM,) * len(results),
        scratch_shapes=scratch,
        name=name,
    )(*map(near, operands))


def body(inverse_factor, arrow_factor, decay, tip_inverse, sigma_end, arrow_end):
    factor_cols = inverse_factor[0]
    order, width = factor_cols.shape
    arrow = tip_inverse.shape[0]
    pieces, devices = lax.axis_size("tm"), lax.axis_size("space")
    chips, cut = devices // CORES, CORES * width
    rows, share = order // pieces, arrow // pieces
    column_at = lax.axis_index("space")
    piece_at = lax.axis_index("tm")
    swapped = [(p, p ^ 1) for p in range(devices)]
    around = [
        (p, (p // CORES + 1 - 2 * (p % CORES)) % chips * CORES + p % CORES) for p in range(devices)
    ]
    depth, both = order - cut, CORES * width
    tall, hops = depth + arrow, chips // 2
    f32, bf16 = jnp.float32, jnp.bfloat16

    def pack_kernel(cols, border, out, top):
        out[:depth, :] = cols[cut:, :]
        out[depth:, :] = border[...]
        top[...] = cols[:cut, :]

    mine, top = pl.pallas_call(
        pack_kernel,
        out_shape=(pltpu.VMEM((tall, width), bf16), pltpu.VMEM((cut, width), bf16)),
        in_specs=[VMEM, VMEM],
        out_specs=(VMEM, VMEM),
        name="pack",
    )(factor_cols, arrow_factor[0])
    first = lax.ppermute(mine, "space", around)
    other = lax.ppermute(mine, "space", swapped)
    other_top = lax.ppermute(top, "space", swapped)
    second = lax.ppermute(other, "space", around)
    own, both_t, total = pl.pallas_call(
        own_kernel,
        out_shape=tuple(map(jax.ShapeDtypeStruct, ((both, width), (both, depth), (arrow, both)), (f32, bf16, f32))),
        name="own",
    )(mine, other, top, other_top)
    kept, given = [], []
    second, total = lax.optimization_barrier((second, total))
    for s in range(hops - 1):
        next_first = lax.ppermute(first, "space", around)
        next_second = lax.ppermute(second, "space", around) if s < hops - 2 else None
        keep, give, total = pl.pallas_call(
            far_kernel,
            out_shape=[jax.ShapeDtypeStruct(shape, f32) for shape in ((both, width), (both, width), (arrow, both))],
            name="far",
        )(first, second, both_t, total)
        kept.append(keep)
        given.append(lax.ppermute(give, "space", swapped))
        first, second = next_first, next_second
        if s < hops - 2:
            first, total = lax.optimization_barrier((first, total))
    keep, give = held(farthest_kernel, "farthest", (((width + arrow, width), f32),) * 2, first, both_t, total)
    kept.append(keep)
    given.append(lax.ppermute(give, "space", swapped))

    by_col = lax.dynamic_slice_in_dim(decay, column_at * width, width, axis=1)
    decay_rows = decay[0].reshape(pieces, rows)
    row_parts = jnp.concatenate(two_parts(decay_rows), axis=1)
    row_parts = jnp.pad(row_parts, ((0, 0), (0, width - 2 * rows)))
    col_parts = jnp.pad(jnp.concatenate(two_parts(by_col), axis=0), ((5, PAD - 7), (0, 0)))
    message = ((pieces, rows + PAD, width), f32)
    pairs = [*kept[:-1], near(kept[-1]), *given[:-1], near(given[-1])]
    sent, plain, own_arrow = pl.pallas_call(
        lambda *refs: message_kernel(rows, chips, hops, *refs),
        out_shape=(
            pltpu.VMEM(*message),
            jax.ShapeDtypeStruct((pieces, rows, width), f32),
            jax.ShapeDtypeStruct((arrow, width), f32),
        ),
        in_specs=[SMEM] + [VMEM] * (2 * hops + 4),
        out_specs=(VMEM, pl.BlockSpec(memory_space=pl.ANY), VMEM),
        scratch_shapes=[pltpu.VMEM((pieces, rows, width), f32), pltpu.SemaphoreType.DMA],
        name="message",
    )(column_at.reshape(1), own, *pairs, near(tip_inverse.T), near(row_parts), near(col_parts))

    def exchange(values):
        moved = lax.all_to_all(values.astype(jnp.float16), "tm", 0, 0, tiled=True)
        return moved.astype(jnp.float32)

    end = jnp.concatenate(
        [
            lax.dynamic_slice_in_dim(sigma_end, piece_at * rows, rows, axis=0),
            lax.dynamic_slice_in_dim(arrow_end.T, piece_at * share, share, axis=0),
            jnp.zeros((PAD - share, width), jnp.float32),
        ],
        axis=0,
    )
    (ahead,) = held(
        lambda *refs: scan_kernel(rows, *refs),
        "suffix",
        (message,),
        *(exchange(sent), end),
        scratch=[pltpu.VMEM((pieces, width), f32)],
    )
    last = (plain, own_arrow, exchange(ahead), jnp.pad(decay_rows, ((0, 0), (0, width - rows))), by_col)
    sigma, arrows = pl.pallas_call(
        lambda *refs: last_kernel(rows, *refs),
        out_shape=(jax.ShapeDtypeStruct((order, width), f32), jax.ShapeDtypeStruct((arrow, width), f32)),
        in_specs=[VMEM] * len(last),
        name="last",
    )(*map(near, last))
    return sigma[None], arrows.T[None]


def solution(mesh):
    placed = (
        P("tm", None, "space"),
        P("tm", None, "space"),
        P("tm", None),
        P(),
        P(None, "space"),
        P("space", None),
    )
    return jax.shard_map(
        body,
        mesh=mesh,
        in_specs=placed,
        out_specs=(P("tm", None, "space"), P("tm", "space", None)),
        check_vma=False,
    )
```

```python
import jax
import jax.numpy as jnp
from jax import lax
from jax.experimental import pallas as pl
from jax.experimental.pallas import tpu as pltpu
from jax.sharding import PartitionSpec as P

CORES = 2
PAD = 8
TOP = 14.0
DECAY = 1024.0


def split3(x):
    hi = x.astype(jnp.bfloat16)
    rest = x - hi.astype(jnp.float32)
    mid = rest.astype(jnp.bfloat16)
    low = (rest - mid.astype(jnp.float32)).astype(jnp.bfloat16)
    return hi, mid, low


def dot(a, b):
    return jnp.dot(a, b, preferred_element_type=jnp.float32)


def border_times(border, tile):
    hi, mid, low = split3(tile)
    return dot(border, hi) + dot(border, mid) + dot(border, low)


def exponent(x):
    largest = jnp.max(jnp.abs(x), axis=0, keepdims=True)
    return jnp.ceil(jnp.log2(jnp.maximum(largest, 2.0**-100)))


def squared(x, level):
    unit = x * jnp.exp2(TOP / 2 - level)
    return unit * jnp.abs(unit)


def rooted(x, level):
    root = jnp.sqrt(jnp.abs(x))
    return jnp.where(x < 0, -root, root) * jnp.exp2(level - TOP / 2)


def encode(panel, pair, extra):
    at = lax.broadcasted_iota(jnp.int32, pair.shape, 0)
    level, pair_level = exponent(panel), exponent(pair)
    tail = jnp.where(at < 2, squared(pair, pair_level), extra)
    tail = jnp.where(at == 2, level, jnp.where(at == 3, pair_level, tail))
    return squared(panel, level), tail


def decode(message, rows):
    tail = message[rows:, :]
    at = lax.broadcasted_iota(jnp.int32, tail.shape, 0)
    panel = rooted(message[:rows, :], tail[2:3, :])
    return panel, jnp.where(at < 2, rooted(tail, tail[3:4, :]), 0.0)


def own_kernel(mine, other, mine_top, other_top, tile, both_t, total):
    tall = mine.shape[0]
    depth = both_t.shape[1]
    turned = jnp.concatenate([mine[:depth, :].T, other[:depth, :].T], axis=0)
    top = jnp.concatenate([mine_top[...].T, other_top[...].T], axis=0)
    both_t[...] = turned
    got = dot(turned, mine[:depth, :]) + dot(top, mine_top[...])
    tile[...] = got
    border = jnp.concatenate([mine[depth:tall, :], other[depth:tall, :]], axis=1)
    total[...] = jnp.concatenate([border_times(border, got), jnp.zeros(total.shape[:1] + got.shape[1:])], axis=1)


def far_tiles(panels, both_t, before):
    tall = panels[0].shape[0]
    depth = tall - before.shape[0]
    joined = jnp.concatenate([p[:depth, :] for p in panels], axis=1)
    border = jnp.concatenate([p[depth:tall, :] for p in panels], axis=1)
    tile = dot(both_t[:, both_t.shape[1] - depth :], joined).T
    return tile, before[...] + border_times(border, tile)


def far_kernel(first, second, both_t, before, keep, give, total):
    tile, total[...] = far_tiles((first, second), both_t, before)
    width = keep.shape[1]
    keep[...] = tile[:, :width]
    give[...] = tile[:, width:]


def farthest_kernel(first, both_t, before, keep, give):
    tile, total = far_tiles((first,), both_t, before)
    width = keep.shape[1]
    count = tile.shape[0]
    keep[:count, :] = tile[:, :width]
    keep[count:, :] = total[:, :width]
    give[:count, :] = tile[:, width:]
    give[count:, :] = total[:, width:]


def message_kernel(rows, chips, hops, at, own, *refs):
    kept, given = refs[:hops], refs[hops : 2 * hops]
    tip_t, decay_rows, decay_cols, out, copied, own_arrow, plain, done = refs[2 * hops :]
    width = own.shape[1]
    per = width // rows
    chip, core = at[0] // CORES, at[0] % CORES
    way = 1 - 2 * core

    def put(block, hop, parity):
        spot = lax.rem(chip + hop + chips, chips) * CORES + parity
        plain[pl.ds(spot * per, per), :, :] = block.reshape(per, rows, width)

    put(own[:width, :], 0, core)
    put(own[width:, :], 0, 1 - core)
    for s in range(hops):
        hop = (s + 1) * way
        put(kept[s][:width, :], -hop, core)
        put(given[s][:width, :], hop, 1 - core)
        if s < hops - 1:
            put(kept[s][width:, :], -hop, 1 - core)
            put(given[s][width:, :], hop, core)
    copy = pltpu.make_async_copy(plain, copied, done)
    copy.start()
    total = kept[-1][width:, :] + given[-1][width:, :]
    arrow = -jnp.dot(tip_t[...], total, precision=lax.Precision.HIGHEST, preferred_element_type=jnp.float32)
    own_arrow[...] = arrow
    fill = jnp.zeros((PAD - 2, width), jnp.float32)
    cols = decay_cols[...]
    place = lax.broadcasted_iota(jnp.int32, cols.shape, 0)
    for r in range(out.shape[0]):
        extra = jnp.where(place == 4, decay_rows[r : r + 1, :], cols)
        pair = jnp.concatenate([arrow[2 * r : 2 * r + 2, :], fill], axis=0)
        out[r, :rows, :], out[r, rows:, :] = encode(plain[r], pair, extra)
    copy.wait()


def scan_kernel(rows, got, end, out, turned):
    pieces, _, width = got.shape
    for s in range(pieces):
        turned[s : s + 1, :] = got[s, rows + 4 : rows + 5, :]
    columns = turned[...].T
    columns = (columns[:rows, :] + columns[rows : 2 * rows, :] * (1 / 256)) * (1 / DECAY)
    carry, pair = end[:rows, :], end[rows:, :]
    for s in range(pieces - 1, -1, -1):
        out[s, :rows, :], out[s, rows:, :] = encode(carry, pair, jnp.zeros_like(pair))
        if s == 0:
            break
        panel, arrow = decode(got[s], rows)
        by_col = (got[s, rows + 5 : rows + 6, :] + got[s, rows + 6 : rows + 7, :] * (1 / 256)) * (1 / DECAY)
        by_row = jnp.broadcast_to(columns[:, s : s + 1], (rows, width))
        carry = panel + by_row * by_col * carry
        pair = arrow + by_col * pair


def last_kernel(rows, plain, own_arrow, got, decay_rows, by_col, sigma, arrows):
    columns = decay_rows[...].T[:rows, :]
    for r in range(plain.shape[0]):
        later, later_arrow = decode(got[r], rows)
        by_row = jnp.broadcast_to(columns[:, r : r + 1], later.shape)
        sigma[r * rows : (r + 1) * rows, :] = plain[r] + by_row * by_col[...] * later
        pair = slice(2 * r, 2 * r + 2)
        arrows[pair, :] = own_arrow[pair, :] + by_col[...] * later_arrow[:2, :]


def two_parts(decay):
    scaled = decay * DECAY
    high = lax.reduce_precision(scaled, 8, 7)
    return high, (scaled - high) * 256


VMEM = pl.BlockSpec(memory_space=pltpu.VMEM)
SMEM = pl.BlockSpec(memory_space=pltpu.SMEM)


def near(x):
    return pltpu.with_memory_space_constraint(x, pltpu.VMEM)


def held(kernel, name, results, *operands, scratch=()):
    return pl.pallas_call(
        kernel,
        out_shape=tuple(pltpu.VMEM(shape, dtype) for shape, dtype in results),
        in_specs=[VMEM] * len(operands),
        out_specs=(VMEM,) * len(results),
        scratch_shapes=scratch,
        name=name,
    )(*map(near, operands))


def body(inverse_factor, arrow_factor, decay, tip_inverse, sigma_end, arrow_end):
    factor_cols = inverse_factor[0]
    order, width = factor_cols.shape
    arrow = tip_inverse.shape[0]
    pieces, devices = lax.axis_size("tm"), lax.axis_size("space")
    chips, cut = devices // CORES, CORES * width
    rows, share = order // pieces, arrow // pieces
    column_at = lax.axis_index("space")
    piece_at = lax.axis_index("tm")
    swapped = [(p, p ^ 1) for p in range(devices)]
    around = [
        (p, (p // CORES + 1 - 2 * (p % CORES)) % chips * CORES + p % CORES) for p in range(devices)
    ]
    depth, both = order - cut, CORES * width
    tall, hops = depth + arrow, chips // 2
    f32, bf16 = jnp.float32, jnp.bfloat16

    def pack_kernel(cols, border, out, top):
        out[:depth, :] = cols[cut:, :]
        out[depth:, :] = border[...]
        top[...] = cols[:cut, :]

    mine, top = pl.pallas_call(
        pack_kernel,
        out_shape=(pltpu.VMEM((tall, width), bf16), pltpu.VMEM((cut, width), bf16)),
        in_specs=[VMEM, VMEM],
        out_specs=(VMEM, VMEM),
        name="pack",
    )(factor_cols, arrow_factor[0])
    first = lax.ppermute(mine, "space", around)
    other = lax.ppermute(mine, "space", swapped)
    other_top = lax.ppermute(top, "space", swapped)
    second = lax.ppermute(other, "space", around)
    own, both_t, total = pl.pallas_call(
        own_kernel,
        out_shape=(
            jax.ShapeDtypeStruct((both, width), f32),
            pltpu.VMEM((both, depth), bf16),
            pltpu.VMEM((arrow, both), f32),
        ),
        in_specs=[VMEM] * 4,
        out_specs=(VMEM,) * 3,
        name="own",
    )(*map(near, (mine, other, top, other_top)))
    kept, given = [], []
    second, total = lax.optimization_barrier((second, total))
    for s in range(hops - 1):
        skip = cut * (s + 2) - (order + arrow - first.shape[0]) if s > 0 else 0
        next_first = lax.ppermute(first[skip:], "space", around)
        next_second = lax.ppermute(second[skip:], "space", around) if s < hops - 2 else None
        keep, give, total = pl.pallas_call(
            far_kernel,
            out_shape=(*[jax.ShapeDtypeStruct((both, width), f32)] * 2, pltpu.VMEM((arrow, both), f32)),
            in_specs=[VMEM] * 4,
            out_specs=(VMEM,) * 3,
            name="far",
        )(*map(near, (first, second, both_t, total)))
        kept.append(keep)
        given.append(lax.ppermute(give, "space", swapped))
        first, second = next_first, next_second
        if s < hops - 2:
            first, total = lax.optimization_barrier((first, total))
    keep, give = held(farthest_kernel, "farthest", (((width + arrow, width), f32),) * 2, first, both_t, total)
    kept.append(keep)
    given.append(lax.ppermute(give, "space", swapped))

    by_col = lax.dynamic_slice_in_dim(decay, column_at * width, width, axis=1)
    decay_rows = decay[0].reshape(pieces, rows)
    row_parts = jnp.concatenate(two_parts(decay_rows), axis=1)
    row_parts = jnp.pad(row_parts, ((0, 0), (0, width - 2 * rows)))
    col_parts = jnp.pad(jnp.concatenate(two_parts(by_col), axis=0), ((5, PAD - 7), (0, 0)))
    message = ((pieces, rows + PAD, width), f32)
    sent, plain, own_arrow = pl.pallas_call(
        lambda *refs: message_kernel(rows, chips, hops, *refs),
        out_shape=(
            pltpu.VMEM(*message),
            jax.ShapeDtypeStruct((pieces, rows, width), f32),
            jax.ShapeDtypeStruct((arrow, width), f32),
        ),
        in_specs=[SMEM] + [VMEM] * (2 * hops + 4),
        out_specs=(VMEM, pl.BlockSpec(memory_space=pl.ANY), VMEM),
        scratch_shapes=[pltpu.VMEM((pieces, rows, width), f32), pltpu.SemaphoreType.DMA],
        name="message",
    )(column_at.reshape(1), *map(near, (own, *kept, *given, tip_inverse.T, row_parts, col_parts)))

    def exchange(values):
        moved = lax.all_to_all(values.astype(jnp.float16), "tm", 0, 0, tiled=True)
        return moved.astype(jnp.float32)

    end = jnp.concatenate(
        [
            lax.dynamic_slice_in_dim(sigma_end, piece_at * rows, rows, axis=0),
            lax.dynamic_slice_in_dim(arrow_end.T, piece_at * share, share, axis=0),
            jnp.zeros((PAD - share, width), jnp.float32),
        ],
        axis=0,
    )
    (ahead,) = held(
        lambda *refs: scan_kernel(rows, *refs),
        "suffix",
        (message,),
        *(exchange(sent), end),
        scratch=[pltpu.VMEM((pieces, width), f32)],
    )
    last = (plain, own_arrow, exchange(ahead), jnp.pad(decay_rows, ((0, 0), (0, width - rows))), by_col)
    sigma, arrows = pl.pallas_call(
        lambda *refs: last_kernel(rows, *refs),
        out_shape=(jax.ShapeDtypeStruct((order, width), f32), jax.ShapeDtypeStruct((arrow, width), f32)),
        in_specs=[VMEM] * len(last),
        name="last",
    )(*map(near, last))
    return sigma[None], arrows.T[None]


def solution(mesh):
    placed = (
        P("tm", None, "space"),
        P("tm", None, "space"),
        P("tm", None),
        P(),
        P(None, "space"),
        P("space", None),
    )
    return jax.shard_map(
        body,
        mesh=mesh,
        in_specs=placed,
        out_specs=(P("tm", None, "space"), P("tm", "space", None)),
        check_vma=False,
    )
```

```python
import jax
import jax.numpy as jnp
from jax import lax
from jax.experimental import pallas as pl
from jax.experimental.pallas import tpu as pltpu
from jax.sharding import PartitionSpec as P

CORES = 2
PAD = 8
TOP = 14.0
DECAY = 1024.0


def split3(x):
    hi = x.astype(jnp.bfloat16)
    rest = x - hi.astype(jnp.float32)
    mid = rest.astype(jnp.bfloat16)
    low = (rest - mid.astype(jnp.float32)).astype(jnp.bfloat16)
    return hi, mid, low


def dot(a, b):
    return jnp.dot(a, b, preferred_element_type=jnp.float32)


def border_times(border, tile):
    hi, mid, low = split3(tile)
    return dot(border, hi) + dot(border, mid) + dot(border, low)


def exponent(x):
    largest = jnp.max(jnp.abs(x), axis=0, keepdims=True)
    return jnp.ceil(jnp.log2(jnp.maximum(largest, 2.0**-100)))


def squared(x, level):
    unit = x * jnp.exp2(TOP / 2 - level)
    return unit * jnp.abs(unit)


def rooted(x, level):
    root = jnp.sqrt(jnp.abs(x))
    return jnp.where(x < 0, -root, root) * jnp.exp2(level - TOP / 2)


def encode(panel, pair, extra):
    at = lax.broadcasted_iota(jnp.int32, pair.shape, 0)
    level, pair_level = exponent(panel), exponent(pair)
    tail = jnp.where(at < 2, squared(pair, pair_level), extra)
    tail = jnp.where(at == 2, level, jnp.where(at == 3, pair_level, tail))
    return squared(panel, level), tail


def decode(message, rows):
    tail = message[rows:, :]
    at = lax.broadcasted_iota(jnp.int32, tail.shape, 0)
    panel = rooted(message[:rows, :], tail[2:3, :])
    return panel, jnp.where(at < 2, rooted(tail, tail[3:4, :]), 0.0)


def own_kernel(mine, other, mine_top, other_top, tile, both_t, token):
    tall, width = mine.shape
    depth = both_t.shape[1]
    turned = jnp.concatenate([mine[:depth, :].T, other[:depth, :].T], axis=0)
    top = jnp.concatenate([mine_top[...].T, other_top[...].T], axis=0)
    both_t[...] = turned
    got = dot(turned, mine[:depth, :]) + dot(top, mine_top[...])
    border = jnp.concatenate([mine[depth:tall, :], other[depth:tall, :]], axis=1)
    tile[: CORES * width, :] = got
    tile[CORES * width :, :] = border_times(border, got)
    token[...] = jnp.zeros_like(token)


def far_tiles(panels, both_t, keep, give):
    tall, width = panels[0].shape
    count = width * len(panels)
    depth = tall - (keep.shape[0] - count)
    joined = jnp.concatenate([p[:depth, :] for p in panels], axis=1)
    border = jnp.concatenate([p[depth:tall, :] for p in panels], axis=1)
    tile = dot(both_t[:, both_t.shape[1] - depth :], joined).T
    total = border_times(border, tile)
    for at, part in ((0, keep), (width, give)):
        part[:count, :] = tile[:, at : at + width]
        part[count:, :] = total[:, at : at + width]


def far_kernel(first, second, both_t, passed, keep, give, token):
    far_tiles((first, second), both_t, keep, give)
    token[...] = passed[...]


def farthest_kernel(first, both_t, passed, keep, give):
    far_tiles((first,), both_t, keep, give)


def message_kernel(rows, chips, hops, at, own, *refs):
    kept, given = refs[:hops], refs[hops : 2 * hops]
    tip_t, decay_rows, decay_cols, out, copied, own_arrow, plain, done = refs[2 * hops :]
    width = own.shape[1]
    per = width // rows
    chip, core = at[0] // CORES, at[0] % CORES
    way = 1 - 2 * core

    def put(block, hop, parity):
        spot = lax.rem(chip + hop + chips, chips) * CORES + parity
        plain[pl.ds(spot * per, per), :, :] = block.reshape(per, rows, width)

    put(own[:width, :], 0, core)
    put(own[width : CORES * width, :], 0, 1 - core)
    for s in range(hops):
        hop = (s + 1) * way
        put(kept[s][:width, :], -hop, core)
        put(given[s][:width, :], hop, 1 - core)
        if s < hops - 1:
            put(kept[s][width : 2 * width, :], -hop, 1 - core)
            put(given[s][width : 2 * width, :], hop, core)
    copy = pltpu.make_async_copy(plain, copied, done)
    copy.start()
    border = own_arrow.shape[0]
    total = own[CORES * width :, :]
    for part in (*kept, *given):
        total = total + part[part.shape[0] - border :, :]
    arrow = -jnp.dot(tip_t[...], total, precision=lax.Precision.HIGHEST, preferred_element_type=jnp.float32)
    own_arrow[...] = arrow
    fill = jnp.zeros((PAD - 2, width), jnp.float32)
    cols = decay_cols[...]
    place = lax.broadcasted_iota(jnp.int32, cols.shape, 0)
    for r in range(out.shape[0]):
        extra = jnp.where(place == 4, decay_rows[r : r + 1, :], cols)
        pair = jnp.concatenate([arrow[2 * r : 2 * r + 2, :], fill], axis=0)
        out[r, :rows, :], out[r, rows:, :] = encode(plain[r], pair, extra)
    copy.wait()


def scan_kernel(rows, got, end, out, turned):
    pieces, _, width = got.shape
    for s in range(pieces):
        turned[s : s + 1, :] = got[s, rows + 4 : rows + 5, :]
    columns = turned[...].T
    columns = (columns[:rows, :] + columns[rows : 2 * rows, :] * (1 / 256)) * (1 / DECAY)
    carry, pair = end[:rows, :], end[rows:, :]
    for s in range(pieces - 1, -1, -1):
        out[s, :rows, :], out[s, rows:, :] = encode(carry, pair, jnp.zeros_like(pair))
        if s == 0:
            break
        panel, arrow = decode(got[s], rows)
        by_col = (got[s, rows + 5 : rows + 6, :] + got[s, rows + 6 : rows + 7, :] * (1 / 256)) * (1 / DECAY)
        by_row = jnp.broadcast_to(columns[:, s : s + 1], (rows, width))
        carry = panel + by_row * by_col * carry
        pair = arrow + by_col * pair


def last_kernel(rows, plain, own_arrow, got, decay_rows, by_col, sigma, arrows):
    columns = decay_rows[...].T[:rows, :]
    for r in range(plain.shape[0]):
        later, later_arrow = decode(got[r], rows)
        by_row = jnp.broadcast_to(columns[:, r : r + 1], later.shape)
        sigma[r * rows : (r + 1) * rows, :] = plain[r] + by_row * by_col[...] * later
        pair = slice(2 * r, 2 * r + 2)
        arrows[pair, :] = own_arrow[pair, :] + by_col[...] * later_arrow[:2, :]


def two_parts(decay):
    scaled = decay * DECAY
    high = lax.reduce_precision(scaled, 8, 7)
    return high, (scaled - high) * 256


VMEM = pl.BlockSpec(memory_space=pltpu.VMEM)
SMEM = pl.BlockSpec(memory_space=pltpu.SMEM)


SMALL = pltpu.CompilerParams(vmem_limit_bytes=12 << 20)


def near(x):
    return pltpu.with_memory_space_constraint(x, pltpu.VMEM)


def held(kernel, name, results, *operands, scratch=()):
    return pl.pallas_call(
        kernel,
        out_shape=tuple(pltpu.VMEM(shape, dtype) for shape, dtype in results),
        in_specs=[VMEM] * len(operands),
        out_specs=(VMEM,) * len(results),
        scratch_shapes=scratch,
        compiler_params=SMALL,
        name=name,
    )(*map(near, operands))


def body(inverse_factor, arrow_factor, decay, tip_inverse, sigma_end, arrow_end):
    factor_cols = inverse_factor[0]
    order, width = factor_cols.shape
    arrow = tip_inverse.shape[0]
    pieces, devices = lax.axis_size("tm"), lax.axis_size("space")
    chips, cut = devices // CORES, CORES * width
    rows, share = order // pieces, arrow // pieces
    column_at = lax.axis_index("space")
    piece_at = lax.axis_index("tm")
    swapped = [(p, p ^ 1) for p in range(devices)]
    around = [
        (p, (p // CORES + 1 - 2 * (p % CORES)) % chips * CORES + p % CORES) for p in range(devices)
    ]
    depth, both = order - cut, CORES * width
    tall, hops = depth + arrow, chips // 2
    f32, bf16 = jnp.float32, jnp.bfloat16

    def pack_kernel(cols, border, out, top):
        out[:depth, :] = cols[cut:, :]
        out[depth:, :] = border[...]
        top[...] = cols[:cut, :]

    mine, top = pl.pallas_call(
        pack_kernel,
        out_shape=(pltpu.VMEM((tall, width), bf16), pltpu.VMEM((cut, width), bf16)),
        in_specs=[VMEM, VMEM],
        out_specs=(VMEM, VMEM),
        compiler_params=SMALL,
        name="pack",
    )(factor_cols, arrow_factor[0])
    first = lax.ppermute(mine, "space", around)
    other = lax.ppermute(mine, "space", swapped)
    other_top = lax.ppermute(top, "space", swapped)
    second = lax.ppermute(other, "space", around)
    mark = jax.ShapeDtypeStruct((8, width), f32)
    own, both_t, token = pl.pallas_call(
        own_kernel,
        out_shape=(
            pltpu.VMEM((both + arrow, width), f32),
            pltpu.VMEM((both, depth), bf16),
            mark,
        ),
        in_specs=[VMEM] * 4,
        out_specs=(VMEM,) * 3,
        compiler_params=SMALL,
        name="own",
    )(*map(near, (mine, other, top, other_top)))
    kept, given = [], []
    second, token = lax.optimization_barrier((second, token))
    for s in range(hops - 1):
        skip = cut * (s + 2) - (order + arrow - first.shape[0]) if s > 0 else 0
        next_first = lax.ppermute(first[skip:], "space", around)
        next_second = lax.ppermute(second[skip:], "space", around) if s < hops - 2 else None
        keep, give, token = pl.pallas_call(
            far_kernel,
            out_shape=(*[pltpu.VMEM((both + arrow, width), f32)] * 2, mark),
            in_specs=[VMEM] * 4,
            out_specs=(VMEM,) * 3,
            compiler_params=SMALL,
            name="far",
        )(*map(near, (first, second, both_t)), token)
        kept.append(keep)
        given.append(lax.ppermute(give, "space", swapped))
        first, second = next_first, next_second
        if s < hops - 2:
            first, token = lax.optimization_barrier((first, token))
    keep, give = held(farthest_kernel, "farthest", (((width + arrow, width), f32),) * 2, first, both_t, token)
    kept.append(keep)
    given.append(lax.ppermute(give, "space", swapped))

    by_col = lax.dynamic_slice_in_dim(decay, column_at * width, width, axis=1)
    decay_rows = decay[0].reshape(pieces, rows)
    row_parts = jnp.concatenate(two_parts(decay_rows), axis=1)
    row_parts = jnp.pad(row_parts, ((0, 0), (0, width - 2 * rows)))
    col_parts = jnp.pad(jnp.concatenate(two_parts(by_col), axis=0), ((5, PAD - 7), (0, 0)))
    message = ((pieces, rows + PAD, width), f32)
    sent, plain, own_arrow = pl.pallas_call(
        lambda *refs: message_kernel(rows, chips, hops, *refs),
        out_shape=(
            pltpu.VMEM(*message),
            jax.ShapeDtypeStruct((pieces, rows, width), f32),
            jax.ShapeDtypeStruct((arrow, width), f32),
        ),
        in_specs=[SMEM] + [VMEM] * (2 * hops + 4),
        out_specs=(VMEM, pl.BlockSpec(memory_space=pl.ANY), VMEM),
        scratch_shapes=[pltpu.VMEM((pieces, rows, width), f32), pltpu.SemaphoreType.DMA],
        compiler_params=SMALL,
        name="message",
    )(column_at.reshape(1), *map(near, (own, *kept, *given, tip_inverse.T, row_parts, col_parts)))

    def exchange(values):
        moved = lax.all_to_all(values.astype(jnp.float16), "tm", 0, 0, tiled=True)
        return moved.astype(jnp.float32)

    end = jnp.concatenate(
        [
            lax.dynamic_slice_in_dim(sigma_end, piece_at * rows, rows, axis=0),
            lax.dynamic_slice_in_dim(arrow_end.T, piece_at * share, share, axis=0),
            jnp.zeros((PAD - share, width), jnp.float32),
        ],
        axis=0,
    )
    (ahead,) = held(
        lambda *refs: scan_kernel(rows, *refs),
        "suffix",
        (message,),
        *(exchange(sent), end),
        scratch=[pltpu.VMEM((pieces, width), f32)],
    )
    last = (plain, own_arrow, exchange(ahead), jnp.pad(decay_rows, ((0, 0), (0, width - rows))), by_col)
    sigma, arrows = pl.pallas_call(
        lambda *refs: last_kernel(rows, *refs),
        out_shape=(jax.ShapeDtypeStruct((order, width), f32), jax.ShapeDtypeStruct((arrow, width), f32)),
        in_specs=[VMEM] * len(last),
        compiler_params=SMALL,
        name="last",
    )(*map(near, last))
    return sigma[None], arrows.T[None]


def solution(mesh):
    placed = (
        P("tm", None, "space"),
        P("tm", None, "space"),
        P("tm", None),
        P(),
        P(None, "space"),
        P("space", None),
    )
    return jax.shard_map(
        body,
        mesh=mesh,
        in_specs=placed,
        out_specs=(P("tm", None, "space"), P("tm", "space", None)),
        check_vma=False,
    )
```

```python
import jax
import jax.numpy as jnp
from jax import lax
from jax.experimental import pallas as pl
from jax.experimental.pallas import tpu as pltpu
from jax.sharding import PartitionSpec as P

CORES = 2
PAD = 8
TOP = 14.0
DECAY = 1024.0


def split3(x):
    hi = x.astype(jnp.bfloat16)
    rest = x - hi.astype(jnp.float32)
    mid = rest.astype(jnp.bfloat16)
    low = (rest - mid.astype(jnp.float32)).astype(jnp.bfloat16)
    return hi, mid, low


def dot(a, b):
    return jnp.dot(a, b, preferred_element_type=jnp.float32)


def border_times(border, tile):
    hi, mid, low = split3(tile)
    return dot(border, hi) + dot(border, mid) + dot(border, low)


def exponent(x):
    largest = jnp.max(jnp.abs(x), axis=0, keepdims=True)
    return jnp.ceil(jnp.log2(jnp.maximum(largest, 2.0**-100)))


def squared(x, level):
    unit = x * jnp.exp2(TOP / 2 - level)
    return unit * jnp.abs(unit)


def rooted(x, level):
    root = jnp.sqrt(jnp.abs(x))
    return jnp.where(x < 0, -root, root) * jnp.exp2(level - TOP / 2)


def encode(panel, pair, extra):
    at = lax.broadcasted_iota(jnp.int32, pair.shape, 0)
    level, pair_level = exponent(panel), exponent(pair)
    tail = jnp.where(at < 2, squared(pair, pair_level), extra)
    tail = jnp.where(at == 2, level, jnp.where(at == 3, pair_level, tail))
    return squared(panel, level), tail


def decode(message, rows):
    tail = message[rows:, :]
    at = lax.broadcasted_iota(jnp.int32, tail.shape, 0)
    panel = rooted(message[:rows, :], tail[2:3, :])
    return panel, jnp.where(at < 2, rooted(tail, tail[3:4, :]), 0.0)


def own_kernel(mine, other, mine_top, other_top, tile, both_t, token):
    tall, width = mine.shape
    depth = both_t.shape[1]
    turned = jnp.concatenate([mine[:depth, :].T, other[:depth, :].T], axis=0)
    top = jnp.concatenate([mine_top[...].T, other_top[...].T], axis=0)
    both_t[...] = turned
    got = dot(turned, mine[:depth, :]) + dot(top, mine_top[...])
    border = jnp.concatenate([mine[depth:tall, :], other[depth:tall, :]], axis=1)
    tile[: CORES * width, :] = got
    tile[CORES * width :, :] = border_times(border, got)
    token[...] = jnp.zeros_like(token)


def far_tiles(panels, both_t, keep, give):
    tall, width = panels[0].shape
    count = width * len(panels)
    depth = tall - (keep.shape[0] - count)
    joined = jnp.concatenate([p[:depth, :] for p in panels], axis=1)
    border = jnp.concatenate([p[depth:tall, :] for p in panels], axis=1)
    tile = dot(both_t[:, both_t.shape[1] - depth :], joined).T
    total = border_times(border, tile)
    for at, part in ((0, keep), (width, give)):
        part[:count, :] = tile[:, at : at + width]
        part[count:, :] = total[:, at : at + width]


def far_kernel(first, second, both_t, passed, keep, give, token):
    far_tiles((first, second), both_t, keep, give)
    token[...] = passed[...]


def farthest_kernel(first, both_t, passed, keep, give):
    far_tiles((first,), both_t, keep, give)


def message_kernel(rows, chips, hops, at, own, *refs):
    kept, given = refs[:hops], refs[hops : 2 * hops]
    tip_t, decay_rows, decay_cols, out, copied, own_arrow, plain, done = refs[2 * hops :]
    width = own.shape[1]
    per = width // rows
    chip, core = at[0] // CORES, at[0] % CORES
    way = 1 - 2 * core

    def put(block, hop, parity):
        spot = lax.rem(chip + hop + chips, chips) * CORES + parity
        plain[pl.ds(spot * per, per), :, :] = block.reshape(per, rows, width)

    put(own[:width, :], 0, core)
    put(own[width : CORES * width, :], 0, 1 - core)
    for s in range(hops):
        hop = (s + 1) * way
        put(kept[s][:width, :], -hop, core)
        put(given[s][:width, :], hop, 1 - core)
        if s < hops - 1:
            put(kept[s][width : 2 * width, :], -hop, 1 - core)
            put(given[s][width : 2 * width, :], hop, core)
    copy = pltpu.make_async_copy(plain, copied, done)
    copy.start()
    border = own_arrow.shape[0]
    total = own[CORES * width :, :]
    for part in (*kept, *given):
        total = total + part[part.shape[0] - border :, :]
    arrow = -jnp.dot(tip_t[...], total, precision=lax.Precision.HIGHEST, preferred_element_type=jnp.float32)
    own_arrow[...] = arrow
    fill = jnp.zeros((PAD - 2, width), jnp.float32)
    cols = decay_cols[...]
    place = lax.broadcasted_iota(jnp.int32, cols.shape, 0)
    for r in range(out.shape[0]):
        extra = jnp.where(place == 4, decay_rows[r : r + 1, :], cols)
        pair = jnp.concatenate([arrow[2 * r : 2 * r + 2, :], fill], axis=0)
        out[r, :rows, :], out[r, rows:, :] = encode(plain[r], pair, extra)
    copy.wait()


def scan_kernel(rows, got, end, out, turned):
    pieces, _, width = got.shape
    for s in range(pieces):
        turned[s : s + 1, :] = got[s, rows + 4 : rows + 5, :]
    columns = turned[...].T
    columns = (columns[:rows, :] + columns[rows : 2 * rows, :] * (1 / 256)) * (1 / DECAY)
    carry, pair = end[:rows, :], end[rows:, :]
    for s in range(pieces - 1, -1, -1):
        out[s, :rows, :], out[s, rows:, :] = encode(carry, pair, jnp.zeros_like(pair))
        if s == 0:
            break
        panel, arrow = decode(got[s], rows)
        by_col = (got[s, rows + 5 : rows + 6, :] + got[s, rows + 6 : rows + 7, :] * (1 / 256)) * (1 / DECAY)
        by_row = jnp.broadcast_to(columns[:, s : s + 1], (rows, width))
        carry = panel + by_row * by_col * carry
        pair = arrow + by_col * pair


def last_kernel(rows, plain, own_arrow, got, decay_rows, by_col, sigma, arrows):
    columns = decay_rows[...].T[:rows, :]
    for r in range(plain.shape[0]):
        later, later_arrow = decode(got[r], rows)
        by_row = jnp.broadcast_to(columns[:, r : r + 1], later.shape)
        sigma[r * rows : (r + 1) * rows, :] = plain[r] + by_row * by_col[...] * later
        pair = slice(2 * r, 2 * r + 2)
        arrows[pair, :] = own_arrow[pair, :] + by_col[...] * later_arrow[:2, :]


def two_parts(decay):
    scaled = decay * DECAY
    high = lax.reduce_precision(scaled, 8, 7)
    return high, (scaled - high) * 256


VMEM = pl.BlockSpec(memory_space=pltpu.VMEM)
SMEM = pl.BlockSpec(memory_space=pltpu.SMEM)


SMALL = pltpu.CompilerParams(vmem_limit_bytes=12 << 20)


def near(x):
    return pltpu.with_memory_space_constraint(x, pltpu.VMEM)


def held(kernel, name, results, *operands, scratch=()):
    return pl.pallas_call(
        kernel,
        out_shape=tuple(pltpu.VMEM(shape, dtype) for shape, dtype in results),
        in_specs=[VMEM] * len(operands),
        out_specs=(VMEM,) * len(results),
        scratch_shapes=scratch,
        compiler_params=SMALL,
        name=name,
    )(*map(near, operands))


def body(inverse_factor, arrow_factor, decay, tip_inverse, sigma_end, arrow_end):
    factor_cols = inverse_factor[0]
    order, width = factor_cols.shape
    arrow = tip_inverse.shape[0]
    pieces, devices = lax.axis_size("tm"), lax.axis_size("space")
    chips, cut = devices // CORES, CORES * width
    rows, share = order // pieces, arrow // pieces
    column_at = lax.axis_index("space")
    piece_at = lax.axis_index("tm")
    swapped = [(p, p ^ 1) for p in range(devices)]
    around = [
        (p, (p // CORES + 1 - 2 * (p % CORES)) % chips * CORES + p % CORES) for p in range(devices)
    ]
    depth, both = order - cut, CORES * width
    tall, hops = depth + arrow, chips // 2
    f32, bf16 = jnp.float32, jnp.bfloat16

    def pack_kernel(cols, border, out, top, done):
        copies = [
            pltpu.make_async_copy(cols.at[pl.ds(cut, depth)], out.at[pl.ds(0, depth)], done.at[0]),
            pltpu.make_async_copy(border, out.at[pl.ds(depth, arrow)], done.at[1]),
            pltpu.make_async_copy(cols.at[pl.ds(0, cut)], top, done.at[2]),
        ]
        for copy in copies:
            copy.start()
        for copy in copies:
            copy.wait()

    mine, top = pl.pallas_call(
        pack_kernel,
        out_shape=(pltpu.VMEM((tall, width), bf16), pltpu.VMEM((cut, width), bf16)),
        in_specs=[pl.BlockSpec(memory_space=pltpu.HBM)] * 2,
        out_specs=(VMEM, VMEM),
        scratch_shapes=[pltpu.SemaphoreType.DMA((3,))],
        compiler_params=SMALL,
        name="pack",
    )(factor_cols, arrow_factor[0])
    first = lax.ppermute(mine, "space", around)
    other = lax.ppermute(mine, "space", swapped)
    other_top = lax.ppermute(top, "space", swapped)
    second = lax.ppermute(other, "space", around)
    mark = jax.ShapeDtypeStruct((8, width), f32)
    own, both_t, token = pl.pallas_call(
        own_kernel,
        out_shape=(
            pltpu.VMEM((both + arrow, width), f32),
            pltpu.VMEM((both, depth), bf16),
            mark,
        ),
        in_specs=[VMEM] * 4,
        out_specs=(VMEM,) * 3,
        compiler_params=SMALL,
        name="own",
    )(*map(near, (mine, other, top, other_top)))
    by_col = lax.dynamic_slice_in_dim(decay, column_at * width, width, axis=1)
    decay_rows = decay[0].reshape(pieces, rows)
    row_parts = jnp.concatenate(two_parts(decay_rows), axis=1)
    row_parts = jnp.pad(row_parts, ((0, 0), (0, width - 2 * rows)))
    col_parts = jnp.pad(jnp.concatenate(two_parts(by_col), axis=0), ((5, PAD - 7), (0, 0)))
    all_rows = jnp.pad(decay_rows, ((0, 0), (0, width - rows)))
    end = jnp.concatenate(
        [
            lax.dynamic_slice_in_dim(sigma_end, piece_at * rows, rows, axis=0),
            lax.dynamic_slice_in_dim(arrow_end.T, piece_at * share, share, axis=0),
            jnp.zeros((PAD - share, width), jnp.float32),
        ],
        axis=0,
    )
    small = (row_parts, col_parts, tip_inverse.T, all_rows, by_col, end)
    kept, given = [], []
    second, token, small = lax.optimization_barrier((second, token, small))
    row_parts, col_parts, tip_t, all_rows, by_col, end = small
    for s in range(hops - 1):
        skip = cut * (s + 2) - (order + arrow - first.shape[0]) if s > 0 else 0
        next_first = lax.ppermute(first[skip:], "space", around)
        next_second = lax.ppermute(second[skip:], "space", around) if s < hops - 2 else None
        keep, give, token = pl.pallas_call(
            far_kernel,
            out_shape=(*[jax.ShapeDtypeStruct((both + arrow, width), f32)] * 2, mark),
            in_specs=[VMEM] * 4,
            out_specs=(VMEM,) * 3,
            compiler_params=SMALL,
            name="far",
        )(*map(near, (first, second, both_t)), token)
        kept.append(keep)
        given.append(lax.ppermute(give, "space", swapped))
        first, second = next_first, next_second
        if s < hops - 2:
            first, token = lax.optimization_barrier((first, token))
    keep, give = held(farthest_kernel, "farthest", (((width + arrow, width), f32),) * 2, first, both_t, token)
    kept.append(keep)
    given.append(lax.ppermute(give, "space", swapped))

    message = ((pieces, rows + PAD, width), f32)
    sent, plain, own_arrow = pl.pallas_call(
        lambda *refs: message_kernel(rows, chips, hops, *refs),
        out_shape=(
            pltpu.VMEM(*message),
            jax.ShapeDtypeStruct((pieces, rows, width), f32),
            jax.ShapeDtypeStruct((arrow, width), f32),
        ),
        in_specs=[SMEM] + [VMEM] * (2 * hops + 4),
        out_specs=(VMEM, pl.BlockSpec(memory_space=pl.ANY), VMEM),
        scratch_shapes=[pltpu.VMEM((pieces, rows, width), f32), pltpu.SemaphoreType.DMA],
        compiler_params=SMALL,
        name="message",
    )(column_at.reshape(1), *map(near, (own, *kept, *given, tip_t, row_parts, col_parts)))

    def exchange(values):
        moved = lax.all_to_all(values.astype(jnp.float16), "tm", 0, 0, tiled=True)
        return moved.astype(jnp.float32)

    (ahead,) = held(
        lambda *refs: scan_kernel(rows, *refs),
        "suffix",
        (message,),
        *(exchange(sent), end),
        scratch=[pltpu.VMEM((pieces, width), f32)],
    )
    last = (plain, own_arrow, exchange(ahead), all_rows, by_col)
    sigma, arrows = pl.pallas_call(
        lambda *refs: last_kernel(rows, *refs),
        out_shape=(jax.ShapeDtypeStruct((order, width), f32), jax.ShapeDtypeStruct((arrow, width), f32)),
        in_specs=[VMEM] * len(last),
        compiler_params=SMALL,
        name="last",
    )(*map(near, last))
    return sigma[None], arrows.T[None]


def solution(mesh):
    placed = (
        P("tm", None, "space"),
        P("tm", None, "space"),
        P("tm", None),
        P(),
        P(None, "space"),
        P("space", None),
    )
    return jax.shard_map(
        body,
        mesh=mesh,
        in_specs=placed,
        out_specs=(P("tm", None, "space"), P("tm", "space", None)),
        check_vma=False,
    )
```

```python
import jax
import jax.numpy as jnp
from jax import lax
from jax.experimental import pallas as pl
from jax.experimental.pallas import tpu as pltpu
from jax.sharding import PartitionSpec as P

CORES = 2
PAD = 8
TOP = 14.0
DECAY = 1024.0


def split3(x):
    hi = x.astype(jnp.bfloat16)
    rest = x - hi.astype(jnp.float32)
    mid = rest.astype(jnp.bfloat16)
    low = (rest - mid.astype(jnp.float32)).astype(jnp.bfloat16)
    return hi, mid, low


def dot(a, b):
    return jnp.dot(a, b, preferred_element_type=jnp.float32)


def border_times(border, tile):
    hi, mid, low = split3(tile)
    return dot(border, hi) + dot(border, mid) + dot(border, low)


def exponent(x):
    largest = jnp.max(jnp.abs(x), axis=0, keepdims=True)
    return jnp.ceil(jnp.log2(jnp.maximum(largest, 2.0**-100)))


def squared(x, level):
    unit = x * jnp.exp2(TOP / 2 - level)
    return unit * jnp.abs(unit)


def rooted(x, level):
    root = jnp.sqrt(jnp.abs(x))
    return jnp.where(x < 0, -root, root) * jnp.exp2(level - TOP / 2)


def encode(panel, pair, extra):
    at = lax.broadcasted_iota(jnp.int32, pair.shape, 0)
    level, pair_level = exponent(panel), exponent(pair)
    tail = jnp.where(at < 2, squared(pair, pair_level), extra)
    tail = jnp.where(at == 2, level, jnp.where(at == 3, pair_level, tail))
    return squared(panel, level), tail


def decode(message, rows):
    tail = message[rows:, :]
    at = lax.broadcasted_iota(jnp.int32, tail.shape, 0)
    panel = rooted(message[:rows, :], tail[2:3, :])
    return panel, jnp.where(at < 2, rooted(tail, tail[3:4, :]), 0.0)


def own_kernel(mine, other, mine_top, other_top, tile, both_t, token):
    tall, width = mine.shape
    depth = both_t.shape[1]
    turned = jnp.concatenate([mine[:depth, :].T, other[:depth, :].T], axis=0)
    top = jnp.concatenate([mine_top[...].T, other_top[...].T], axis=0)
    both_t[...] = turned
    got = dot(turned, mine[:depth, :]) + dot(top, mine_top[...])
    border = jnp.concatenate([mine[depth:tall, :], other[depth:tall, :]], axis=1)
    tile[: CORES * width, :] = got
    tile[CORES * width :, :] = border_times(border, got)
    token[...] = jnp.zeros_like(token)


def far_tiles(panels, both_t, keep, give):
    tall, width = panels[0].shape
    count = width * len(panels)
    depth = tall - (keep.shape[0] - count)
    joined = jnp.concatenate([p[:depth, :] for p in panels], axis=1)
    border = jnp.concatenate([p[depth:tall, :] for p in panels], axis=1)
    tile = dot(both_t[:, both_t.shape[1] - depth :], joined).T
    total = border_times(border, tile)
    for at, part in ((0, keep), (width, give)):
        part[:count, :] = tile[:, at : at + width]
        part[count:, :] = total[:, at : at + width]


def far_kernel(first, second, both_t, passed, keep, give, token):
    far_tiles((first, second), both_t, keep, give)
    token[...] = passed[...]


def farthest_kernel(first, second, straight, both_t, token, keep, give, near_part, far_part):
    count = CORES * first.shape[1]
    far_tiles((first, second), both_t, near_part.at[0], near_part.at[1])
    far_tiles((straight,), both_t, far_part.at[0], far_part.at[1])
    single = straight.shape[1]
    for at, out in enumerate((keep, give)):
        out[:count, :] = near_part[at, :count, :]
        out[count : count + single, :] = far_part[at, :single, :]
        out[count + single :, :] = near_part[at, count:, :] + far_part[at, single:, :]


def message_kernel(rows, chips, hops, at, own, *refs):
    kept, given = refs[: hops - 1], refs[hops - 1 : 2 * hops - 2]
    tip_t, decay_rows, decay_cols, out, copied, own_arrow, plain, done = refs[2 * hops - 2 :]
    width = own.shape[1]
    per = width // rows
    chip, core = at[0] // CORES, at[0] % CORES
    way = 1 - 2 * core

    def put(block, hop, parity):
        spot = lax.rem(chip + hop + chips, chips) * CORES + parity
        plain[pl.ds(spot * per, per), :, :] = block.reshape(per, rows, width)

    put(own[:width, :], 0, core)
    put(own[width : CORES * width, :], 0, 1 - core)
    for s in range(hops - 1):
        hop = (s + 1) * way
        put(kept[s][:width, :], -hop, core)
        put(given[s][:width, :], hop, 1 - core)
        put(kept[s][width : 2 * width, :], -hop, 1 - core)
        put(given[s][width : 2 * width, :], hop, core)
    put(kept[-1][2 * width : 3 * width, :], hops, core)
    put(given[-1][2 * width : 3 * width, :], hops, 1 - core)
    copy = pltpu.make_async_copy(plain, copied, done)
    copy.start()
    border = own_arrow.shape[0]
    total = own[CORES * width :, :]
    for part in (*kept, *given):
        total = total + part[part.shape[0] - border :, :]
    arrow = -jnp.dot(tip_t[...], total, precision=lax.Precision.HIGHEST, preferred_element_type=jnp.float32)
    own_arrow[...] = arrow
    fill = jnp.zeros((PAD - 2, width), jnp.float32)
    cols = decay_cols[...]
    place = lax.broadcasted_iota(jnp.int32, cols.shape, 0)
    for r in range(out.shape[0]):
        extra = jnp.where(place == 4, decay_rows[r : r + 1, :], cols)
        pair = jnp.concatenate([arrow[2 * r : 2 * r + 2, :], fill], axis=0)
        out[r, :rows, :], out[r, rows:, :] = encode(plain[r], pair, extra)
    copy.wait()


def scan_kernel(rows, got, end, out, turned):
    pieces, _, width = got.shape
    for s in range(pieces):
        turned[s : s + 1, :] = got[s, rows + 4 : rows + 5, :]
    columns = turned[...].T
    columns = (columns[:rows, :] + columns[rows : 2 * rows, :] * (1 / 256)) * (1 / DECAY)
    carry, pair = end[:rows, :], end[rows:, :]
    for s in range(pieces - 1, -1, -1):
        out[s, :rows, :], out[s, rows:, :] = encode(carry, pair, jnp.zeros_like(pair))
        if s == 0:
            break
        panel, arrow = decode(got[s], rows)
        by_col = (got[s, rows + 5 : rows + 6, :] + got[s, rows + 6 : rows + 7, :] * (1 / 256)) * (1 / DECAY)
        by_row = jnp.broadcast_to(columns[:, s : s + 1], (rows, width))
        carry = panel + by_row * by_col * carry
        pair = arrow + by_col * pair


def last_kernel(rows, plain, own_arrow, got, decay_rows, by_col, sigma, arrows, whole, done):
    columns = decay_rows[...].T[:rows, :]
    pieces, parts = plain.shape[0], done.shape[0]
    span = pieces // parts * rows
    copies = []
    for r in range(pieces):
        later, later_arrow = decode(got[r], rows)
        by_row = jnp.broadcast_to(columns[:, r : r + 1], later.shape)
        whole[r * rows : (r + 1) * rows, :] = plain[r] + by_row * by_col[...] * later
        pair = slice(2 * r, 2 * r + 2)
        arrows[pair, :] = own_arrow[pair, :] + by_col[...] * later_arrow[:2, :]
        if (r + 1) % (pieces // parts) == 0:
            part = len(copies)
            spot = pl.ds(part * span, span)
            copies.append(pltpu.make_async_copy(whole.at[spot], sigma.at[spot], done.at[part]))
            copies[-1].start()
    for copy in copies:
        copy.wait()


def two_parts(decay):
    scaled = decay * DECAY
    high = lax.reduce_precision(scaled, 8, 7)
    return high, (scaled - high) * 256


VMEM = pl.BlockSpec(memory_space=pltpu.VMEM)
SMEM = pl.BlockSpec(memory_space=pltpu.SMEM)


SMALL = pltpu.CompilerParams(vmem_limit_bytes=12 << 20)


def near(x):
    return pltpu.with_memory_space_constraint(x, pltpu.VMEM)


def held(kernel, name, results, *operands, scratch=()):
    return pl.pallas_call(
        kernel,
        out_shape=tuple(pltpu.VMEM(shape, dtype) for shape, dtype in results),
        in_specs=[VMEM] * len(operands),
        out_specs=(VMEM,) * len(results),
        scratch_shapes=scratch,
        compiler_params=SMALL,
        name=name,
    )(*map(near, operands))


def body(inverse_factor, arrow_factor, decay, tip_inverse, sigma_end, arrow_end):
    factor_cols = inverse_factor[0]
    order, width = factor_cols.shape
    arrow = tip_inverse.shape[0]
    pieces, devices = lax.axis_size("tm"), lax.axis_size("space")
    chips, cut = devices // CORES, CORES * width
    rows, share = order // pieces, arrow // pieces
    column_at = lax.axis_index("space")
    piece_at = lax.axis_index("tm")
    swapped = [(p, p ^ 1) for p in range(devices)]
    depth, both = order - cut, CORES * width
    tall, hops = depth + arrow, chips // 2
    f32, bf16 = jnp.float32, jnp.bfloat16

    def pack_kernel(cols, border, out, top, done):
        copies = [
            pltpu.make_async_copy(cols.at[pl.ds(cut, depth)], out.at[pl.ds(0, depth)], done.at[0]),
            pltpu.make_async_copy(border, out.at[pl.ds(depth, arrow)], done.at[1]),
            pltpu.make_async_copy(cols.at[pl.ds(0, cut)], top, done.at[2]),
        ]
        for copy in copies:
            copy.start()
        for copy in copies:
            copy.wait()

    mine, top = pl.pallas_call(
        pack_kernel,
        out_shape=(pltpu.VMEM((tall, width), bf16), pltpu.VMEM((cut, width), bf16)),
        in_specs=[pl.BlockSpec(memory_space=pltpu.HBM)] * 2,
        out_specs=(VMEM, VMEM),
        scratch_shapes=[pltpu.SemaphoreType.DMA((3,))],
        compiler_params=SMALL,
        name="pack",
    )(*[pltpu.with_memory_space_constraint(x, pltpu.HBM) for x in (factor_cols, arrow_factor[0])])

    def hop(panel, count=1):
        pairs = []
        for p in range(devices):
            chip, core = p // CORES, p % CORES
            pairs.append((p, (chip + count * (1 - 2 * core)) % chips * CORES + core))
        return lax.ppermute(panel, "space", pairs)

    def shared(panel, count):
        return panel[cut * count - (order + arrow - panel.shape[0]) :]

    first = hop(mine)
    other = lax.ppermute(mine, "space", swapped)
    other_top = lax.ppermute(top, "space", swapped)
    second = hop(other)
    mark = jax.ShapeDtypeStruct((8, width), f32)
    own, both_t, token = pl.pallas_call(
        own_kernel,
        out_shape=(
            pltpu.VMEM((both + arrow, width), f32),
            pltpu.VMEM((both, depth), bf16),
            mark,
        ),
        in_specs=[VMEM] * 4,
        out_specs=(VMEM,) * 3,
        compiler_params=SMALL,
        name="own",
    )(*map(near, (mine, other, top, other_top)))
    by_col = lax.dynamic_slice_in_dim(decay, column_at * width, width, axis=1)
    decay_rows = decay[0].reshape(pieces, rows)
    row_parts = jnp.concatenate(two_parts(decay_rows), axis=1)
    row_parts = jnp.pad(row_parts, ((0, 0), (0, width - 2 * rows)))
    col_parts = jnp.pad(jnp.concatenate(two_parts(by_col), axis=0), ((5, PAD - 7), (0, 0)))
    all_rows = jnp.pad(decay_rows, ((0, 0), (0, width - rows)))
    end = jnp.concatenate(
        [
            lax.dynamic_slice_in_dim(sigma_end, piece_at * rows, rows, axis=0),
            lax.dynamic_slice_in_dim(arrow_end.T, piece_at * share, share, axis=0),
            jnp.zeros((PAD - share, width), jnp.float32),
        ],
        axis=0,
    )
    small = (row_parts, col_parts, tip_inverse.T, all_rows, by_col, end)

    def far(first, second, token):
        return pl.pallas_call(
            far_kernel,
            out_shape=(*[jax.ShapeDtypeStruct((both + arrow, width), f32)] * 2, mark),
            in_specs=[VMEM] * 4,
            out_specs=(VMEM,) * 3,
            compiler_params=SMALL,
            name="far",
        )(*map(near, (first, second, both_t)), token)

    def swap(tile):
        return lax.ppermute(tile, "space", swapped)

    first_2 = hop(shared(first, 2))
    second, token, small = lax.optimization_barrier((second, token, small))
    second_2 = hop(shared(second, 2))
    second_3 = hop(shared(second_2, 3))
    keep_1, give_1, token = far(first, second, token)
    first_2, token = lax.optimization_barrier((first_2, token))
    first_4 = hop(shared(first_2, 4), 2)
    first_3 = hop(shared(first_2, 3))
    given_1 = swap(give_1)
    keep_2, give_2, token = far(first_2, second_2, token)
    given_2 = swap(give_2)
    token, given_1, given_2 = lax.optimization_barrier((token, given_1, given_2))
    stacked = (3 * width + arrow, width)
    keep, give = held(
        farthest_kernel,
        "farthest",
        ((stacked, f32),) * 2,
        *(first_3, second_3, first_4, both_t, token),
        scratch=[pltpu.VMEM((2, both + arrow, width), f32), pltpu.VMEM((2, width + arrow, width), f32)],
    )
    kept, given = (keep_1, keep_2, keep), (given_1, given_2, swap(give))
    row_parts, col_parts, tip_t, all_rows, by_col, end = small

    message = ((pieces, rows + PAD, width), f32)
    sent, plain, own_arrow = pl.pallas_call(
        lambda *refs: message_kernel(rows, chips, hops, *refs),
        out_shape=(
            pltpu.VMEM(*message),
            jax.ShapeDtypeStruct((pieces, rows, width), f32),
            jax.ShapeDtypeStruct((arrow, width), f32),
        ),
        in_specs=[SMEM] + [VMEM] * (2 * hops + 2),
        out_specs=(VMEM, pl.BlockSpec(memory_space=pl.ANY), VMEM),
        scratch_shapes=[pltpu.VMEM((pieces, rows, width), f32), pltpu.SemaphoreType.DMA],
        compiler_params=SMALL,
        name="message",
    )(column_at.reshape(1), *map(near, (own, *kept, *given, tip_t, row_parts, col_parts)))

    def exchange(values):
        moved = lax.all_to_all(values.astype(jnp.float16), "tm", 0, 0, tiled=True)
        return moved.astype(jnp.float32)

    (ahead,) = held(
        lambda *refs: scan_kernel(rows, *refs),
        "suffix",
        (message,),
        *(exchange(sent), end),
        scratch=[pltpu.VMEM((pieces, width), f32)],
    )
    last = (plain, own_arrow, exchange(ahead), all_rows, by_col)
    sigma, arrows = pl.pallas_call(
        lambda *refs: last_kernel(rows, *refs),
        out_shape=(jax.ShapeDtypeStruct((order, width), f32), jax.ShapeDtypeStruct((arrow, width), f32)),
        in_specs=[VMEM] * len(last),
        out_specs=(pl.BlockSpec(memory_space=pltpu.HBM), VMEM),
        scratch_shapes=[pltpu.VMEM((order, width), f32), pltpu.SemaphoreType.DMA((4,))],
        compiler_params=SMALL,
        name="last",
    )(*map(near, last))
    return sigma[None], arrows.T[None]


def solution(mesh):
    placed = (
        P("tm", None, "space"),
        P("tm", None, "space"),
        P("tm", None),
        P(),
        P(None, "space"),
        P("space", None),
    )
    return jax.shard_map(
        body,
        mesh=mesh,
        in_specs=placed,
        out_specs=(P("tm", None, "space"), P("tm", "space", None)),
        check_vma=False,
    )
```

```python
import jax
import jax.numpy as jnp
from jax import lax
from jax.experimental import pallas as pl
from jax.experimental.pallas import tpu as pltpu
from jax.sharding import PartitionSpec as P

CORES = 2
PAD = 8
TOP = 14.0
DECAY = 1024.0


def split3(x):
    hi = x.astype(jnp.bfloat16)
    rest = x - hi.astype(jnp.float32)
    mid = rest.astype(jnp.bfloat16)
    low = (rest - mid.astype(jnp.float32)).astype(jnp.bfloat16)
    return hi, mid, low


def dot(a, b):
    return jnp.dot(a, b, preferred_element_type=jnp.float32)


def border_times(border, tile):
    hi, mid, low = split3(tile)
    return dot(border, hi) + dot(border, mid) + dot(border, low)


def exponent(x):
    largest = jnp.max(jnp.abs(x), axis=0, keepdims=True)
    return jnp.ceil(jnp.log2(jnp.maximum(largest, 2.0**-100)))


def squared(x, level):
    unit = x * jnp.exp2(TOP / 2 - level)
    return unit * jnp.abs(unit)


def rooted(x, level):
    root = jnp.sqrt(jnp.abs(x))
    return jnp.where(x < 0, -root, root) * jnp.exp2(level - TOP / 2)


def encode(panel, pair, extra):
    at = lax.broadcasted_iota(jnp.int32, pair.shape, 0)
    level, pair_level = exponent(panel), exponent(pair)
    tail = jnp.where(at < 2, squared(pair, pair_level), extra)
    tail = jnp.where(at == 2, level, jnp.where(at == 3, pair_level, tail))
    return squared(panel, level), tail


def decode(message, rows):
    tail = message[rows:, :]
    at = lax.broadcasted_iota(jnp.int32, tail.shape, 0)
    panel = rooted(message[:rows, :], tail[2:3, :])
    return panel, jnp.where(at < 2, rooted(tail, tail[3:4, :]), 0.0)


def own_kernel(mine, other, tile, both_t, token):
    width = mine.shape[1]
    depth = both_t.shape[1]
    turned = jnp.concatenate([mine[:depth, :].T, other[:depth, :].T], axis=0)
    both_t[...] = turned
    got = dot(turned, mine[:depth, :])
    border = jnp.concatenate([mine[depth:, :], other[depth:, :]], axis=1)
    tile[: CORES * width, :] = got
    tile[CORES * width :, :] = border_times(border, got)
    token[...] = jnp.zeros_like(token)


def far_tiles(panels, both_t, keep, give):
    tall, width = panels[0].shape
    count = width * len(panels)
    depth = tall - (keep.shape[0] - count)
    joined = jnp.concatenate([p[:depth, :] for p in panels], axis=1)
    border = jnp.concatenate([p[depth:tall, :] for p in panels], axis=1)
    tile = dot(both_t[:, both_t.shape[1] - depth :], joined).T
    total = border_times(border, tile)
    for at, part in ((0, keep), (width, give)):
        part[:count, :] = tile[:, at : at + width]
        part[count:, :] = total[:, at : at + width]


def far_kernel(first, second, both_t, passed, keep, give, token):
    far_tiles((first, second), both_t, keep, give)
    token[...] = passed[...]


def three_kernel(first, second, straight, both_t, passed, keep, give, token, pair, single):
    count, width = CORES * first.shape[1], straight.shape[1]
    far_tiles((first, second), both_t, pair.at[0], pair.at[1])
    far_tiles((straight,), both_t, single.at[0], single.at[1])
    for at, out in enumerate((keep, give)):
        out[:count, :] = pair[at, :count, :]
        out[count : count + width, :] = single[at, :width, :]
        out[count + width :, :] = pair[at, count:, :] + single[at, width:, :]
    token[...] = passed[...]


def two_parts(decay):
    scaled = decay * DECAY
    high = scaled.astype(jnp.bfloat16).astype(jnp.float32)
    return high, (scaled - high) * 256


def message_kernel(rows, chips, hops, at, own, *refs):
    kept, given = refs[: hops - 1], refs[hops - 1 : 2 * hops - 2]
    tip, decay, out, copied, own_arrow, plain, done = refs[2 * hops - 2 :]
    width = own.shape[1]
    per = width // rows
    chip, core = at[0] // CORES, at[0] % CORES
    way = 1 - 2 * core

    def put(block, hop, parity):
        spot = lax.rem(chip + hop + chips, chips) * CORES + parity
        plain[pl.ds(spot * per, per), :, :] = block.reshape(per, rows, width)

    put(own[:width, :], 0, core)
    put(own[width : CORES * width, :], 0, 1 - core)
    for s in range(hops - 1):
        hop = (s + 1) * way
        put(kept[s][:width, :], -hop, core)
        put(given[s][:width, :], hop, 1 - core)
        put(kept[s][width : 2 * width, :], -hop, 1 - core)
        put(given[s][width : 2 * width, :], hop, core)
        if kept[s].shape[0] > 3 * width:
            put(kept[s][2 * width : 3 * width, :], hops, core)
            put(given[s][2 * width : 3 * width, :], hops, 1 - core)
    copy = pltpu.make_async_copy(plain, copied, done)
    copy.start()
    border = own_arrow.shape[0]
    total = own[CORES * width :, :]
    for part in (*kept, *given):
        total = total + part[part.shape[0] - border :, :]
    arrow = -lax.dot_general(
        tip[...],
        total,
        (((0,), (0,)), ((), ())),
        precision=lax.Precision.HIGHEST,
        preferred_element_type=jnp.float32,
    )
    own_arrow[...] = arrow
    fill = jnp.zeros((PAD - 2, width), jnp.float32)
    place = lax.broadcasted_iota(jnp.int32, (PAD, width), 0)
    by_col = decay[:, pl.ds(pl.multiple_of(at[0] * width, width), width)]
    col_high, col_low = two_parts(by_col)
    cols = jnp.where(place == 5, col_high, jnp.where(place == 6, col_low, 0.0))
    for r in range(out.shape[0]):
        by_row = jnp.concatenate(two_parts(decay[:, r * rows : (r + 1) * rows]), axis=1)
        extra = jnp.where(place == 4, by_row, cols)
        pair = jnp.concatenate([arrow[2 * r : 2 * r + 2, :], fill], axis=0)
        out[r, :rows, :], out[r, rows:, :] = encode(plain[r], pair, extra)
    copy.wait()


def scan_kernel(rows, at, got, sigma_end, arrow_end, out, turned):
    pieces, _, width = got.shape
    share = arrow_end.shape[0] // pieces
    for s in range(pieces):
        turned[s : s + 1, :] = got[s, rows + 4 : rows + 5, :]
    columns = turned[...].T
    columns = (columns[:rows, :] + columns[rows : 2 * rows, :] * (1 / 256)) * (1 / DECAY)
    carry = sigma_end[pl.ds(pl.multiple_of(at[0] * rows, rows), rows), :]
    place = lax.broadcasted_iota(jnp.int32, (PAD, width), 0)
    pair = jnp.zeros((PAD, width), jnp.float32)
    for r in range(share):
        pair = jnp.where(place == r, arrow_end[pl.ds(at[0] * share + r, 1), :], pair)
    for s in range(pieces - 1, -1, -1):
        out[s, :rows, :], out[s, rows:, :] = encode(carry, pair, jnp.zeros_like(pair))
        if s == 0:
            break
        panel, arrow = decode(got[s], rows)
        by_col = (got[s, rows + 5 : rows + 6, :] + got[s, rows + 6 : rows + 7, :] * (1 / 256)) * (1 / DECAY)
        by_row = jnp.broadcast_to(columns[:, s : s + 1], (rows, width))
        carry = panel + by_row * by_col * carry
        pair = arrow + by_col * pair


def last_kernel(rows, at, plain, own_arrow, got, decay, sigma, arrows, turned):
    pieces, _, width = plain.shape
    for r in range(pieces):
        turned[r : r + 1, :rows] = decay[:, r * rows : (r + 1) * rows]
        turned[r : r + 1, rows:] = jnp.zeros((1, width - rows), jnp.float32)
    columns = turned[...].T[:rows, :]
    by_col = decay[:, pl.ds(pl.multiple_of(at[0] * width, width), width)]
    for r in range(pieces):
        later, later_arrow = decode(got[r], rows)
        by_row = jnp.broadcast_to(columns[:, r : r + 1], later.shape)
        sigma[r * rows : (r + 1) * rows, :] = plain[r] + by_row * by_col * later
        pair = slice(2 * r, 2 * r + 2)
        arrows[pair, :] = own_arrow[pair, :] + by_col * later_arrow[:2, :]


VMEM = pl.BlockSpec(memory_space=pltpu.VMEM)
SMEM = pl.BlockSpec(memory_space=pltpu.SMEM)


SMALL = pltpu.CompilerParams(vmem_limit_bytes=12 << 20)


def near(x):
    return pltpu.with_memory_space_constraint(x, pltpu.VMEM)


def body(inverse_factor, arrow_factor, decay, tip_inverse, sigma_end, arrow_end):
    factor_cols = inverse_factor[0]
    order, width = factor_cols.shape
    arrow = tip_inverse.shape[0]
    pieces, devices = lax.axis_size("tm"), lax.axis_size("space")
    chips, cut = devices // CORES, CORES * width
    rows, both, hops = order // pieces, CORES * width, chips // 2
    f32, bf16 = jnp.float32, jnp.bfloat16
    column_at = lax.axis_index("space").reshape(1)
    piece_at = lax.axis_index("tm").reshape(1)
    hbm = pl.BlockSpec(memory_space=pltpu.HBM)

    def pack_kernel(cols, border, out, done):
        copies = [
            pltpu.make_async_copy(cols, out.at[pl.ds(0, order)], done.at[0]),
            pltpu.make_async_copy(border, out.at[pl.ds(order, arrow)], done.at[1]),
        ]
        for copy in copies:
            copy.start()
        for copy in copies:
            copy.wait()

    mine = pl.pallas_call(
        pack_kernel,
        out_shape=pltpu.VMEM((order + arrow, width), bf16),
        in_specs=[hbm, hbm],
        out_specs=VMEM,
        scratch_shapes=[pltpu.SemaphoreType.DMA((2,))],
        compiler_params=SMALL,
        name="pack",
    )(*[pltpu.with_memory_space_constraint(x, pltpu.HBM) for x in (factor_cols, arrow_factor[0])])

    def hop(panel, count=1):
        pairs = []
        for p in range(devices):
            chip, core = p // CORES, p % CORES
            pairs.append((p, (chip + count * (1 - 2 * core)) % chips * CORES + core))
        return lax.ppermute(panel, "space", pairs)

    def swap(tile):
        return lax.ppermute(tile, "space", [(p, p ^ 1) for p in range(devices)])

    def shared(panel, count):
        return panel[cut * count - (order + arrow - panel.shape[0]) :]

    def product(kernel, name, count, panels, token, scratch=()):
        tall = count * width + arrow
        return pl.pallas_call(
            kernel,
            out_shape=(*[jax.ShapeDtypeStruct((tall, width), f32)] * 2, mark),
            in_specs=[VMEM] * (len(panels) + 2),
            out_specs=(VMEM,) * 3,
            scratch_shapes=scratch,
            compiler_params=SMALL,
            name=name,
        )(*map(near, panels), near(both_t), token)

    first = hop(shared(mine, 1))
    other = swap(mine)
    second = hop(shared(other, 1))
    mark = jax.ShapeDtypeStruct((8, width), f32)
    own, both_t, token = pl.pallas_call(
        own_kernel,
        out_shape=(pltpu.VMEM((both + arrow, width), f32), pltpu.VMEM((both, order), bf16), mark),
        in_specs=[VMEM] * 2,
        out_specs=(VMEM,) * 3,
        compiler_params=SMALL,
        name="own",
    )(near(mine), near(other))

    first_2 = hop(shared(first, 2))
    second, token = lax.optimization_barrier((second, token))
    second_2 = hop(shared(second, 2))
    keep_1, give_1, token = product(far_kernel, "far", 2, (first, second), token)
    first_2, token = lax.optimization_barrier((first_2, token))
    first_4 = hop(shared(first_2, 4), 2)
    first_3 = hop(shared(first_2, 3))
    second_3 = hop(shared(second_2, 3))
    given_1 = swap(give_1)
    token, given_1 = lax.optimization_barrier((token, given_1))
    keep_2, give_2, token = product(
        three_kernel,
        "three",
        3,
        (first_2, second_2, first_4),
        token,
        [pltpu.VMEM((2, both + arrow, width), f32), pltpu.VMEM((2, width + arrow, width), f32)],
    )
    given_2 = swap(give_2)
    keep_3, give_3, token = product(far_kernel, "far", 2, (first_3, second_3), token)
    kept, given = (keep_1, keep_2, keep_3), (given_1, given_2, swap(give_3))

    message = (pieces, rows + PAD, width)
    sent, plain, own_arrow = pl.pallas_call(
        lambda *refs: message_kernel(rows, chips, hops, *refs),
        out_shape=(
            pltpu.VMEM(message, f32),
            jax.ShapeDtypeStruct((pieces, rows, width), f32),
            jax.ShapeDtypeStruct((arrow, width), f32),
        ),
        in_specs=[SMEM] + [VMEM] * (2 * hops + 1),
        out_specs=(VMEM, pl.BlockSpec(memory_space=pl.ANY), VMEM),
        scratch_shapes=[pltpu.VMEM((pieces, rows, width), f32), pltpu.SemaphoreType.DMA],
        compiler_params=SMALL,
        name="message",
    )(column_at, *map(near, (own, *kept, *given, tip_inverse, decay)))

    def exchange(values):
        moved = lax.all_to_all(values.astype(jnp.float16), "tm", 0, 0, tiled=True)
        return moved.astype(jnp.float32)

    ahead = pl.pallas_call(
        lambda *refs: scan_kernel(rows, *refs),
        out_shape=pltpu.VMEM(message, f32),
        in_specs=[SMEM] + [VMEM] * 3,
        out_specs=VMEM,
        scratch_shapes=[pltpu.VMEM((pieces, width), f32)],
        compiler_params=SMALL,
        name="suffix",
    )(piece_at, *map(near, (exchange(sent), sigma_end, arrow_end.T)))
    sigma, arrows = pl.pallas_call(
        lambda *refs: last_kernel(rows, *refs),
        out_shape=(jax.ShapeDtypeStruct((order, width), f32), jax.ShapeDtypeStruct((arrow, width), f32)),
        in_specs=[SMEM] + [VMEM] * 4,
        scratch_shapes=[pltpu.VMEM((pieces, width), f32)],
        compiler_params=SMALL,
        name="last",
    )(column_at, *map(near, (plain, own_arrow, exchange(ahead), decay)))
    return sigma[None], arrows.T[None]


def solution(mesh):
    placed = (
        P("tm", None, "space"),
        P("tm", None, "space"),
        P("tm", None),
        P(),
        P(None, "space"),
        P("space", None),
    )
    return jax.shard_map(
        body,
        mesh=mesh,
        in_specs=placed,
        out_specs=(P("tm", None, "space"), P("tm", "space", None)),
        check_vma=False,
    )
```

```python
import jax
import jax.numpy as jnp
from jax import lax
from jax.experimental import pallas as pl
from jax.experimental.pallas import tpu as pltpu
from jax.sharding import PartitionSpec as P

CORES = 2
PAD = 8
TOP = 14.0
DECAY = 1024.0


def split3(x):
    hi = x.astype(jnp.bfloat16)
    rest = x - hi.astype(jnp.float32)
    mid = rest.astype(jnp.bfloat16)
    low = (rest - mid.astype(jnp.float32)).astype(jnp.bfloat16)
    return hi, mid, low


def dot(a, b):
    return jnp.dot(a, b, preferred_element_type=jnp.float32)


def border_times(border, tile):
    hi, mid, low = split3(tile)
    return dot(border, hi) + dot(border, mid) + dot(border, low)


def exponent(x):
    largest = jnp.max(jnp.abs(x), axis=0, keepdims=True)
    return jnp.ceil(jnp.log2(jnp.maximum(largest, 2.0**-100)))


def squared(x, level):
    unit = x * jnp.exp2(TOP / 2 - level)
    return unit * jnp.abs(unit)


def rooted(x, level):
    return x * (lax.rsqrt(jnp.maximum(jnp.abs(x), 2.0**-60)) * jnp.exp2(level - TOP / 2))


def encode(panel, pair, extra):
    at = lax.broadcasted_iota(jnp.int32, pair.shape, 0)
    level, pair_level = exponent(panel), exponent(pair)
    tail = jnp.where(at < 2, squared(pair, pair_level), extra)
    tail = jnp.where(at == 2, level, jnp.where(at == 3, pair_level, tail))
    return squared(panel, level), tail


def decode(message, rows):
    tail = message[rows:, :]
    at = lax.broadcasted_iota(jnp.int32, tail.shape, 0)
    panel = rooted(message[:rows, :], tail[2:3, :])
    return panel, jnp.where(at < 2, rooted(tail, tail[3:4, :]), 0.0)


def own_kernel(at, mine, other, sigma_end, arrow_end, tile, both_t, end, token, done):
    width = mine.shape[1]
    depth = both_t.shape[1]
    rows = end.shape[0] - PAD
    share = arrow_end.shape[0] * rows // depth
    spot = pl.ds(pl.multiple_of(at[0] * rows, rows), rows)
    copy = pltpu.make_async_copy(sigma_end.at[spot], end.at[pl.ds(0, rows)], done)
    copy.start()
    place = lax.broadcasted_iota(jnp.int32, (PAD, width), 0)
    pair = jnp.zeros((PAD, width), jnp.float32)
    for r in range(share):
        pair = jnp.where(place == r, arrow_end[pl.ds(at[0] * share + r, 1), :], pair)
    end[rows:, :] = pair
    turned = jnp.concatenate([mine[:depth, :].T, other[:depth, :].T], axis=0)
    both_t[...] = turned
    got = dot(turned, mine[:depth, :])
    border = jnp.concatenate([mine[depth:, :], other[depth:, :]], axis=1)
    tile[: CORES * width, :] = got
    tile[CORES * width :, :] = border_times(border, got)
    token[...] = jnp.zeros_like(token)
    copy.wait()


def far_tiles(panels, both_t, keep, give):
    tall, width = panels[0].shape
    count = width * len(panels)
    depth = tall - (keep.shape[0] - count)
    joined = jnp.concatenate([p[:depth, :] for p in panels], axis=1)
    border = jnp.concatenate([p[depth:tall, :] for p in panels], axis=1)
    tile = dot(both_t[:, both_t.shape[1] - depth :], joined).T
    total = border_times(border, tile)
    for at, part in ((0, keep), (width, give)):
        part[:count, :] = tile[:, at : at + width]
        part[count:, :] = total[:, at : at + width]


def far_kernel(first, second, both_t, passed, keep, give, token):
    far_tiles((first, second), both_t, keep, give)
    token[...] = passed[...]


def three_kernel(first, second, straight, both_t, passed, keep, give, token, pair, single):
    count, width = CORES * first.shape[1], straight.shape[1]
    far_tiles((first, second), both_t, pair.at[0], pair.at[1])
    far_tiles((straight,), both_t, single.at[0], single.at[1])
    for at, out in enumerate((keep, give)):
        out[:count, :] = pair[at, :count, :]
        out[count : count + width, :] = single[at, :width, :]
        out[count + width :, :] = pair[at, count:, :] + single[at, width:, :]
    token[...] = passed[...]


def two_parts(decay):
    scaled = decay * DECAY
    high = scaled.astype(jnp.bfloat16).astype(jnp.float32)
    return high, (scaled - high) * 256


def message_kernel(rows, chips, hops, at, own, *refs):
    kept, given = refs[: hops - 1], refs[hops - 1 : 2 * hops - 2]
    tip, decay, out, copied, own_arrow, plain, done = refs[2 * hops - 2 :]
    width = own.shape[1]
    per = width // rows
    chip, core = at[0] // CORES, at[0] % CORES
    way = 1 - 2 * core

    def put(block, hop, parity):
        spot = lax.rem(chip + hop + chips, chips) * CORES + parity
        plain[pl.ds(spot * per, per), :, :] = block.reshape(per, rows, width)

    put(own[:width, :], 0, core)
    put(own[width : CORES * width, :], 0, 1 - core)
    for s in range(hops - 1):
        hop = (s + 1) * way
        put(kept[s][:width, :], -hop, core)
        put(given[s][:width, :], hop, 1 - core)
        put(kept[s][width : 2 * width, :], -hop, 1 - core)
        put(given[s][width : 2 * width, :], hop, core)
        if kept[s].shape[0] > 3 * width:
            put(kept[s][2 * width : 3 * width, :], hops, core)
            put(given[s][2 * width : 3 * width, :], hops, 1 - core)
    copy = pltpu.make_async_copy(plain, copied, done)
    copy.start()
    border = own_arrow.shape[0]
    total = own[CORES * width :, :]
    for part in (*kept, *given):
        total = total + part[part.shape[0] - border :, :]
    arrow = -lax.dot_general(
        tip[...],
        total,
        (((0,), (0,)), ((), ())),
        precision=lax.Precision.HIGHEST,
        preferred_element_type=jnp.float32,
    )
    own_arrow[...] = arrow
    fill = jnp.zeros((PAD - 2, width), jnp.float32)
    place = lax.broadcasted_iota(jnp.int32, (PAD, width), 0)
    by_col = decay[:, pl.ds(pl.multiple_of(at[0] * width, width), width)]
    col_high, col_low = two_parts(by_col)
    cols = jnp.where(place == 5, col_high, jnp.where(place == 6, col_low, 0.0))
    for r in range(out.shape[0]):
        by_row = jnp.concatenate(two_parts(decay[:, r * rows : (r + 1) * rows]), axis=1)
        extra = jnp.where(place == 4, by_row, cols)
        pair = jnp.concatenate([arrow[2 * r : 2 * r + 2, :], fill], axis=0)
        out[r, :rows, :], out[r, rows:, :] = encode(plain[r], pair, extra)
    copy.wait()


def scan_kernel(rows, got, end, out, turned):
    pieces, _, width = got.shape
    for s in range(pieces):
        turned[s : s + 1, :] = got[s, rows + 4 : rows + 5, :]
    columns = turned[...].T
    columns = (columns[:rows, :] + columns[rows : 2 * rows, :] * (1 / 256)) * (1 / DECAY)
    carry, pair = end[:rows, :], end[rows:, :]
    for s in range(pieces - 1, -1, -1):
        out[s, :rows, :], out[s, rows:, :] = encode(carry, pair, jnp.zeros_like(pair))
        if s == 0:
            break
        panel, arrow = decode(got[s], rows)
        by_col = (got[s, rows + 5 : rows + 6, :] + got[s, rows + 6 : rows + 7, :] * (1 / 256)) * (1 / DECAY)
        by_row = jnp.broadcast_to(columns[:, s : s + 1], (rows, width))
        carry = panel + by_row * by_col * carry
        pair = arrow + by_col * pair


def last_kernel(rows, at, plain, own_arrow, got, decay, sigma, arrows, turned):
    pieces, _, width = plain.shape
    for r in range(pieces):
        turned[r : r + 1, :rows] = decay[:, r * rows : (r + 1) * rows]
        turned[r : r + 1, rows:] = jnp.zeros((1, width - rows), jnp.float32)
    columns = turned[...].T[:rows, :]
    by_col = decay[:, pl.ds(pl.multiple_of(at[0] * width, width), width)]
    for r in range(pieces):
        later, later_arrow = decode(got[r], rows)
        by_row = jnp.broadcast_to(columns[:, r : r + 1], later.shape)
        sigma[r * rows : (r + 1) * rows, :] = plain[r] + by_row * by_col * later
        pair = slice(2 * r, 2 * r + 2)
        arrows[pair, :] = own_arrow[pair, :] + by_col * later_arrow[:2, :]


VMEM = pl.BlockSpec(memory_space=pltpu.VMEM)
SMEM = pl.BlockSpec(memory_space=pltpu.SMEM)


SMALL = pltpu.CompilerParams(vmem_limit_bytes=12 << 20)


def near(x):
    return pltpu.with_memory_space_constraint(x, pltpu.VMEM)


def far_off(x):
    return pltpu.with_memory_space_constraint(x, pltpu.HBM)


def body(inverse_factor, arrow_factor, decay, tip_inverse, sigma_end, arrow_end):
    factor_cols = inverse_factor[0]
    order, width = factor_cols.shape
    arrow = tip_inverse.shape[0]
    pieces, devices = lax.axis_size("tm"), lax.axis_size("space")
    chips, cut = devices // CORES, CORES * width
    rows, both, hops = order // pieces, CORES * width, chips // 2
    f32, bf16 = jnp.float32, jnp.bfloat16
    column_at = lax.axis_index("space").reshape(1)
    piece_at = lax.axis_index("tm").reshape(1)
    hbm = pl.BlockSpec(memory_space=pltpu.HBM)

    def pack_kernel(cols, border, out, done):
        copies = [
            pltpu.make_async_copy(cols, out.at[pl.ds(0, order)], done.at[0]),
            pltpu.make_async_copy(border, out.at[pl.ds(order, arrow)], done.at[1]),
        ]
        for copy in copies:
            copy.start()
        for copy in copies:
            copy.wait()

    mine = pl.pallas_call(
        pack_kernel,
        out_shape=pltpu.VMEM((order + arrow, width), bf16),
        in_specs=[hbm, hbm],
        out_specs=VMEM,
        scratch_shapes=[pltpu.SemaphoreType.DMA((2,))],
        compiler_params=SMALL,
        name="pack",
    )(far_off(factor_cols), far_off(arrow_factor[0]))

    def hop(panel, count=1, cross=0):
        pairs = []
        for p in range(devices):
            chip, core = p // CORES, p % CORES ^ cross
            pairs.append((p, (chip + count * (1 - 2 * core)) % chips * CORES + core))
        return lax.ppermute(panel, "space", pairs)

    def swap(tile):
        return lax.ppermute(tile, "space", [(p, p ^ 1) for p in range(devices)])

    def shared(panel, count):
        return panel[cut * count - (order + arrow - panel.shape[0]) :]

    def product(kernel, name, count, panels, token, scratch=()):
        tall = count * width + arrow
        return pl.pallas_call(
            kernel,
            out_shape=(*[jax.ShapeDtypeStruct((tall, width), f32)] * 2, mark),
            in_specs=[VMEM] * (len(panels) + 2),
            out_specs=(VMEM,) * 3,
            scratch_shapes=scratch,
            compiler_params=SMALL,
            name=name,
        )(*map(near, panels), near(both_t), token)

    start = shared(mine, 1)
    first, second = hop(start), hop(start, cross=1)
    other = swap(mine)
    mark = jax.ShapeDtypeStruct((8, width), f32)
    own, both_t, end, token = pl.pallas_call(
        own_kernel,
        out_shape=(
            pltpu.VMEM((both + arrow, width), f32),
            pltpu.VMEM((both, order), bf16),
            pltpu.VMEM((rows + PAD, width), f32),
            mark,
        ),
        in_specs=[SMEM, VMEM, VMEM, hbm, VMEM],
        out_specs=(VMEM,) * 4,
        scratch_shapes=[pltpu.SemaphoreType.DMA],
        compiler_params=SMALL,
        name="own",
    )(piece_at, near(mine), near(other), far_off(sigma_end), near(arrow_end.T))

    first_2 = hop(shared(first, 2))
    second, token = lax.optimization_barrier((second, token))
    second_2 = hop(shared(second, 2))
    keep_1, give_1, token = product(far_kernel, "far", 2, (first, second), token)
    first_2, token = lax.optimization_barrier((first_2, token))
    first_4 = hop(shared(first_2, 4), 2)
    first_3 = hop(shared(first_2, 3))
    second_3 = hop(shared(second_2, 3))
    given_1 = swap(give_1)
    token, given_1 = lax.optimization_barrier((token, given_1))
    keep_2, give_2, token = product(
        three_kernel,
        "three",
        3,
        (first_2, second_2, first_4),
        token,
        [pltpu.VMEM((2, both + arrow, width), f32), pltpu.VMEM((2, width + arrow, width), f32)],
    )
    given_2 = swap(give_2)
    keep_3, give_3, token = product(far_kernel, "far", 2, (first_3, second_3), token)
    kept, given = (keep_1, keep_2, keep_3), (given_1, given_2, swap(give_3))

    message = (pieces, rows + PAD, width)
    sent, plain, own_arrow = pl.pallas_call(
        lambda *refs: message_kernel(rows, chips, hops, *refs),
        out_shape=(
            pltpu.VMEM(message, f32),
            jax.ShapeDtypeStruct((pieces, rows, width), f32),
            jax.ShapeDtypeStruct((arrow, width), f32),
        ),
        in_specs=[SMEM] + [VMEM] * (2 * hops + 1),
        out_specs=(VMEM, pl.BlockSpec(memory_space=pl.ANY), VMEM),
        scratch_shapes=[pltpu.VMEM((pieces, rows, width), f32), pltpu.SemaphoreType.DMA],
        compiler_params=SMALL,
        name="message",
    )(column_at, *map(near, (own, *kept, *given, tip_inverse, decay)))

    def exchange(values):
        moved = lax.all_to_all(values.astype(jnp.float16), "tm", 0, 0, tiled=True)
        return moved.astype(jnp.float32)

    ahead = pl.pallas_call(
        lambda *refs: scan_kernel(rows, *refs),
        out_shape=pltpu.VMEM(message, f32),
        in_specs=[VMEM] * 2,
        out_specs=VMEM,
        scratch_shapes=[pltpu.VMEM((pieces, width), f32)],
        compiler_params=SMALL,
        name="suffix",
    )(near(exchange(sent)), near(end))
    sigma, arrows = pl.pallas_call(
        lambda *refs: last_kernel(rows, *refs),
        out_shape=(jax.ShapeDtypeStruct((order, width), f32), jax.ShapeDtypeStruct((arrow, width), f32)),
        in_specs=[SMEM] + [VMEM] * 4,
        scratch_shapes=[pltpu.VMEM((pieces, width), f32)],
        compiler_params=SMALL,
        name="last",
    )(column_at, *map(near, (plain, own_arrow, exchange(ahead), decay)))
    return sigma[None], arrows.T[None]


def solution(mesh):
    placed = (
        P("tm", None, "space"),
        P("tm", None, "space"),
        P("tm", None),
        P(),
        P(None, "space"),
        P("space", None),
    )
    return jax.shard_map(
        body,
        mesh=mesh,
        in_specs=placed,
        out_specs=(P("tm", None, "space"), P("tm", "space", None)),
        check_vma=False,
    )
```

```python
import jax
import jax.numpy as jnp
from jax import lax
from jax.experimental import pallas as pl
from jax.experimental.pallas import tpu as pltpu
from jax.sharding import PartitionSpec as P

CORES = 2
PAD = 8
TOP = 14.0
DECAY = 1024.0


def split3(x):
    hi = x.astype(jnp.bfloat16)
    rest = x - hi.astype(jnp.float32)
    mid = rest.astype(jnp.bfloat16)
    low = (rest - mid.astype(jnp.float32)).astype(jnp.bfloat16)
    return hi, mid, low


def dot(a, b):
    return jnp.dot(a, b, preferred_element_type=jnp.float32)


def border_times(border, tile):
    hi, mid, low = split3(tile)
    return dot(border, hi) + dot(border, mid) + dot(border, low)


def exponent(x):
    largest = jnp.max(jnp.abs(x), axis=0, keepdims=True)
    return jnp.ceil(jnp.log2(jnp.maximum(largest, 2.0**-100)))


def squared(x, level):
    unit = x * jnp.exp2(TOP / 2 - level)
    return unit * jnp.abs(unit)


def rooted(x, level):
    return x * (lax.rsqrt(jnp.maximum(jnp.abs(x), 2.0**-60)) * jnp.exp2(level - TOP / 2))


def encode(panel, pair, extra):
    at = lax.broadcasted_iota(jnp.int32, pair.shape, 0)
    level, pair_level = exponent(panel), exponent(pair)
    tail = jnp.where(at < 2, squared(pair, pair_level), extra)
    tail = jnp.where(at == 2, level, jnp.where(at == 3, pair_level, tail))
    return squared(panel, level), tail


def decode(message, rows):
    tail = message[rows:, :]
    at = lax.broadcasted_iota(jnp.int32, tail.shape, 0)
    panel = rooted(message[:rows, :], tail[2:3, :])
    return panel, jnp.where(at < 2, rooted(tail, tail[3:4, :]), 0.0)


def own_kernel(at, mine, other, sigma_end, arrow_end, tile, both_t, end, token, done):
    width = mine.shape[1]
    depth = both_t.shape[1]
    rows = end.shape[0] - PAD
    share = arrow_end.shape[0] * rows // depth
    spot = pl.ds(pl.multiple_of(at[0] * rows, rows), rows)
    copy = pltpu.make_async_copy(sigma_end.at[spot], end.at[pl.ds(0, rows)], done)
    copy.start()
    place = lax.broadcasted_iota(jnp.int32, (PAD, width), 0)
    pair = jnp.zeros((PAD, width), jnp.float32)
    for r in range(share):
        pair = jnp.where(place == r, arrow_end[pl.ds(at[0] * share + r, 1), :], pair)
    end[rows:, :] = pair
    turned = jnp.concatenate([mine[:depth, :].T, other[:depth, :].T], axis=0)
    both_t[...] = turned
    got = dot(turned, mine[:depth, :])
    border = jnp.concatenate([mine[depth:, :], other[depth:, :]], axis=1)
    tile[: CORES * width, :] = got
    tile[CORES * width :, :] = border_times(border, got)
    token[...] = jnp.zeros_like(token)
    copy.wait()


def far_tiles(panels, both_t, keep, give):
    tall, width = panels[0].shape
    count = width * len(panels)
    depth = tall - (keep.shape[0] - count)
    joined = jnp.concatenate([p[:depth, :] for p in panels], axis=1)
    border = jnp.concatenate([p[depth:tall, :] for p in panels], axis=1)
    tile = dot(both_t[:, both_t.shape[1] - depth :], joined).T
    total = border_times(border, tile)
    for at, part in ((0, keep), (width, give)):
        part[:count, :] = tile[:, at : at + width]
        part[count:, :] = total[:, at : at + width]


def far_kernel(first, second, both_t, passed, keep, give, token):
    far_tiles((first, second), both_t, keep, give)
    token[...] = passed[...]


def three_kernel(first, second, straight, both_t, passed, keep, give, token, pair, single):
    count, width = CORES * first.shape[1], straight.shape[1]
    far_tiles((first, second), both_t, pair.at[0], pair.at[1])
    far_tiles((straight,), both_t, single.at[0], single.at[1])
    for at, out in enumerate((keep, give)):
        out[:count, :] = pair[at, :count, :]
        out[count : count + width, :] = single[at, :width, :]
        out[count + width :, :] = pair[at, count:, :] + single[at, width:, :]
    token[...] = passed[...]


def two_parts(decay):
    scaled = decay * DECAY
    high = scaled.astype(jnp.bfloat16).astype(jnp.float32)
    return high, (scaled - high) * 256


def message_kernel(rows, chips, hops, at, own, *refs):
    kept, given = refs[: hops - 1], refs[hops - 1 : 2 * hops - 2]
    tip, decay, out, copied, own_arrow, plain, done = refs[2 * hops - 2 :]
    width = own.shape[1]
    per = width // rows
    chip, core = at[0] // CORES, at[0] % CORES
    way = 1 - 2 * core

    def put(block, hop, parity):
        spot = lax.rem(chip + hop + chips, chips) * CORES + parity
        plain[pl.ds(spot * per, per), :, :] = block.reshape(per, rows, width)

    put(own[:width, :], 0, core)
    put(own[width : CORES * width, :], 0, 1 - core)
    for s in range(hops - 1):
        hop = (s + 1) * way
        put(kept[s][:width, :], -hop, core)
        put(given[s][:width, :], hop, 1 - core)
        put(kept[s][width : 2 * width, :], -hop, 1 - core)
        put(given[s][width : 2 * width, :], hop, core)
        if kept[s].shape[0] > 3 * width:
            put(kept[s][2 * width : 3 * width, :], hops, core)
            put(given[s][2 * width : 3 * width, :], hops, 1 - core)
    copy = pltpu.make_async_copy(plain, copied, done)
    copy.start()
    border = own_arrow.shape[0]
    total = own[CORES * width :, :]
    for part in (*kept, *given):
        total = total + part[part.shape[0] - border :, :]
    arrow = -lax.dot_general(
        tip[...],
        total,
        (((0,), (0,)), ((), ())),
        precision=lax.Precision.HIGHEST,
        preferred_element_type=jnp.float32,
    )
    own_arrow[...] = arrow
    fill = jnp.zeros((PAD - 2, width), jnp.float32)
    place = lax.broadcasted_iota(jnp.int32, (PAD, width), 0)
    by_col = decay[:, pl.ds(pl.multiple_of(at[0] * width, width), width)]
    col_high, col_low = two_parts(by_col)
    cols = jnp.where(place == 5, col_high, jnp.where(place == 6, col_low, 0.0))
    for r in range(out.shape[0]):
        by_row = jnp.concatenate(two_parts(decay[:, r * rows : (r + 1) * rows]), axis=1)
        extra = jnp.where(place == 4, by_row, cols)
        pair = jnp.concatenate([arrow[2 * r : 2 * r + 2, :], fill], axis=0)
        out[r, :rows, :], out[r, rows:, :] = encode(plain[r], pair, extra)
    copy.wait()


def scan_kernel(rows, got, end, out, turned):
    pieces, _, width = got.shape
    for s in range(pieces):
        turned[s : s + 1, :] = got[s, rows + 4 : rows + 5, :]
    columns = turned[...].T
    columns = (columns[:rows, :] + columns[rows : 2 * rows, :] * (1 / 256)) * (1 / DECAY)
    carry, pair = end[:rows, :], end[rows:, :]
    for s in range(pieces - 1, -1, -1):
        out[s, :rows, :], out[s, rows:, :] = encode(carry, pair, jnp.zeros_like(pair))
        if s == 0:
            break
        panel, arrow = decode(got[s], rows)
        by_col = (got[s, rows + 5 : rows + 6, :] + got[s, rows + 6 : rows + 7, :] * (1 / 256)) * (1 / DECAY)
        by_row = jnp.broadcast_to(columns[:, s : s + 1], (rows, width))
        carry = panel + by_row * by_col * carry
        pair = arrow + by_col * pair


def last_kernel(rows, at, plain, own_arrow, got, decay, sigma, arrows, turned):
    pieces, _, width = plain.shape
    for r in range(pieces):
        turned[r : r + 1, :rows] = decay[:, r * rows : (r + 1) * rows]
        turned[r : r + 1, rows:] = jnp.zeros((1, width - rows), jnp.float32)
    columns = turned[...].T[:rows, :]
    by_col = decay[:, pl.ds(pl.multiple_of(at[0] * width, width), width)]
    for r in range(pieces):
        later, later_arrow = decode(got[r], rows)
        by_row = jnp.broadcast_to(columns[:, r : r + 1], later.shape)
        sigma[r * rows : (r + 1) * rows, :] = plain[r] + by_row * by_col * later
        pair = slice(2 * r, 2 * r + 2)
        arrows[pair, :] = own_arrow[pair, :] + by_col * later_arrow[:2, :]


VMEM = pl.BlockSpec(memory_space=pltpu.VMEM)
SMEM = pl.BlockSpec(memory_space=pltpu.SMEM)


SMALL = pltpu.CompilerParams(vmem_limit_bytes=12 << 20)


def near(x):
    return pltpu.with_memory_space_constraint(x, pltpu.VMEM)


def far_off(x):
    return pltpu.with_memory_space_constraint(x, pltpu.HBM)


def body(inverse_factor, arrow_factor, decay, tip_inverse, sigma_end, arrow_end):
    factor_cols = inverse_factor[0]
    order, width = factor_cols.shape
    arrow = tip_inverse.shape[0]
    pieces, devices = lax.axis_size("tm"), lax.axis_size("space")
    chips, cut = devices // CORES, CORES * width
    rows, both, hops = order // pieces, CORES * width, chips // 2
    f32, bf16 = jnp.float32, jnp.bfloat16
    column_at = lax.axis_index("space").reshape(1)
    piece_at = lax.axis_index("tm").reshape(1)
    hbm = pl.BlockSpec(memory_space=pltpu.HBM)

    def pack_kernel(cols, border, out, done):
        copies = [
            pltpu.make_async_copy(cols, out.at[pl.ds(0, order)], done.at[0]),
            pltpu.make_async_copy(border, out.at[pl.ds(order, arrow)], done.at[1]),
        ]
        for copy in copies:
            copy.start()
        for copy in copies:
            copy.wait()

    mine = pl.pallas_call(
        pack_kernel,
        out_shape=pltpu.VMEM((order + arrow, width), bf16),
        in_specs=[hbm, hbm],
        out_specs=VMEM,
        scratch_shapes=[pltpu.SemaphoreType.DMA((2,))],
        compiler_params=SMALL,
        name="pack",
    )(far_off(factor_cols), far_off(arrow_factor[0]))

    def hop(panel, count=1):
        pairs = []
        for p in range(devices):
            chip, core = p // CORES, p % CORES
            pairs.append((p, (chip + count * (1 - 2 * core)) % chips * CORES + core))
        return lax.ppermute(panel, "space", pairs)

    def swap(tile):
        return lax.ppermute(tile, "space", [(p, p ^ 1) for p in range(devices)])

    def shared(panel, count):
        return panel[cut * count - (order + arrow - panel.shape[0]) :]

    def product(kernel, name, count, panels, token, scratch=()):
        tall = count * width + arrow
        return pl.pallas_call(
            kernel,
            out_shape=(*[jax.ShapeDtypeStruct((tall, width), f32)] * 2, mark),
            in_specs=[VMEM] * (len(panels) + 2),
            out_specs=(VMEM,) * 3,
            scratch_shapes=scratch,
            compiler_params=SMALL,
            name=name,
        )(*map(near, panels), near(both_t), token)

    first = hop(shared(mine, 1))
    other = swap(mine)
    second = hop(shared(other, 1))
    mark = jax.ShapeDtypeStruct((8, width), f32)
    own, both_t, end, token = pl.pallas_call(
        own_kernel,
        out_shape=(
            pltpu.VMEM((both + arrow, width), f32),
            pltpu.VMEM((both, order), bf16),
            pltpu.VMEM((rows + PAD, width), f32),
            mark,
        ),
        in_specs=[SMEM, VMEM, VMEM, hbm, VMEM],
        out_specs=(VMEM,) * 4,
        scratch_shapes=[pltpu.SemaphoreType.DMA],
        compiler_params=SMALL,
        name="own",
    )(piece_at, near(mine), near(other), far_off(sigma_end), near(arrow_end.T))

    first_2 = hop(shared(first, 2))
    second, token = lax.optimization_barrier((second, token))
    second_2 = hop(shared(second, 2))
    keep_1, give_1, token = product(far_kernel, "far", 2, (first, second), token)
    first_2, token = lax.optimization_barrier((first_2, token))
    first_4 = hop(shared(first_2, 4), 2)
    first_3 = hop(shared(first_2, 3))
    second_3 = hop(shared(second_2, 3))
    given_1 = swap(give_1)
    token, given_1 = lax.optimization_barrier((token, given_1))
    keep_2, give_2, token = product(
        three_kernel,
        "three",
        3,
        (first_2, second_2, first_4),
        token,
        [pltpu.VMEM((2, both + arrow, width), f32), pltpu.VMEM((2, width + arrow, width), f32)],
    )
    given_2 = swap(give_2)
    keep_3, give_3, token = product(far_kernel, "far", 2, (first_3, second_3), token)
    kept, given = (keep_1, keep_2, keep_3), (given_1, given_2, swap(give_3))

    message = (pieces, rows + PAD, width)
    sent, plain, own_arrow = pl.pallas_call(
        lambda *refs: message_kernel(rows, chips, hops, *refs),
        out_shape=(
            pltpu.VMEM(message, f32),
            jax.ShapeDtypeStruct((pieces, rows, width), f32),
            jax.ShapeDtypeStruct((arrow, width), f32),
        ),
        in_specs=[SMEM] + [VMEM] * (2 * hops + 1),
        out_specs=(VMEM, pl.BlockSpec(memory_space=pl.ANY), VMEM),
        scratch_shapes=[pltpu.VMEM((pieces, rows, width), f32), pltpu.SemaphoreType.DMA],
        compiler_params=SMALL,
        name="message",
    )(column_at, *map(near, (own, *kept, *given, tip_inverse, decay)))

    def exchange(values):
        moved = lax.all_to_all(values.astype(jnp.float16), "tm", 0, 0, tiled=True)
        return moved.astype(jnp.float32)

    ahead = pl.pallas_call(
        lambda *refs: scan_kernel(rows, *refs),
        out_shape=pltpu.VMEM(message, f32),
        in_specs=[VMEM] * 2,
        out_specs=VMEM,
        scratch_shapes=[pltpu.VMEM((pieces, width), f32)],
        compiler_params=SMALL,
        name="suffix",
    )(near(exchange(sent)), near(end))
    sigma, arrows = pl.pallas_call(
        lambda *refs: last_kernel(rows, *refs),
        out_shape=(jax.ShapeDtypeStruct((order, width), f32), jax.ShapeDtypeStruct((arrow, width), f32)),
        in_specs=[SMEM] + [VMEM] * 4,
        scratch_shapes=[pltpu.VMEM((pieces, width), f32)],
        compiler_params=SMALL,
        name="last",
    )(column_at, *map(near, (plain, own_arrow, exchange(ahead), decay)))
    return sigma[None], arrows.T[None]


def solution(mesh):
    placed = (
        P("tm", None, "space"),
        P("tm", None, "space"),
        P("tm", None),
        P(),
        P(None, "space"),
        P("space", None),
    )
    return jax.shard_map(
        body,
        mesh=mesh,
        in_specs=placed,
        out_specs=(P("tm", None, "space"), P("tm", "space", None)),
        check_vma=False,
    )
```

```python
import jax
import jax.numpy as jnp
from jax import lax
from jax.experimental import pallas as pl
from jax.experimental.pallas import tpu as pltpu
from jax.sharding import PartitionSpec as P

CORES = 2
PAD = 8
TOP = 14.0
DECAY = 1024.0


def split3(x):
    hi = x.astype(jnp.bfloat16)
    rest = x - hi.astype(jnp.float32)
    mid = rest.astype(jnp.bfloat16)
    low = (rest - mid.astype(jnp.float32)).astype(jnp.bfloat16)
    return hi, mid, low


def dot(a, b):
    return jnp.dot(a, b, preferred_element_type=jnp.float32)


def border_times(border, tile):
    hi, mid, low = split3(tile)
    return dot(border, hi) + dot(border, mid) + dot(border, low)


def exponent(x):
    largest = jnp.max(jnp.abs(x), axis=0, keepdims=True)
    return jnp.ceil(jnp.log2(jnp.maximum(largest, 2.0**-100)))


def squared(x, level):
    unit = x * jnp.exp2(TOP / 2 - level)
    return unit * jnp.abs(unit)


def rooted(x, level):
    return x * (lax.rsqrt(jnp.maximum(jnp.abs(x), 2.0**-60)) * jnp.exp2(level - TOP / 2))


def encode(panel, pair, extra):
    at = lax.broadcasted_iota(jnp.int32, pair.shape, 0)
    level, pair_level = exponent(panel), exponent(pair)
    tail = jnp.where(at < 2, squared(pair, pair_level), extra)
    tail = jnp.where(at == 2, level, jnp.where(at == 3, pair_level, tail))
    return squared(panel, level), tail


def decode(message, rows):
    tail = message[rows:, :]
    at = lax.broadcasted_iota(jnp.int32, tail.shape, 0)
    panel = rooted(message[:rows, :], tail[2:3, :])
    return panel, jnp.where(at < 2, rooted(tail, tail[3:4, :]), 0.0)


def own_kernel(at, mine, other, sigma_end, arrow_end, tile, both_t, end, token, done):
    width = mine.shape[1]
    depth = both_t.shape[1]
    rows = end.shape[0] - PAD
    share = arrow_end.shape[0] * rows // depth
    spot = pl.ds(pl.multiple_of(at[0] * rows, rows), rows)
    copy = pltpu.make_async_copy(sigma_end.at[spot], end.at[pl.ds(0, rows)], done)
    copy.start()
    place = lax.broadcasted_iota(jnp.int32, (PAD, width), 0)
    pair = jnp.zeros((PAD, width), jnp.float32)
    for r in range(share):
        pair = jnp.where(place == r, arrow_end[pl.ds(at[0] * share + r, 1), :], pair)
    end[rows:, :] = pair
    turned = jnp.concatenate([mine[:depth, :].T, other[:depth, :].T], axis=0)
    both_t[...] = turned
    got = dot(turned, mine[:depth, :])
    border = jnp.concatenate([mine[depth:, :], other[depth:, :]], axis=1)
    tile[: CORES * width, :] = got
    tile[CORES * width :, :] = border_times(border, got)
    token[...] = jnp.zeros_like(token)
    copy.wait()


def far_tiles(panels, both_t, keep, give):
    tall, width = panels[0].shape
    count = width * len(panels)
    depth = tall - (keep.shape[0] - count)
    joined = jnp.concatenate([p[:depth, :] for p in panels], axis=1)
    border = jnp.concatenate([p[depth:tall, :] for p in panels], axis=1)
    tile = dot(both_t[:, both_t.shape[1] - depth :], joined).T
    total = border_times(border, tile)
    for at, part in ((0, keep), (width, give)):
        part[:count, :] = tile[:, at : at + width]
        part[count:, :] = total[:, at : at + width]


def far_kernel(first, second, both_t, passed, keep, give, token):
    far_tiles((first, second), both_t, keep, give)
    token[...] = passed[...]


def farthest_kernel(straight, both_t, passed, keep, give, token):
    far_tiles((straight,), both_t, keep, give)
    token[...] = passed[...]


def two_parts(decay):
    scaled = decay * DECAY
    high = scaled.astype(jnp.bfloat16).astype(jnp.float32)
    return high, (scaled - high) * 256


def message_kernel(rows, chips, hops, at, own, *refs):
    kept, given = refs[:hops], refs[hops : 2 * hops]
    tip, decay, out, copied, own_arrow, plain, done = refs[2 * hops :]
    width = own.shape[1]
    per = width // rows
    chip, core = at[0] // CORES, at[0] % CORES
    way = 1 - 2 * core

    def put(block, hop, parity):
        spot = lax.rem(chip + hop + chips, chips) * CORES + parity
        plain[pl.ds(spot * per, per), :, :] = block.reshape(per, rows, width)

    put(own[:width, :], 0, core)
    put(own[width : CORES * width, :], 0, 1 - core)
    for s in range(hops):
        hop = (s + 1) * way
        put(kept[s][:width, :], -hop, core)
        put(given[s][:width, :], hop, 1 - core)
        if s < hops - 1:
            put(kept[s][width : 2 * width, :], -hop, 1 - core)
            put(given[s][width : 2 * width, :], hop, core)
    copy = pltpu.make_async_copy(plain, copied, done)
    copy.start()
    border = own_arrow.shape[0]
    total = own[CORES * width :, :]
    for part in (*kept, *given):
        total = total + part[part.shape[0] - border :, :]
    arrow = -lax.dot_general(
        tip[...],
        total,
        (((0,), (0,)), ((), ())),
        precision=lax.Precision.HIGHEST,
        preferred_element_type=jnp.float32,
    )
    own_arrow[...] = arrow
    fill = jnp.zeros((PAD - 2, width), jnp.float32)
    place = lax.broadcasted_iota(jnp.int32, (PAD, width), 0)
    by_col = decay[:, pl.ds(pl.multiple_of(at[0] * width, width), width)]
    col_high, col_low = two_parts(by_col)
    cols = jnp.where(place == 5, col_high, jnp.where(place == 6, col_low, 0.0))
    for r in range(out.shape[0]):
        by_row = jnp.concatenate(two_parts(decay[:, r * rows : (r + 1) * rows]), axis=1)
        extra = jnp.where(place == 4, by_row, cols)
        pair = jnp.concatenate([arrow[2 * r : 2 * r + 2, :], fill], axis=0)
        out[r, :rows, :], out[r, rows:, :] = encode(plain[r], pair, extra)
    copy.wait()


def scan_kernel(rows, got, end, out, turned):
    pieces, _, width = got.shape
    for s in range(pieces):
        turned[s : s + 1, :] = got[s, rows + 4 : rows + 5, :]
    columns = turned[...].T
    columns = (columns[:rows, :] + columns[rows : 2 * rows, :] * (1 / 256)) * (1 / DECAY)
    carry, pair = end[:rows, :], end[rows:, :]
    for s in range(pieces - 1, -1, -1):
        out[s, :rows, :], out[s, rows:, :] = encode(carry, pair, jnp.zeros_like(pair))
        if s == 0:
            break
        panel, arrow = decode(got[s], rows)
        by_col = (got[s, rows + 5 : rows + 6, :] + got[s, rows + 6 : rows + 7, :] * (1 / 256)) * (1 / DECAY)
        by_row = jnp.broadcast_to(columns[:, s : s + 1], (rows, width))
        carry = panel + by_row * by_col * carry
        pair = arrow + by_col * pair


def last_kernel(rows, at, plain, own_arrow, got, decay, sigma, arrows, turned):
    pieces, _, width = plain.shape
    for r in range(pieces):
        turned[r : r + 1, :rows] = decay[:, r * rows : (r + 1) * rows]
        turned[r : r + 1, rows:] = jnp.zeros((1, width - rows), jnp.float32)
    columns = turned[...].T[:rows, :]
    by_col = decay[:, pl.ds(pl.multiple_of(at[0] * width, width), width)]
    for r in range(pieces):
        later, later_arrow = decode(got[r], rows)
        by_row = jnp.broadcast_to(columns[:, r : r + 1], later.shape)
        sigma[r * rows : (r + 1) * rows, :] = plain[r] + by_row * by_col * later
        pair = slice(2 * r, 2 * r + 2)
        arrows[pair, :] = own_arrow[pair, :] + by_col * later_arrow[:2, :]


VMEM = pl.BlockSpec(memory_space=pltpu.VMEM)
SMEM = pl.BlockSpec(memory_space=pltpu.SMEM)


SMALL = pltpu.CompilerParams(vmem_limit_bytes=12 << 20)


def near(x):
    return pltpu.with_memory_space_constraint(x, pltpu.VMEM)


def far_off(x):
    return pltpu.with_memory_space_constraint(x, pltpu.HBM)


def body(inverse_factor, arrow_factor, decay, tip_inverse, sigma_end, arrow_end):
    factor_cols = inverse_factor[0]
    order, width = factor_cols.shape
    arrow = tip_inverse.shape[0]
    pieces, devices = lax.axis_size("tm"), lax.axis_size("space")
    chips, cut = devices // CORES, CORES * width
    rows, both, hops = order // pieces, CORES * width, chips // 2
    f32, bf16 = jnp.float32, jnp.bfloat16
    column_at = lax.axis_index("space").reshape(1)
    piece_at = lax.axis_index("tm").reshape(1)
    hbm = pl.BlockSpec(memory_space=pltpu.HBM)

    def pack_kernel(cols, border, out, done):
        copies = [
            pltpu.make_async_copy(cols, out.at[pl.ds(0, order)], done.at[0]),
            pltpu.make_async_copy(border, out.at[pl.ds(order, arrow)], done.at[1]),
        ]
        for copy in copies:
            copy.start()
        for copy in copies:
            copy.wait()

    mine = pl.pallas_call(
        pack_kernel,
        out_shape=pltpu.VMEM((order + arrow, width), bf16),
        in_specs=[hbm, hbm],
        out_specs=VMEM,
        scratch_shapes=[pltpu.SemaphoreType.DMA((2,))],
        compiler_params=SMALL,
        name="pack",
    )(far_off(factor_cols), far_off(arrow_factor[0]))

    def hop(panel, count=1):
        pairs = []
        for p in range(devices):
            chip, core = p // CORES, p % CORES
            pairs.append((p, (chip + count * (1 - 2 * core)) % chips * CORES + core))
        return lax.ppermute(panel, "space", pairs)

    def swap(tile):
        return lax.ppermute(tile, "space", [(p, p ^ 1) for p in range(devices)])

    def shared(panel, count):
        return panel[cut * count - (order + arrow - panel.shape[0]) :]

    def product(kernel, name, count, panels, token):
        tall = count * width + arrow
        return pl.pallas_call(
            kernel,
            out_shape=(*[jax.ShapeDtypeStruct((tall, width), f32)] * 2, mark),
            in_specs=[VMEM] * (len(panels) + 2),
            out_specs=(VMEM,) * 3,
            compiler_params=SMALL,
            name=name,
        )(*map(near, panels), near(both_t), token)

    first = hop(shared(mine, 1))
    other = swap(mine)
    second = hop(shared(other, 1))
    mark = jax.ShapeDtypeStruct((8, width), f32)
    own, both_t, end, token = pl.pallas_call(
        own_kernel,
        out_shape=(
            pltpu.VMEM((both + arrow, width), f32),
            pltpu.VMEM((both, order), bf16),
            pltpu.VMEM((rows + PAD, width), f32),
            mark,
        ),
        in_specs=[SMEM, VMEM, VMEM, hbm, VMEM],
        out_specs=(VMEM,) * 4,
        scratch_shapes=[pltpu.SemaphoreType.DMA],
        compiler_params=SMALL,
        name="own",
    )(piece_at, near(mine), near(other), far_off(sigma_end), near(arrow_end.T))

    first_2 = hop(shared(first, 2))
    second, token = lax.optimization_barrier((second, token))
    second_2 = hop(shared(second, 2))
    keep_1, give_1, token = product(far_kernel, "far", 2, (first, second), token)
    first_2, token = lax.optimization_barrier((first_2, token))
    first_3 = hop(shared(first_2, 3))
    second_3 = hop(shared(second_2, 3))
    first_4 = hop(shared(first_2, 4), 2)
    given_1 = swap(give_1)
    keep_2, give_2, token = product(far_kernel, "far", 2, (first_2, second_2), token)
    given_2 = swap(give_2)
    token, given_1, given_2 = lax.optimization_barrier((token, given_1, given_2))
    keep_3, give_3, token = product(far_kernel, "far", 2, (first_3, second_3), token)
    keep_4, give_4, token = product(farthest_kernel, "farthest", 1, (first_4,), token)
    kept, given = (keep_1, keep_2, keep_3, keep_4), (given_1, given_2, swap(give_3), swap(give_4))

    message = (pieces, rows + PAD, width)
    sent, plain, own_arrow = pl.pallas_call(
        lambda *refs: message_kernel(rows, chips, hops, *refs),
        out_shape=(
            pltpu.VMEM(message, f32),
            jax.ShapeDtypeStruct((pieces, rows, width), f32),
            jax.ShapeDtypeStruct((arrow, width), f32),
        ),
        in_specs=[SMEM] + [VMEM] * (2 * hops + 3),
        out_specs=(VMEM, pl.BlockSpec(memory_space=pl.ANY), VMEM),
        scratch_shapes=[pltpu.VMEM((pieces, rows, width), f32), pltpu.SemaphoreType.DMA],
        compiler_params=SMALL,
        name="message",
    )(column_at, *map(near, (own, *kept, *given, tip_inverse, decay)))

    def exchange(values):
        moved = lax.all_to_all(values.astype(jnp.float16), "tm", 0, 0, tiled=True)
        return moved.astype(jnp.float32)

    ahead = pl.pallas_call(
        lambda *refs: scan_kernel(rows, *refs),
        out_shape=pltpu.VMEM(message, f32),
        in_specs=[VMEM] * 2,
        out_specs=VMEM,
        scratch_shapes=[pltpu.VMEM((pieces, width), f32)],
        compiler_params=SMALL,
        name="suffix",
    )(near(exchange(sent)), near(end))
    sigma, arrows = pl.pallas_call(
        lambda *refs: last_kernel(rows, *refs),
        out_shape=(jax.ShapeDtypeStruct((order, width), f32), jax.ShapeDtypeStruct((arrow, width), f32)),
        in_specs=[SMEM] + [VMEM] * 4,
        scratch_shapes=[pltpu.VMEM((pieces, width), f32)],
        compiler_params=SMALL,
        name="last",
    )(column_at, *map(near, (plain, own_arrow, exchange(ahead), decay)))
    return sigma[None], arrows.T[None]


def solution(mesh):
    placed = (
        P("tm", None, "space"),
        P("tm", None, "space"),
        P("tm", None),
        P(),
        P(None, "space"),
        P("space", None),
    )
    return jax.shard_map(
        body,
        mesh=mesh,
        in_specs=placed,
        out_specs=(P("tm", None, "space"), P("tm", "space", None)),
        check_vma=False,
    )
```

```python
import jax
import jax.numpy as jnp
from jax import lax
from jax.experimental import pallas as pl
from jax.experimental.pallas import tpu as pltpu
from jax.sharding import PartitionSpec as P

CORES = 2
PAD = 8
TOP = 14.0
DECAY = 1024.0


def split3(x):
    hi = x.astype(jnp.bfloat16)
    rest = x - hi.astype(jnp.float32)
    mid = rest.astype(jnp.bfloat16)
    low = (rest - mid.astype(jnp.float32)).astype(jnp.bfloat16)
    return hi, mid, low


def dot(a, b):
    return jnp.dot(a, b, preferred_element_type=jnp.float32)


def border_times(border, tile):
    hi, mid, low = split3(tile)
    return dot(border, hi) + dot(border, mid) + dot(border, low)


def exponent(x):
    largest = jnp.max(jnp.abs(x), axis=0, keepdims=True)
    return jnp.ceil(jnp.log2(jnp.maximum(largest, 2.0**-100)))


def squared(x, level):
    unit = x * jnp.exp2(TOP / 2 - level)
    return unit * jnp.abs(unit)


def rooted(x, level):
    return x * (lax.rsqrt(jnp.maximum(jnp.abs(x), 2.0**-60)) * jnp.exp2(level - TOP / 2))


def encode(panel, pair, extra):
    at = lax.broadcasted_iota(jnp.int32, pair.shape, 0)
    level, pair_level = exponent(panel), exponent(pair)
    tail = jnp.where(at < 2, squared(pair, pair_level), extra)
    tail = jnp.where(at == 2, level, jnp.where(at == 3, pair_level, tail))
    return squared(panel, level), tail


def decode(message, rows):
    tail = message[rows:, :]
    at = lax.broadcasted_iota(jnp.int32, tail.shape, 0)
    panel = rooted(message[:rows, :], tail[2:3, :])
    return panel, jnp.where(at < 2, rooted(tail, tail[3:4, :]), 0.0)


def own_kernel(at, mine, other, mine_top, other_top, sigma_end, arrow_end, tile, both_t, end, token, done):
    tall, width = mine.shape
    depth = both_t.shape[1]
    order = depth + mine_top.shape[0]
    rows = end.shape[0] - PAD
    share = arrow_end.shape[0] * rows // order
    spot = pl.ds(pl.multiple_of(at[0] * rows, rows), rows)
    copy = pltpu.make_async_copy(sigma_end.at[spot], end.at[pl.ds(0, rows)], done)
    copy.start()
    place = lax.broadcasted_iota(jnp.int32, (PAD, width), 0)
    pair = jnp.zeros((PAD, width), jnp.float32)
    for r in range(share):
        pair = jnp.where(place == r, arrow_end[pl.ds(at[0] * share + r, 1), :], pair)
    end[rows:, :] = pair
    turned = jnp.concatenate([mine[:depth, :].T, other[:depth, :].T], axis=0)
    top = jnp.concatenate([mine_top[...].T, other_top[...].T], axis=0)
    both_t[...] = turned
    got = dot(turned, mine[:depth, :]) + dot(top, mine_top[...])
    border = jnp.concatenate([mine[depth:tall, :], other[depth:tall, :]], axis=1)
    tile[: CORES * width, :] = got
    tile[CORES * width :, :] = border_times(border, got)
    token[...] = jnp.zeros_like(token)
    copy.wait()


def far_tiles(panels, both_t, keep, give):
    tall, width = panels[0].shape
    count = width * len(panels)
    depth = tall - (keep.shape[0] - count)
    joined = jnp.concatenate([p[:depth, :] for p in panels], axis=1)
    border = jnp.concatenate([p[depth:tall, :] for p in panels], axis=1)
    tile = dot(both_t[:, both_t.shape[1] - depth :], joined).T
    total = border_times(border, tile)
    for at, part in ((0, keep), (width, give)):
        part[:count, :] = tile[:, at : at + width]
        part[count:, :] = total[:, at : at + width]


def far_kernel(first, second, both_t, passed, keep, give, token):
    far_tiles((first, second), both_t, keep, give)
    token[...] = passed[...]


def half_kernel(low, first, second, both_t, passed, out):
    tall, width = first.shape
    count = CORES * width
    depth = tall - (out.shape[0] - count)
    joined = jnp.concatenate([first[:depth, :], second[:depth, :]], axis=1)
    border = jnp.concatenate([first[depth:tall, :], second[depth:tall, :]], axis=1)
    tile = dot(both_t[low : low + width, both_t.shape[1] - depth :], joined).T
    out[:count, :] = tile
    out[count:, :] = border_times(border, tile)


def three_kernel(first, second, straight, both_t, passed, keep, give, token, pair, single):
    count, width = CORES * first.shape[1], straight.shape[1]
    far_tiles((first, second), both_t, pair.at[0], pair.at[1])
    far_tiles((straight,), both_t, single.at[0], single.at[1])
    for at, out in enumerate((keep, give)):
        out[:count, :] = pair[at, :count, :]
        out[count : count + width, :] = single[at, :width, :]
        out[count + width :, :] = pair[at, count:, :] + single[at, width:, :]
    token[...] = passed[...]


def two_parts(decay):
    scaled = decay * DECAY
    high = scaled.astype(jnp.bfloat16).astype(jnp.float32)
    return high, (scaled - high) * 256


def message_kernel(rows, chips, hops, at, own, *refs):
    kept, given = refs[: hops - 1], refs[hops - 1 : 2 * hops - 2]
    tip, decay, out, copied, own_arrow, plain, done = refs[2 * hops - 2 :]
    width = own.shape[1]
    per = width // rows
    chip, core = at[0] // CORES, at[0] % CORES
    way = 1 - 2 * core

    def put(block, hop, parity):
        spot = lax.rem(chip + hop + chips, chips) * CORES + parity
        plain[pl.ds(spot * per, per), :, :] = block.reshape(per, rows, width)

    put(own[:width, :], 0, core)
    put(own[width : CORES * width, :], 0, 1 - core)
    for s in range(hops - 1):
        hop = (s + 1) * way
        put(kept[s][:width, :], -hop, core)
        put(given[s][:width, :], hop, 1 - core)
        put(kept[s][width : 2 * width, :], -hop, 1 - core)
        put(given[s][width : 2 * width, :], hop, core)
        if kept[s].shape[0] > 3 * width:
            put(kept[s][2 * width : 3 * width, :], hops, core)
            put(given[s][2 * width : 3 * width, :], hops, 1 - core)
    copy = pltpu.make_async_copy(plain, copied, done)
    copy.start()
    border = own_arrow.shape[0]
    total = own[CORES * width :, :]
    for part in (*kept, *given):
        total = total + part[part.shape[0] - border :, :]
    arrow = -lax.dot_general(
        tip[...],
        total,
        (((0,), (0,)), ((), ())),
        precision=lax.Precision.HIGHEST,
        preferred_element_type=jnp.float32,
    )
    own_arrow[...] = arrow
    fill = jnp.zeros((PAD - 2, width), jnp.float32)
    place = lax.broadcasted_iota(jnp.int32, (PAD, width), 0)
    by_col = decay[:, pl.ds(pl.multiple_of(at[0] * width, width), width)]
    col_high, col_low = two_parts(by_col)
    cols = jnp.where(place == 5, col_high, jnp.where(place == 6, col_low, 0.0))
    for r in range(out.shape[0]):
        by_row = jnp.concatenate(two_parts(decay[:, r * rows : (r + 1) * rows]), axis=1)
        extra = jnp.where(place == 4, by_row, cols)
        pair = jnp.concatenate([arrow[2 * r : 2 * r + 2, :], fill], axis=0)
        out[r, :rows, :], out[r, rows:, :] = encode(plain[r], pair, extra)
    copy.wait()


def scan_kernel(rows, got, end, out, turned):
    pieces, _, width = got.shape
    for s in range(pieces):
        turned[s : s + 1, :] = got[s, rows + 4 : rows + 5, :]
    columns = turned[...].T
    columns = (columns[:rows, :] + columns[rows : 2 * rows, :] * (1 / 256)) * (1 / DECAY)
    carry, pair = end[:rows, :], end[rows:, :]
    for s in range(pieces - 1, -1, -1):
        out[s, :rows, :], out[s, rows:, :] = encode(carry, pair, jnp.zeros_like(pair))
        if s == 0:
            break
        panel, arrow = decode(got[s], rows)
        by_col = (got[s, rows + 5 : rows + 6, :] + got[s, rows + 6 : rows + 7, :] * (1 / 256)) * (1 / DECAY)
        by_row = jnp.broadcast_to(columns[:, s : s + 1], (rows, width))
        carry = panel + by_row * by_col * carry
        pair = arrow + by_col * pair


def last_kernel(rows, at, plain, own_arrow, got, decay, sigma, arrows, turned):
    pieces, _, width = plain.shape
    for r in range(pieces):
        turned[r : r + 1, :rows] = decay[:, r * rows : (r + 1) * rows]
        turned[r : r + 1, rows:] = jnp.zeros((1, width - rows), jnp.float32)
    columns = turned[...].T[:rows, :]
    by_col = decay[:, pl.ds(pl.multiple_of(at[0] * width, width), width)]
    for r in range(pieces):
        later, later_arrow = decode(got[r], rows)
        by_row = jnp.broadcast_to(columns[:, r : r + 1], later.shape)
        sigma[r * rows : (r + 1) * rows, :] = plain[r] + by_row * by_col * later
        pair = slice(2 * r, 2 * r + 2)
        arrows[pair, :] = own_arrow[pair, :] + by_col * later_arrow[:2, :]


VMEM = pl.BlockSpec(memory_space=pltpu.VMEM)
SMEM = pl.BlockSpec(memory_space=pltpu.SMEM)


SMALL = pltpu.CompilerParams(vmem_limit_bytes=12 << 20)


def near(x):
    return pltpu.with_memory_space_constraint(x, pltpu.VMEM)


def far_off(x):
    return pltpu.with_memory_space_constraint(x, pltpu.HBM)


def body(inverse_factor, arrow_factor, decay, tip_inverse, sigma_end, arrow_end):
    factor_cols = inverse_factor[0]
    order, width = factor_cols.shape
    arrow = tip_inverse.shape[0]
    pieces, devices = lax.axis_size("tm"), lax.axis_size("space")
    chips, cut = devices // CORES, CORES * width
    rows, both, hops = order // pieces, CORES * width, chips // 2
    f32, bf16 = jnp.float32, jnp.bfloat16
    column_at = lax.axis_index("space").reshape(1)
    piece_at = lax.axis_index("tm").reshape(1)
    hbm = pl.BlockSpec(memory_space=pltpu.HBM)

    def pack_kernel(cols, border, out, top, done):
        depth = order - cut
        copies = [
            pltpu.make_async_copy(cols.at[pl.ds(cut, depth)], out.at[pl.ds(0, depth)], done.at[0]),
            pltpu.make_async_copy(border, out.at[pl.ds(depth, arrow)], done.at[1]),
            pltpu.make_async_copy(cols.at[pl.ds(0, cut)], top, done.at[2]),
        ]
        for copy in copies:
            copy.start()
        for copy in copies:
            copy.wait()

    mine, top = pl.pallas_call(
        pack_kernel,
        out_shape=(pltpu.VMEM((order - cut + arrow, width), bf16), pltpu.VMEM((cut, width), bf16)),
        in_specs=[hbm, hbm],
        out_specs=(VMEM, VMEM),
        scratch_shapes=[pltpu.SemaphoreType.DMA((3,))],
        compiler_params=SMALL,
        name="pack",
    )(far_off(factor_cols), far_off(arrow_factor[0]))

    def hop(panel, count=1):
        pairs = []
        for p in range(devices):
            chip, core = p // CORES, p % CORES
            pairs.append((p, (chip + count * (1 - 2 * core)) % chips * CORES + core))
        return lax.ppermute(panel, "space", pairs)

    def swap(tile):
        return lax.ppermute(tile, "space", [(p, p ^ 1) for p in range(devices)])

    def shared(panel, count):
        return panel[cut * count - (order + arrow - panel.shape[0]) :]

    def product(kernel, name, count, panels, token, scratch=()):
        tall = count * width + arrow
        return pl.pallas_call(
            kernel,
            out_shape=(*[jax.ShapeDtypeStruct((tall, width), f32)] * 2, mark),
            in_specs=[VMEM] * (len(panels) + 2),
            out_specs=(VMEM,) * 3,
            scratch_shapes=scratch,
            compiler_params=SMALL,
            name=name,
        )(*map(near, panels), near(both_t), token)

    first = hop(mine)
    other, other_top = swap(mine), swap(top)
    second = hop(other)
    mark = jax.ShapeDtypeStruct((8, width), f32)
    own, both_t, end, token = pl.pallas_call(
        own_kernel,
        out_shape=(
            pltpu.VMEM((both + arrow, width), f32),
            pltpu.VMEM((both, order - cut), bf16),
            pltpu.VMEM((rows + PAD, width), f32),
            mark,
        ),
        in_specs=[SMEM, VMEM, VMEM, VMEM, VMEM, hbm, VMEM],
        out_specs=(VMEM,) * 4,
        scratch_shapes=[pltpu.SemaphoreType.DMA],
        compiler_params=SMALL,
        name="own",
    )(piece_at, *map(near, (mine, other, top, other_top)), far_off(sigma_end), near(arrow_end.T))

    first_2 = hop(shared(first, 2))
    second, token = lax.optimization_barrier((second, token))
    second_2 = hop(shared(second, 2))
    keep_1, give_1, token = product(far_kernel, "far", 2, (first, second), token)
    first_2, token = lax.optimization_barrier((first_2, token))
    first_4 = hop(shared(first_2, 4), 2)
    first_3 = hop(shared(first_2, 3))
    second_3 = hop(shared(second_2, 3))
    given_1 = swap(give_1)
    token, given_1 = lax.optimization_barrier((token, given_1))
    keep_2, give_2, token = product(
        three_kernel,
        "three",
        3,
        (first_2, second_2, first_4),
        token,
        [pltpu.VMEM((2, both + arrow, width), f32), pltpu.VMEM((2, width + arrow, width), f32)],
    )
    given_2 = swap(give_2)
    give_3, keep_3 = [
        pl.pallas_call(
            lambda *refs, low=low: half_kernel(low, *refs),
            out_shape=jax.ShapeDtypeStruct((both + arrow, width), f32),
            in_specs=[VMEM] * 4,
            out_specs=VMEM,
            compiler_params=SMALL,
            name=name,
        )(near(first_3), near(second_3), near(both_t), token)
        for name, low in (("give", width), ("keep", 0))
    ]
    kept, given = (keep_1, keep_2, keep_3), (given_1, given_2, swap(give_3))

    message = (pieces, rows + PAD, width)
    sent, plain, own_arrow = pl.pallas_call(
        lambda *refs: message_kernel(rows, chips, hops, *refs),
        out_shape=(
            pltpu.VMEM(message, f32),
            jax.ShapeDtypeStruct((pieces, rows, width), f32),
            jax.ShapeDtypeStruct((arrow, width), f32),
        ),
        in_specs=[SMEM] + [VMEM] * (2 * hops + 1),
        out_specs=(VMEM, pl.BlockSpec(memory_space=pl.ANY), VMEM),
        scratch_shapes=[pltpu.VMEM((pieces, rows, width), f32), pltpu.SemaphoreType.DMA],
        compiler_params=SMALL,
        name="message",
    )(column_at, *map(near, (own, *kept, *given, tip_inverse, decay)))

    def exchange(values):
        moved = lax.all_to_all(values.astype(jnp.float16), "tm", 0, 0, tiled=True)
        return moved.astype(jnp.float32)

    ahead = pl.pallas_call(
        lambda *refs: scan_kernel(rows, *refs),
        out_shape=pltpu.VMEM(message, f32),
        in_specs=[VMEM] * 2,
        out_specs=VMEM,
        scratch_shapes=[pltpu.VMEM((pieces, width), f32)],
        compiler_params=SMALL,
        name="suffix",
    )(near(exchange(sent)), near(end))
    sigma, arrows = pl.pallas_call(
        lambda *refs: last_kernel(rows, *refs),
        out_shape=(jax.ShapeDtypeStruct((order, width), f32), jax.ShapeDtypeStruct((arrow, width), f32)),
        in_specs=[SMEM] + [VMEM] * 4,
        scratch_shapes=[pltpu.VMEM((pieces, width), f32)],
        compiler_params=SMALL,
        name="last",
    )(column_at, *map(near, (plain, own_arrow, exchange(ahead), decay)))
    return sigma[None], arrows.T[None]


def solution(mesh):
    placed = (
        P("tm", None, "space"),
        P("tm", None, "space"),
        P("tm", None),
        P(),
        P(None, "space"),
        P("space", None),
    )
    return jax.shard_map(
        body,
        mesh=mesh,
        in_specs=placed,
        out_specs=(P("tm", None, "space"), P("tm", "space", None)),
        check_vma=False,
    )
```

```python
import jax
import jax.numpy as jnp
from jax import lax
from jax.experimental import pallas as pl
from jax.experimental.pallas import tpu as pltpu
from jax.sharding import PartitionSpec as P

CORES = 2
PAD = 8
TOP = 14.0
DECAY = 1024.0


def split3(x):
    hi = x.astype(jnp.bfloat16)
    rest = x - hi.astype(jnp.float32)
    mid = rest.astype(jnp.bfloat16)
    low = (rest - mid.astype(jnp.float32)).astype(jnp.bfloat16)
    return hi, mid, low


def dot(a, b):
    return jnp.dot(a, b, preferred_element_type=jnp.float32)


def border_times(border, tile):
    hi, mid, low = split3(tile)
    return dot(border, hi) + dot(border, mid) + dot(border, low)


def exponent(x):
    largest = jnp.max(jnp.abs(x), axis=0, keepdims=True)
    return jnp.ceil(jnp.log2(jnp.maximum(largest, 2.0**-100)))


def squared(x, level):
    unit = x * jnp.exp2(TOP / 2 - level)
    return unit * jnp.abs(unit)


def rooted(x, level):
    return x * (lax.rsqrt(jnp.maximum(jnp.abs(x), 2.0**-60)) * jnp.exp2(level - TOP / 2))


def encode(panel, pair, extra):
    at = lax.broadcasted_iota(jnp.int32, pair.shape, 0)
    level, pair_level = exponent(panel), exponent(pair)
    tail = jnp.where(at < 2, squared(pair, pair_level), extra)
    tail = jnp.where(at == 2, level, jnp.where(at == 3, pair_level, tail))
    return squared(panel, level), tail


def decode(message, rows):
    tail = message[rows:, :]
    at = lax.broadcasted_iota(jnp.int32, tail.shape, 0)
    panel = rooted(message[:rows, :], tail[2:3, :])
    return panel, jnp.where(at < 2, rooted(tail, tail[3:4, :]), 0.0)


def own_kernel(at, mine, other, mine_top, other_top, sigma_end, arrow_end, tile, both_t, end, token, done):
    tall, width = mine.shape
    depth = both_t.shape[1]
    order = depth + mine_top.shape[0]
    rows = end.shape[0] - PAD
    share = arrow_end.shape[0] * rows // order
    spot = pl.ds(pl.multiple_of(at[0] * rows, rows), rows)
    copy = pltpu.make_async_copy(sigma_end.at[spot], end.at[pl.ds(0, rows)], done)
    copy.start()
    place = lax.broadcasted_iota(jnp.int32, (PAD, width), 0)
    pair = jnp.zeros((PAD, width), jnp.float32)
    for r in range(share):
        pair = jnp.where(place == r, arrow_end[pl.ds(at[0] * share + r, 1), :], pair)
    end[rows:, :] = pair
    turned = jnp.concatenate([mine[:depth, :].T, other[:depth, :].T], axis=0)
    top = jnp.concatenate([mine_top[...].T, other_top[...].T], axis=0)
    both_t[...] = turned
    got = dot(turned, mine[:depth, :]) + dot(top, mine_top[...])
    border = jnp.concatenate([mine[depth:tall, :], other[depth:tall, :]], axis=1)
    tile[: CORES * width, :] = got
    tile[CORES * width :, :] = border_times(border, got)
    token[...] = jnp.zeros_like(token)
    copy.wait()


def far_tiles(panels, both_t, keep, give):
    tall, width = panels[0].shape
    count = width * len(panels)
    depth = tall - (keep.shape[0] - count)
    joined = jnp.concatenate([p[:depth, :] for p in panels], axis=1)
    border = jnp.concatenate([p[depth:tall, :] for p in panels], axis=1)
    tile = dot(both_t[:, both_t.shape[1] - depth :], joined).T
    total = border_times(border, tile)
    for at, part in ((0, keep), (width, give)):
        part[:count, :] = tile[:, at : at + width]
        part[count:, :] = total[:, at : at + width]


def far_kernel(first, second, both_t, passed, keep, give, token):
    far_tiles((first, second), both_t, keep, give)
    token[...] = passed[...]


def half_kernel(low, first, second, both_t, passed, out):
    tall, width = first.shape
    count = CORES * width
    depth = tall - (out.shape[0] - count)
    joined = jnp.concatenate([first[:depth, :], second[:depth, :]], axis=1)
    border = jnp.concatenate([first[depth:tall, :], second[depth:tall, :]], axis=1)
    tile = dot(both_t[low : low + width, both_t.shape[1] - depth :], joined).T
    out[:count, :] = tile
    out[count:, :] = border_times(border, tile)


def three_kernel(first, second, straight, both_t, passed, keep, give, token, pair, single):
    count, width = CORES * first.shape[1], straight.shape[1]
    far_tiles((first, second), both_t, pair.at[0], pair.at[1])
    far_tiles((straight,), both_t, single.at[0], single.at[1])
    for at, out in enumerate((keep, give)):
        out[:count, :] = pair[at, :count, :]
        out[count : count + width, :] = single[at, :width, :]
        out[count + width :, :] = pair[at, count:, :] + single[at, width:, :]
    token[...] = passed[...]


def two_parts(decay):
    scaled = decay * DECAY
    high = scaled.astype(jnp.bfloat16).astype(jnp.float32)
    return high, (scaled - high) * 256


def message_kernel(rows, chips, hops, at, own, *refs):
    kept, given = refs[: hops - 1], refs[hops - 1 : 2 * hops - 2]
    tip, decay, out, plain, own_arrow = refs[2 * hops - 2 :]
    width = own.shape[1]
    per = width // rows
    chip, core = at[0] // CORES, at[0] % CORES
    way = 1 - 2 * core

    def put(block, hop, parity):
        spot = lax.rem(chip + hop + chips, chips) * CORES + parity
        plain[pl.ds(spot * per, per), :, :] = block.reshape(per, rows, width)

    put(own[:width, :], 0, core)
    put(own[width : CORES * width, :], 0, 1 - core)
    for s in range(hops - 1):
        hop = (s + 1) * way
        put(kept[s][:width, :], -hop, core)
        put(given[s][:width, :], hop, 1 - core)
        put(kept[s][width : 2 * width, :], -hop, 1 - core)
        put(given[s][width : 2 * width, :], hop, core)
        if kept[s].shape[0] > 3 * width:
            put(kept[s][2 * width : 3 * width, :], hops, core)
            put(given[s][2 * width : 3 * width, :], hops, 1 - core)
    border = own_arrow.shape[0]
    total = own[CORES * width :, :]
    for part in (*kept, *given):
        total = total + part[part.shape[0] - border :, :]
    arrow = -lax.dot_general(
        tip[...],
        total,
        (((0,), (0,)), ((), ())),
        precision=lax.Precision.HIGHEST,
        preferred_element_type=jnp.float32,
    )
    own_arrow[...] = arrow
    fill = jnp.zeros((PAD - 2, width), jnp.float32)
    place = lax.broadcasted_iota(jnp.int32, (PAD, width), 0)
    by_col = decay[:, pl.ds(pl.multiple_of(at[0] * width, width), width)]
    col_high, col_low = two_parts(by_col)
    cols = jnp.where(place == 5, col_high, jnp.where(place == 6, col_low, 0.0))
    for r in range(out.shape[0]):
        by_row = jnp.concatenate(two_parts(decay[:, r * rows : (r + 1) * rows]), axis=1)
        extra = jnp.where(place == 4, by_row, cols)
        pair = jnp.concatenate([arrow[2 * r : 2 * r + 2, :], fill], axis=0)
        out[r, :rows, :], out[r, rows:, :] = encode(plain[r], pair, extra)


def scan_kernel(rows, got, end, out, turned):
    pieces, _, width = got.shape
    for s in range(pieces):
        turned[s : s + 1, :] = got[s, rows + 4 : rows + 5, :]
    columns = turned[...].T
    columns = (columns[:rows, :] + columns[rows : 2 * rows, :] * (1 / 256)) * (1 / DECAY)
    carry, pair = end[:rows, :], end[rows:, :]
    for s in range(pieces - 1, -1, -1):
        out[s, :rows, :], out[s, rows:, :] = encode(carry, pair, jnp.zeros_like(pair))
        if s == 0:
            break
        panel, arrow = decode(got[s], rows)
        by_col = (got[s, rows + 5 : rows + 6, :] + got[s, rows + 6 : rows + 7, :] * (1 / 256)) * (1 / DECAY)
        by_row = jnp.broadcast_to(columns[:, s : s + 1], (rows, width))
        carry = panel + by_row * by_col * carry
        pair = arrow + by_col * pair


def last_kernel(rows, at, plain, own_arrow, got, decay, sigma, arrows, turned):
    pieces, _, width = plain.shape
    for r in range(pieces):
        turned[r : r + 1, :rows] = decay[:, r * rows : (r + 1) * rows]
        turned[r : r + 1, rows:] = jnp.zeros((1, width - rows), jnp.float32)
    columns = turned[...].T[:rows, :]
    by_col = decay[:, pl.ds(pl.multiple_of(at[0] * width, width), width)]
    for r in range(pieces):
        later, later_arrow = decode(got[r], rows)
        by_row = jnp.broadcast_to(columns[:, r : r + 1], later.shape)
        sigma[r * rows : (r + 1) * rows, :] = plain[r] + by_row * by_col * later
        pair = slice(2 * r, 2 * r + 2)
        arrows[pair, :] = own_arrow[pair, :] + by_col * later_arrow[:2, :]


VMEM = pl.BlockSpec(memory_space=pltpu.VMEM)
SMEM = pl.BlockSpec(memory_space=pltpu.SMEM)


SMALL = pltpu.CompilerParams(vmem_limit_bytes=12 << 20)


def near(x):
    return pltpu.with_memory_space_constraint(x, pltpu.VMEM)


def far_off(x):
    return pltpu.with_memory_space_constraint(x, pltpu.HBM)


def body(inverse_factor, arrow_factor, decay, tip_inverse, sigma_end, arrow_end):
    factor_cols = inverse_factor[0]
    order, width = factor_cols.shape
    arrow = tip_inverse.shape[0]
    pieces, devices = lax.axis_size("tm"), lax.axis_size("space")
    chips, cut = devices // CORES, CORES * width
    rows, both, hops = order // pieces, CORES * width, chips // 2
    f32, bf16 = jnp.float32, jnp.bfloat16
    column_at = lax.axis_index("space").reshape(1)
    piece_at = lax.axis_index("tm").reshape(1)
    hbm = pl.BlockSpec(memory_space=pltpu.HBM)

    def pack_kernel(cols, border, out, top, done):
        depth = order - cut
        copies = [
            pltpu.make_async_copy(cols.at[pl.ds(cut, depth)], out.at[pl.ds(0, depth)], done.at[0]),
            pltpu.make_async_copy(border, out.at[pl.ds(depth, arrow)], done.at[1]),
            pltpu.make_async_copy(cols.at[pl.ds(0, cut)], top, done.at[2]),
        ]
        for copy in copies:
            copy.start()
        for copy in copies:
            copy.wait()

    mine, top = pl.pallas_call(
        pack_kernel,
        out_shape=(pltpu.VMEM((order - cut + arrow, width), bf16), pltpu.VMEM((cut, width), bf16)),
        in_specs=[hbm, hbm],
        out_specs=(VMEM, VMEM),
        scratch_shapes=[pltpu.SemaphoreType.DMA((3,))],
        compiler_params=SMALL,
        name="pack",
    )(far_off(factor_cols), far_off(arrow_factor[0]))

    def hop(panel, count=1):
        pairs = []
        for p in range(devices):
            chip, core = p // CORES, p % CORES
            pairs.append((p, (chip + count * (1 - 2 * core)) % chips * CORES + core))
        return lax.ppermute(panel, "space", pairs)

    def swap(tile):
        return lax.ppermute(tile, "space", [(p, p ^ 1) for p in range(devices)])

    def shared(panel, count):
        return panel[cut * count - (order + arrow - panel.shape[0]) :]

    def product(kernel, name, count, panels, token, scratch=()):
        tall = count * width + arrow
        return pl.pallas_call(
            kernel,
            out_shape=(*[jax.ShapeDtypeStruct((tall, width), f32)] * 2, mark),
            in_specs=[VMEM] * (len(panels) + 2),
            out_specs=(VMEM,) * 3,
            scratch_shapes=scratch,
            compiler_params=SMALL,
            name=name,
        )(*map(near, panels), near(both_t), token)

    first = hop(mine)
    other, other_top = swap(mine), swap(top)
    second = hop(other)
    mark = jax.ShapeDtypeStruct((8, width), f32)
    own, both_t, end, token = pl.pallas_call(
        own_kernel,
        out_shape=(
            pltpu.VMEM((both + arrow, width), f32),
            pltpu.VMEM((both, order - cut), bf16),
            pltpu.VMEM((rows + PAD, width), f32),
            mark,
        ),
        in_specs=[SMEM, VMEM, VMEM, VMEM, VMEM, hbm, VMEM],
        out_specs=(VMEM,) * 4,
        scratch_shapes=[pltpu.SemaphoreType.DMA],
        compiler_params=SMALL,
        name="own",
    )(piece_at, *map(near, (mine, other, top, other_top)), far_off(sigma_end), near(arrow_end.T))

    first_2 = hop(shared(first, 2))
    second, token = lax.optimization_barrier((second, token))
    second_2 = hop(shared(second, 2))
    keep_1, give_1, token = product(far_kernel, "far", 2, (first, second), token)
    first_2, token = lax.optimization_barrier((first_2, token))
    first_4 = hop(shared(first_2, 4), 2)
    first_3 = hop(shared(first_2, 3))
    second_3 = hop(shared(second_2, 3))
    given_1 = swap(give_1)
    token, given_1 = lax.optimization_barrier((token, given_1))
    keep_2, give_2, token = product(
        three_kernel,
        "three",
        3,
        (first_2, second_2, first_4),
        token,
        [pltpu.VMEM((2, both + arrow, width), f32), pltpu.VMEM((2, width + arrow, width), f32)],
    )
    given_2 = swap(give_2)
    give_3, keep_3 = [
        pl.pallas_call(
            lambda *refs, low=low: half_kernel(low, *refs),
            out_shape=jax.ShapeDtypeStruct((both + arrow, width), f32),
            in_specs=[VMEM] * 4,
            out_specs=VMEM,
            compiler_params=SMALL,
            name=name,
        )(near(first_3), near(second_3), near(both_t), token)
        for name, low in (("give", width), ("keep", 0))
    ]
    kept, given = (keep_1, keep_2, keep_3), (given_1, given_2, swap(give_3))

    message = (pieces, rows + PAD, width)
    sent, plain, own_arrow = pl.pallas_call(
        lambda *refs: message_kernel(rows, chips, hops, *refs),
        out_shape=(
            pltpu.VMEM(message, f32),
            pltpu.VMEM((pieces, rows, width), f32),
            pltpu.VMEM((arrow, width), f32),
        ),
        in_specs=[SMEM] + [VMEM] * (2 * hops + 1),
        out_specs=(VMEM,) * 3,
        compiler_params=SMALL,
        name="message",
    )(column_at, *map(near, (own, *kept, *given, tip_inverse, decay)))

    def exchange(values):
        moved = lax.all_to_all(values.astype(jnp.float16), "tm", 0, 0, tiled=True)
        return moved.astype(jnp.float32)

    ahead = pl.pallas_call(
        lambda *refs: scan_kernel(rows, *refs),
        out_shape=pltpu.VMEM(message, f32),
        in_specs=[VMEM] * 2,
        out_specs=VMEM,
        scratch_shapes=[pltpu.VMEM((pieces, width), f32)],
        compiler_params=SMALL,
        name="suffix",
    )(near(exchange(sent)), near(end))
    sigma, arrows = pl.pallas_call(
        lambda *refs: last_kernel(rows, *refs),
        out_shape=(jax.ShapeDtypeStruct((order, width), f32), jax.ShapeDtypeStruct((arrow, width), f32)),
        in_specs=[SMEM] + [VMEM] * 4,
        scratch_shapes=[pltpu.VMEM((pieces, width), f32)],
        compiler_params=SMALL,
        name="last",
    )(column_at, *map(near, (plain, own_arrow, exchange(ahead), decay)))
    return sigma[None], arrows.T[None]


def solution(mesh):
    placed = (
        P("tm", None, "space"),
        P("tm", None, "space"),
        P("tm", None),
        P(),
        P(None, "space"),
        P("space", None),
    )
    return jax.shard_map(
        body,
        mesh=mesh,
        in_specs=placed,
        out_specs=(P("tm", None, "space"), P("tm", "space", None)),
        check_vma=False,
    )
```

```python
import jax
import jax.numpy as jnp
from jax import lax
from jax.experimental import pallas as pl
from jax.experimental.pallas import tpu as pltpu
from jax.sharding import PartitionSpec as P

CORES = 2
PAD = 8
TOP = 14.0
DECAY = 1024.0


def split3(x):
    hi = x.astype(jnp.bfloat16)
    rest = x - hi.astype(jnp.float32)
    mid = rest.astype(jnp.bfloat16)
    low = (rest - mid.astype(jnp.float32)).astype(jnp.bfloat16)
    return hi, mid, low


def dot(a, b):
    return jnp.dot(a, b, preferred_element_type=jnp.float32)


def border_times(border, tile):
    hi, mid, low = split3(tile)
    return dot(border, hi) + dot(border, mid) + dot(border, low)


def exponent(x):
    largest = jnp.max(jnp.abs(x), axis=0, keepdims=True)
    return jnp.ceil(jnp.log2(jnp.maximum(largest, 2.0**-100)))


def squared(x, level):
    unit = x * jnp.exp2(TOP / 2 - level)
    return unit * jnp.abs(unit)


def rooted(x, level):
    return x * (lax.rsqrt(jnp.maximum(jnp.abs(x), 2.0**-60)) * jnp.exp2(level - TOP / 2))


def encode(panel, pair, extra):
    at = lax.broadcasted_iota(jnp.int32, pair.shape, 0)
    level, pair_level = exponent(panel), exponent(pair)
    tail = jnp.where(at < 2, squared(pair, pair_level), extra)
    tail = jnp.where(at == 2, level, jnp.where(at == 3, pair_level, tail))
    return squared(panel, level), tail


def decode(message, rows):
    tail = message[rows:, :]
    at = lax.broadcasted_iota(jnp.int32, tail.shape, 0)
    panel = rooted(message[:rows, :], tail[2:3, :])
    return panel, jnp.where(at < 2, rooted(tail, tail[3:4, :]), 0.0)


def own_kernel(at, mine, other, mine_top, other_top, sigma_end, arrow_end, tile, both_t, end, token, done):
    tall, width = mine.shape
    depth = both_t.shape[1]
    order = depth + mine_top.shape[0]
    rows = end.shape[0] - PAD
    share = arrow_end.shape[0] * rows // order
    spot = pl.ds(pl.multiple_of(at[0] * rows, rows), rows)
    copy = pltpu.make_async_copy(sigma_end.at[spot], end.at[pl.ds(0, rows)], done)
    copy.start()
    place = lax.broadcasted_iota(jnp.int32, (PAD, width), 0)
    pair = jnp.zeros((PAD, width), jnp.float32)
    for r in range(share):
        pair = jnp.where(place == r, arrow_end[pl.ds(at[0] * share + r, 1), :], pair)
    end[rows:, :] = pair
    turned = jnp.concatenate([mine[:depth, :].T, other[:depth, :].T], axis=0)
    top = jnp.concatenate([mine_top[...].T, other_top[...].T], axis=0)
    both_t[...] = turned
    got = dot(turned, mine[:depth, :]) + dot(top, mine_top[...])
    border = jnp.concatenate([mine[depth:tall, :], other[depth:tall, :]], axis=1)
    tile[: CORES * width, :] = got
    tile[CORES * width :, :] = border_times(border, got)
    token[...] = jnp.zeros_like(token)
    copy.wait()


def far_tiles(panels, both_t, keep, give):
    tall, width = panels[0].shape
    count = width * len(panels)
    depth = tall - (keep.shape[0] - count)
    joined = jnp.concatenate([p[:depth, :] for p in panels], axis=1)
    border = jnp.concatenate([p[depth:tall, :] for p in panels], axis=1)
    tile = dot(both_t[:, both_t.shape[1] - depth :], joined).T
    total = border_times(border, tile)
    for at, part in ((0, keep), (width, give)):
        part[:count, :] = tile[:, at : at + width]
        part[count:, :] = total[:, at : at + width]


def far_kernel(first, second, both_t, passed, keep, give, token):
    far_tiles((first, second), both_t, keep, give)
    token[...] = passed[...]


def half_kernel(low, first, second, both_t, passed, out):
    tall, width = first.shape
    count = CORES * width
    depth = tall - (out.shape[0] - count)
    joined = jnp.concatenate([first[:depth, :], second[:depth, :]], axis=1)
    border = jnp.concatenate([first[depth:tall, :], second[depth:tall, :]], axis=1)
    tile = dot(both_t[low : low + width, both_t.shape[1] - depth :], joined).T
    out[:count, :] = tile
    out[count:, :] = border_times(border, tile)


def three_kernel(first, second, straight, both_t, passed, keep, give, token, pair, single):
    count, width = CORES * first.shape[1], straight.shape[1]
    far_tiles((first, second), both_t, pair.at[0], pair.at[1])
    far_tiles((straight,), both_t, single.at[0], single.at[1])
    for at, out in enumerate((keep, give)):
        out[:count, :] = pair[at, :count, :]
        out[count : count + width, :] = single[at, :width, :]
        out[count + width :, :] = pair[at, count:, :] + single[at, width:, :]
    token[...] = passed[...]


def two_parts(decay):
    scaled = decay * DECAY
    high = scaled.astype(jnp.bfloat16).astype(jnp.float32)
    return high, (scaled - high) * 256


def message_kernel(rows, chips, hops, at, own, *refs):
    kept, given = refs[: hops - 1], refs[hops - 1 : 2 * hops - 2]
    tip, decay, out, plain, own_arrow = refs[2 * hops - 2 :]
    width = own.shape[1]
    per = width // rows
    chip, core = at[0] // CORES, at[0] % CORES
    way = 1 - 2 * core

    def put(block, hop, parity):
        spot = lax.rem(chip + hop + chips, chips) * CORES + parity
        plain[pl.ds(spot * per, per), :, :] = block.reshape(per, rows, width)

    put(own[:width, :], 0, core)
    put(own[width : CORES * width, :], 0, 1 - core)
    for s in range(hops - 1):
        hop = (s + 1) * way
        put(kept[s][:width, :], -hop, core)
        put(given[s][:width, :], hop, 1 - core)
        put(kept[s][width : 2 * width, :], -hop, 1 - core)
        put(given[s][width : 2 * width, :], hop, core)
        if kept[s].shape[0] > 3 * width:
            put(kept[s][2 * width : 3 * width, :], hops, core)
            put(given[s][2 * width : 3 * width, :], hops, 1 - core)
    border = own_arrow.shape[0]
    total = own[CORES * width :, :]
    for part in (*kept, *given):
        total = total + part[part.shape[0] - border :, :]
    arrow = -lax.dot_general(
        tip[...],
        total,
        (((0,), (0,)), ((), ())),
        precision=lax.Precision.HIGHEST,
        preferred_element_type=jnp.float32,
    )
    own_arrow[...] = arrow
    fill = jnp.zeros((PAD - 2, width), jnp.float32)
    place = lax.broadcasted_iota(jnp.int32, (PAD, width), 0)
    by_col = decay[:, pl.ds(pl.multiple_of(at[0] * width, width), width)]
    col_high, col_low = two_parts(by_col)
    cols = jnp.where(place == 5, col_high, jnp.where(place == 6, col_low, 0.0))
    for r in range(out.shape[0]):
        by_row = jnp.concatenate(two_parts(decay[:, r * rows : (r + 1) * rows]), axis=1)
        extra = jnp.where(place == 4, by_row, cols)
        pair = jnp.concatenate([arrow[2 * r : 2 * r + 2, :], fill], axis=0)
        out[r, :rows, :], out[r, rows:, :] = encode(plain[r], pair, extra)


def scan_kernel(rows, got, end, out, turned):
    pieces, _, width = got.shape
    for s in range(pieces):
        turned[s : s + 1, :] = got[s, rows + 4 : rows + 5, :]
    columns = turned[...].T
    columns = (columns[:rows, :] + columns[rows : 2 * rows, :] * (1 / 256)) * (1 / DECAY)
    carry, pair = end[:rows, :], end[rows:, :]
    for s in range(pieces - 1, -1, -1):
        out[s, :rows, :], out[s, rows:, :] = encode(carry, pair, jnp.zeros_like(pair))
        if s == 0:
            break
        panel, arrow = decode(got[s], rows)
        by_col = (got[s, rows + 5 : rows + 6, :] + got[s, rows + 6 : rows + 7, :] * (1 / 256)) * (1 / DECAY)
        by_row = jnp.broadcast_to(columns[:, s : s + 1], (rows, width))
        carry = panel + by_row * by_col * carry
        pair = arrow + by_col * pair


def last_kernel(rows, at, plain, own_arrow, got, decay, sigma, arrows, turned):
    pieces, _, width = plain.shape
    for r in range(pieces):
        turned[r : r + 1, :rows] = decay[:, r * rows : (r + 1) * rows]
        turned[r : r + 1, rows:] = jnp.zeros((1, width - rows), jnp.float32)
    columns = turned[...].T[:rows, :]
    by_col = decay[:, pl.ds(pl.multiple_of(at[0] * width, width), width)]
    for r in range(pieces):
        later, later_arrow = decode(got[r], rows)
        by_row = jnp.broadcast_to(columns[:, r : r + 1], later.shape)
        sigma[r * rows : (r + 1) * rows, :] = plain[r] + by_row * by_col * later
        pair = slice(2 * r, 2 * r + 2)
        arrows[pair, :] = own_arrow[pair, :] + by_col * later_arrow[:2, :]


VMEM = pl.BlockSpec(memory_space=pltpu.VMEM)
SMEM = pl.BlockSpec(memory_space=pltpu.SMEM)


SMALL = pltpu.CompilerParams(vmem_limit_bytes=12 << 20)


def near(x):
    return pltpu.with_memory_space_constraint(x, pltpu.VMEM)


def far_off(x):
    return pltpu.with_memory_space_constraint(x, pltpu.HBM)


def body(inverse_factor, arrow_factor, decay, tip_inverse, sigma_end, arrow_end):
    factor_cols = inverse_factor[0]
    order, width = factor_cols.shape
    arrow = tip_inverse.shape[0]
    pieces, devices = lax.axis_size("tm"), lax.axis_size("space")
    chips, cut = devices // CORES, CORES * width
    rows, both, hops = order // pieces, CORES * width, chips // 2
    f32, bf16 = jnp.float32, jnp.bfloat16
    column_at = lax.axis_index("space").reshape(1)
    piece_at = lax.axis_index("tm").reshape(1)
    hbm = pl.BlockSpec(memory_space=pltpu.HBM)

    def pack_kernel(cols, border, out, top, done):
        depth = order - cut
        copies = [
            pltpu.make_async_copy(border, out.at[pl.ds(depth, arrow)], done.at[0]),
            pltpu.make_async_copy(cols.at[pl.ds(0, cut)], top, done.at[1]),
        ]
        for at in range(0, depth, cut):
            spot = pl.ds(at, cut)
            copies.append(
                pltpu.make_async_copy(cols.at[pl.ds(cut + at, cut)], out.at[spot], done.at[1 + (at + cut) // cut])
            )
        for copy in copies:
            copy.start()
        for copy in copies:
            copy.wait()

    mine, top = pl.pallas_call(
        pack_kernel,
        out_shape=(pltpu.VMEM((order - cut + arrow, width), bf16), pltpu.VMEM((cut, width), bf16)),
        in_specs=[hbm, hbm],
        out_specs=(VMEM, VMEM),
        scratch_shapes=[pltpu.SemaphoreType.DMA((order // cut + 1,))],
        compiler_params=SMALL,
        name="pack",
    )(far_off(factor_cols), far_off(arrow_factor[0]))

    def hop(panel, count=1):
        pairs = []
        for p in range(devices):
            chip, core = p // CORES, p % CORES
            pairs.append((p, (chip + count * (1 - 2 * core)) % chips * CORES + core))
        return lax.ppermute(panel, "space", pairs)

    def swap(tile):
        return lax.ppermute(tile, "space", [(p, p ^ 1) for p in range(devices)])

    def shared(panel, count):
        return panel[cut * count - (order + arrow - panel.shape[0]) :]

    def product(kernel, name, count, panels, token, scratch=()):
        tall = count * width + arrow
        return pl.pallas_call(
            kernel,
            out_shape=(*[jax.ShapeDtypeStruct((tall, width), f32)] * 2, mark),
            in_specs=[VMEM] * (len(panels) + 2),
            out_specs=(VMEM,) * 3,
            scratch_shapes=scratch,
            compiler_params=SMALL,
            name=name,
        )(*map(near, panels), near(both_t), token)

    first = hop(mine)
    other, other_top = swap(mine), swap(top)
    second = hop(other)
    mark = jax.ShapeDtypeStruct((8, width), f32)
    own, both_t, end, token = pl.pallas_call(
        own_kernel,
        out_shape=(
            pltpu.VMEM((both + arrow, width), f32),
            pltpu.VMEM((both, order - cut), bf16),
            pltpu.VMEM((rows + PAD, width), f32),
            mark,
        ),
        in_specs=[SMEM, VMEM, VMEM, VMEM, VMEM, hbm, VMEM],
        out_specs=(VMEM,) * 4,
        scratch_shapes=[pltpu.SemaphoreType.DMA],
        compiler_params=SMALL,
        name="own",
    )(piece_at, *map(near, (mine, other, top, other_top)), far_off(sigma_end), near(arrow_end.T))

    first_2 = hop(shared(first, 2))
    second, token = lax.optimization_barrier((second, token))
    second_2 = hop(shared(second, 2))
    keep_1, give_1, token = product(far_kernel, "far", 2, (first, second), token)
    first_2, token = lax.optimization_barrier((first_2, token))
    first_4 = hop(shared(first_2, 4), 2)
    first_3 = hop(shared(first_2, 3))
    second_3 = hop(shared(second_2, 3))
    given_1 = swap(give_1)
    token, given_1 = lax.optimization_barrier((token, given_1))
    keep_2, give_2, token = product(
        three_kernel,
        "three",
        3,
        (first_2, second_2, first_4),
        token,
        [pltpu.VMEM((2, both + arrow, width), f32), pltpu.VMEM((2, width + arrow, width), f32)],
    )
    given_2 = swap(give_2)
    give_3, keep_3 = [
        pl.pallas_call(
            lambda *refs, low=low: half_kernel(low, *refs),
            out_shape=jax.ShapeDtypeStruct((both + arrow, width), f32),
            in_specs=[VMEM] * 4,
            out_specs=VMEM,
            compiler_params=SMALL,
            name=name,
        )(near(first_3), near(second_3), near(both_t), token)
        for name, low in (("give", width), ("keep", 0))
    ]
    kept, given = (keep_1, keep_2, keep_3), (given_1, given_2, swap(give_3))

    message = (pieces, rows + PAD, width)
    sent, plain, own_arrow = pl.pallas_call(
        lambda *refs: message_kernel(rows, chips, hops, *refs),
        out_shape=(
            pltpu.VMEM(message, f32),
            pltpu.VMEM((pieces, rows, width), f32),
            pltpu.VMEM((arrow, width), f32),
        ),
        in_specs=[SMEM] + [VMEM] * (2 * hops + 1),
        out_specs=(VMEM,) * 3,
        compiler_params=SMALL,
        name="message",
    )(column_at, *map(near, (own, *kept, *given, tip_inverse, decay)))

    def exchange(values):
        moved = lax.all_to_all(values.astype(jnp.float16), "tm", 0, 0, tiled=True)
        return moved.astype(jnp.float32)

    ahead = pl.pallas_call(
        lambda *refs: scan_kernel(rows, *refs),
        out_shape=pltpu.VMEM(message, f32),
        in_specs=[VMEM] * 2,
        out_specs=VMEM,
        scratch_shapes=[pltpu.VMEM((pieces, width), f32)],
        compiler_params=SMALL,
        name="suffix",
    )(near(exchange(sent)), near(end))
    sigma, arrows = pl.pallas_call(
        lambda *refs: last_kernel(rows, *refs),
        out_shape=(jax.ShapeDtypeStruct((order, width), f32), jax.ShapeDtypeStruct((arrow, width), f32)),
        in_specs=[SMEM] + [VMEM] * 4,
        scratch_shapes=[pltpu.VMEM((pieces, width), f32)],
        compiler_params=SMALL,
        name="last",
    )(column_at, *map(near, (plain, own_arrow, exchange(ahead), decay)))
    return sigma[None], arrows.T[None]


def solution(mesh):
    placed = (
        P("tm", None, "space"),
        P("tm", None, "space"),
        P("tm", None),
        P(),
        P(None, "space"),
        P("space", None),
    )
    return jax.shard_map(
        body,
        mesh=mesh,
        in_specs=placed,
        out_specs=(P("tm", None, "space"), P("tm", "space", None)),
        check_vma=False,
    )
```
